32 devices in a mesh: dp: 8 (over z, y), mp: 4 (over x, core).
Axes of the slice: x: 2, y: 2, z: 4, core: 2. Of those that a mesh axis runs over, the one named last changes fastest.
Arguments:
- tokens: bfloat16 [128, 147, 768], P('dp'), may hold values from -6 to 6
- cotangent: bfloat16 [128, 147, 768], P('dp'), may hold values from -6 to 6
- visible: int32 [128, 147], P('dp'), may hold values from 0 to 587, as said below
- tile_counts: int32 [8], P('dp'), may hold values from 1 to 16, as said below
- attend_weight: float32 [768, 3, 768], P('dp', None, 'mp'), may hold values from -0.3125 to 0.3125
- project_weight: float32 [768, 768], P('mp', 'dp'), may hold values from -0.875 to 0.875
- widen_weight: float32 [768, 3072], P('dp', 'mp'), may hold values from -0.21875 to 0.21875
- narrow_weight: float32 [3072, 768], P('mp', 'dp'), may hold values from -0.109375 to 0.109375
- heads_offset: float32 [2, 12, 64], P(None, 'mp', 'dp'), may hold values from -0.6 to 0.6
- hidden_offset: float32 [48, 64], P('mp', 'dp'), may hold values from -0.6 to 0.6
- layer_vectors: float32 [6, 768], P(None, 'dp'), may hold values from -1 to 2
- attend_first: float32 [768, 3, 768], P('dp', None, 'mp')
- project_first: float32 [768, 768], P('mp', 'dp')
- widen_first: float32 [768, 3072], P('dp', 'mp')
- narrow_first: float32 [3072, 768], P('mp', 'dp')
- heads_first: float32 [2, 12, 64], P(None, 'mp', 'dp')
- hidden_first: float32 [48, 64], P('mp', 'dp')
- vectors_first: float32 [6, 768], P(None, 'dp')
- attend_second: float32 [768, 3, 768], P('dp', None, 'mp')
- project_second: float32 [768, 768], P('mp', 'dp')
- widen_second: float32 [768, 3072], P('dp', 'mp')
- narrow_second: float32 [3072, 768], P('mp', 'dp')
- heads_second: float32 [2, 12, 64], P(None, 'mp', 'dp')
- hidden_second: float32 [48, 64], P('mp', 'dp')
- vectors_second: float32 [6, 768], P(None, 'dp')
Outputs:
- output: bfloat16 [128, 147, 768], P('dp')
- input_grad: float32 [128, 147, 768], P('dp')
- grad_attend: float32 [768, 3, 768], P('dp', None, 'mp')
- grad_project: float32 [768, 768], P('mp', 'dp')
- grad_widen: float32 [768, 3072], P('dp', 'mp')
- grad_narrow: float32 [3072, 768], P('mp', 'dp')
- grad_heads: float32 [2, 12, 64], P(None, 'mp', 'dp')
- grad_hidden: float32 [48, 64], P('mp', 'dp')
- grad_vectors: float32 [6, 768], P(None, 'dp')
- new_attend: float32 [768, 3, 768], P('dp', None, 'mp')
- new_project: float32 [768, 768], P('mp', 'dp')
- new_widen: float32 [768, 3072], P('dp', 'mp')
- new_narrow: float32 [3072, 768], P('mp', 'dp')
- new_heads: float32 [2, 12, 64], P(None, 'mp', 'dp')
- new_hidden: float32 [48, 64], P('mp', 'dp')
- new_vectors: float32 [6, 768], P(None, 'dp')
- first_attend: float32 [768, 3, 768], P('dp', None, 'mp')
- first_project: float32 [768, 768], P('mp', 'dp')
- first_widen: float32 [768, 3072], P('dp', 'mp')
- first_narrow: float32 [3072, 768], P('mp', 'dp')
- first_heads: float32 [2, 12, 64], P(None, 'mp', 'dp')
- first_hidden: float32 [48, 64], P('mp', 'dp')
- first_vectors: float32 [6, 768], P(None, 'dp')
- second_attend: float32 [768, 3, 768], P('dp', None, 'mp')
- second_project: float32 [768, 768], P('mp', 'dp')
- second_widen: float32 [768, 3072], P('dp', 'mp')
- second_narrow: float32 [3072, 768], P('mp', 'dp')
- second_heads: float32 [2, 12, 64], P(None, 'mp', 'dp')
- second_hidden: float32 [48, 64], P('mp', 'dp')
- second_vectors: float32 [6, 768], P(None, 'dp')
- copy_attend: bfloat16 [768, 3, 768], P('dp', None, 'mp')
- copy_project: bfloat16 [768, 768], P('mp', 'dp')
- copy_widen: bfloat16 [768, 3072], P('dp', 'mp')
- copy_narrow: bfloat16 [3072, 768], P('mp', 'dp')
- copy_heads: bfloat16 [2, 12, 64], P(None, 'mp', 'dp')
- copy_hidden: bfloat16 [48, 64], P('mp', 'dp')
- copy_vectors: bfloat16 [6, 768], P(None, 'dp')
The draws below stay inside these ranges and needn't reach their ends.
Inputs may be any that keep to these rules, and one draw needn't show every extreme that they name: `visible`: the 147 places of one tile are distinct, of 3 frames of 14 x 14 patches. `tile_counts`: slots from this count on hold padding; some device has every slot live and some has one.
All inputs are finite; a program needn't handle non-finite values.
Results may differ from the reference program's by a relative error of at most 0.017.
The reference program's roundings to bfloat16 on the way count: a program that leaves them out, or rounds other values in their place, can miss the bound.
Values may be sent and summed in bfloat16 or wider, within the bound.
A program may use at most 192 MiB of HBM per device.

```python
import math
import jax
import jax.numpy as jnp
from jax import lax

D = 768
FF = 3072
H = 12
HD = 64
FRAMES = 3
GRID = 14
STEP = 3
TILES_DEV = 16
SEQ = 147
TILES = 128


def live_tokens():
    return TILES * SEQ * (TILES_DEV + 1) / (2.0 * TILES_DEV)


def moment_first(key, array_shape, factor):
    normal_draw = jnp.clip(jax.random.normal(key, array_shape, jnp.float32), -4.0, 4.0)
    return factor * math.sqrt(live_tokens()) * normal_draw


def moment_second(key, array_shape, factor):
    square_size = factor * factor * live_tokens()
    spread = jax.random.uniform(key, array_shape, jnp.float32, math.log(0.7), math.log(4.0))
    return square_size * jnp.exp(spread)


def draw_visible(key, part):
    tile_keys = jax.random.split(key, TILES)

    def one_tile(tile_key):
        return jax.random.permutation(tile_key, FRAMES * GRID * GRID)[:SEQ]
    return jax.vmap(one_tile)(tile_keys).astype(jnp.int32)


def draw_tile_counts(key, part):
    devices_dp = TILES // TILES_DEV
    count_key = jax.random.fold_in(key, 11)
    place_key = jax.random.fold_in(key, 12)
    counts = jax.random.randint(count_key, (devices_dp,), 1, TILES_DEV + 1).astype(jnp.int32)
    places = jax.random.permutation(place_key, devices_dp)
    counts = counts.at[places[0]].set(TILES_DEV)
    counts = counts.at[places[1]].set(1)
    return counts.astype(jnp.int32)


def draw_layer_vectors(key, part):
    gain_key = jax.random.fold_in(key, 21)
    shift_key = jax.random.fold_in(key, 22)
    gains = jax.random.uniform(gain_key, (6, D), jnp.float32, 0.5, 1.5)
    shifts = 0.1 * jnp.clip(jax.random.normal(shift_key, (6, D), jnp.float32), -5.0, 5.0)
    row_number = jnp.arange(6)[:, None]
    is_gain = (row_number == 0) | (row_number == 2)
    return jnp.where(is_gain, gains, shifts)


def draw_attend_first(key, part):
    return moment_first(key, (D, 3, D), 0.7)


def draw_project_first(key, part):
    return moment_first(key, (D, D), 0.35)


def draw_widen_first(key, part):
    return moment_first(key, (D, FF), 0.3)


def draw_narrow_first(key, part):
    return moment_first(key, (FF, D), 0.6)


def draw_heads_first(key, part):
    return moment_first(key, (2, H, HD), 0.7)


def draw_hidden_first(key, part):
    return moment_first(key, (FF // HD, HD), 0.3)


def draw_vectors_first(key, part):
    return moment_first(key, (6, D), 1.0)


def draw_attend_second(key, part):
    return moment_second(key, (D, 3, D), 0.7)


def draw_project_second(key, part):
    return moment_second(key, (D, D), 0.35)


def draw_widen_second(key, part):
    return moment_second(key, (D, FF), 0.3)


def draw_narrow_second(key, part):
    return moment_second(key, (FF, D), 0.6)


def draw_heads_second(key, part):
    return moment_second(key, (2, H, HD), 0.7)


def draw_hidden_second(key, part):
    return moment_second(key, (FF // HD, HD), 0.3)


def draw_vectors_second(key, part):
    return moment_second(key, (6, D), 1.0)


def steps_of(own_key, shape, cuts, smallest, largest):
    loudness, own = 1.0, jax.random.fold_in(own_key, 6)
    for axis_at, shards_of in cuts:
        heights = jnp.exp(jax.random.uniform(jax.random.fold_in(own, axis_at), (shards_of,), jnp.float32, smallest / len(cuts), largest / len(cuts)))
        loudness = loudness * jnp.repeat(heights, shape[axis_at] // shards_of).reshape([-1 if axis == axis_at else 1 for axis in range(len(shape))])
    return loudness


def centred(stream_key, shape, deviation, limit, pieces=(), kind=jnp.bfloat16):
    entries = jax.random.normal(stream_key, shape, jnp.float32) * deviation
    if len(pieces) > 0:
        entries = steps_of(stream_key, shape, pieces, -0.22, 0.18) * entries
    return jnp.clip(entries, min=-limit, max=limit).astype(kind)


def setup_inputs(seed: int = 0) -> dict:
    keys = jax.random.split(jax.random.key(seed), 26)
    tokens = centred(keys[0], (TILES, SEQ, D), 1.0, 6.0, ((0, 8),))
    cotangent = centred(keys[1], (TILES, SEQ, D), 1.0, 6.0, ((0, 8),))
    visible = draw_visible(jax.random.fold_in(keys[25], 71), 0)
    tile_counts = draw_tile_counts(jax.random.fold_in(keys[25], 71), 0)
    attend_weight = centred(keys[4], (D, 3, D), (D // 2) ** -0.5, 0.3125, ((0, 8), (2, 4)), jnp.float32)
    project_weight = centred(keys[5], (D, D), (D // 16) ** -0.5, 0.875, ((0, 4), (1, 8)), jnp.float32)
    widen_weight = centred(keys[6], (D, FF), D ** -0.5, 0.21875, ((0, 8), (1, 4)), jnp.float32)
    narrow_weight = centred(keys[7], (FF, D), FF ** -0.5, 0.109375, ((0, 4), (1, 8)), jnp.float32)
    heads_offset = centred(keys[8], (2, H, HD), 0.1, 0.6, ((1, 4), (2, 8)), jnp.float32)
    hidden_offset = centred(keys[9], (FF // HD, HD), 0.1, 0.6, ((0, 4), (1, 8)), jnp.float32)
    layer_vectors = draw_layer_vectors(jax.random.fold_in(keys[25], 71), 0)
    attend_first = draw_attend_first(jax.random.fold_in(keys[25], 71), 0)
    project_first = draw_project_first(jax.random.fold_in(keys[25], 71), 0)
    widen_first = draw_widen_first(jax.random.fold_in(keys[25], 71), 0)
    narrow_first = draw_narrow_first(jax.random.fold_in(keys[25], 71), 0)
    heads_first = draw_heads_first(jax.random.fold_in(keys[25], 71), 0)
    hidden_first = draw_hidden_first(jax.random.fold_in(keys[25], 71), 0)
    vectors_first = draw_vectors_first(jax.random.fold_in(keys[25], 71), 0)
    attend_second = draw_attend_second(jax.random.fold_in(keys[25], 71), 0)
    project_second = draw_project_second(jax.random.fold_in(keys[25], 71), 0)
    widen_second = draw_widen_second(jax.random.fold_in(keys[25], 71), 0)
    narrow_second = draw_narrow_second(jax.random.fold_in(keys[25], 71), 0)
    heads_second = draw_heads_second(jax.random.fold_in(keys[25], 71), 0)
    hidden_second = draw_hidden_second(jax.random.fold_in(keys[25], 71), 0)
    vectors_second = draw_vectors_second(jax.random.fold_in(keys[25], 71), 0)
    return dict(tokens=tokens, cotangent=cotangent, visible=visible, tile_counts=tile_counts, attend_weight=attend_weight, project_weight=project_weight, widen_weight=widen_weight, narrow_weight=narrow_weight, heads_offset=heads_offset, hidden_offset=hidden_offset, layer_vectors=layer_vectors, attend_first=attend_first, project_first=project_first, widen_first=widen_first, narrow_first=narrow_first, heads_first=heads_first, hidden_first=hidden_first, vectors_first=vectors_first, attend_second=attend_second, project_second=project_second, widen_second=widen_second, narrow_second=narrow_second, heads_second=heads_second, hidden_second=hidden_second, vectors_second=vectors_second)


@jax.custom_vjp
def low(v):
    return lax.optimization_barrier(v.astype(jnp.bfloat16)).astype(jnp.float32)

@jax.custom_vjp
def low_back(v):
    return v

def low_keep(v):
    return (low(v), None)

def low_pass(kept, grad):
    return (grad,)

def back_keep(v):
    return (v, None)

def back_low(kept, grad):
    return (low(grad),)
low.defvjp(low_keep, low_pass)
low_back.defvjp(back_keep, back_low)
LN_EPS = 1e-06
BETA_ONE = 0.5
BETA_TWO = 0.5
ADAM_EPS = 1e-08
DECAY = 0.05

def sine_table(places, feature_width):
    half_width = feature_width // 2
    spread = jnp.arange(half_width, dtype=jnp.float32) / half_width
    frequency = jnp.exp(-math.log(10000.0) * spread)
    angles = places[..., None] * frequency
    return jnp.concatenate([jnp.sin(angles), jnp.cos(angles)], axis=-1)

def position_table(visible, feature_width):
    plane_size = GRID * GRID
    frame_place = (visible // plane_size).astype(jnp.float32)
    within = visible % plane_size
    row_place = (within // GRID).astype(jnp.float32)
    column_place = (within % GRID).astype(jnp.float32)
    time_width = feature_width // 16 * 4
    space_width = feature_width // 16 * 6
    return jnp.concatenate([sine_table(frame_place, time_width), sine_table(row_place, space_width), sine_table(column_place, space_width)], axis=-1)

def normalize(values):
    center = values - lax.optimization_barrier(jnp.mean(values, axis=-1, keepdims=True))
    return center * lax.rsqrt(lax.optimization_barrier(jnp.mean(center * center, axis=-1, keepdims=True)) + LN_EPS)

def adamw_update(master, first_moment, second_moment, gradient, step_rate, weight_decay, correction):
    first_new = BETA_ONE * first_moment + (1.0 - BETA_ONE) * gradient
    second_new = BETA_TWO * second_moment + (1.0 - BETA_TWO) * gradient * gradient
    ratio = first_new / correction / (jnp.sqrt(second_new / correction) + ADAM_EPS)
    master_new = master - step_rate * (ratio + weight_decay * master)
    return (master_new, first_new, second_new)

def reference(tokens, cotangent, visible, tile_counts, attend_weight, project_weight, widen_weight, narrow_weight, heads_offset, hidden_offset, layer_vectors, attend_first, project_first, widen_first, narrow_first, heads_first, hidden_first, vectors_first, attend_second, project_second, widen_second, narrow_second, heads_second, hidden_second, vectors_second):
    masters = (attend_weight, project_weight, widen_weight, narrow_weight, heads_offset, hidden_offset, layer_vectors)
    working = tuple((member.astype(jnp.bfloat16).astype(jnp.float32) for member in masters))
    tile_index = jnp.arange(TILES, dtype=jnp.int32)
    live_tiles = (tile_index % TILES_DEV < tile_counts[tile_index // TILES_DEV]).astype(jnp.float32)
    table = position_table(visible, D)
    score_scale = 1.0 / math.sqrt(HD)
    highest = lax.Precision.HIGHEST

    def forward(inputs_wide, attend, project, widen, narrow, heads, hidden_bias, vectors):
        summed = inputs_wide + table
        attend_in = low(normalize(summed) * vectors[0] + vectors[1])
        linear = jnp.einsum('tsd,dce->tsce', attend_in, attend, precision=highest)
        offsets = heads.reshape(2, D)
        query = low(low_back(linear[:, :, 0] + offsets[0])).reshape(TILES, SEQ, H, HD)
        keys_low = low(low_back(linear[:, :, 1])).reshape(TILES, SEQ, H, HD)
        values_low = low(low_back(linear[:, :, 2] + offsets[1])).reshape(TILES, SEQ, H, HD)
        scores = low_back(jnp.einsum('tqhd,tkhd->thqk', query, keys_low, precision=highest) * score_scale)
        weights = low(jax.nn.softmax(scores, axis=-1))
        context = jnp.einsum('thqk,tkhd->tqhd', weights, values_low, precision=highest).reshape(TILES, SEQ, D)
        context = low(low_back(context))
        middle = summed + low_back(jnp.einsum('tsd,de->tse', context, project, precision=highest)) + vectors[4]
        widen_in = low(normalize(middle) * vectors[2] + vectors[3])
        hidden = low_back(jnp.einsum('tsd,df->tsf', widen_in, widen, precision=highest) + hidden_bias.reshape(FF))
        active = low(jax.nn.gelu(hidden, approximate=False))
        feed_sum = low_back(jnp.einsum('tsf,fd->tsd', active, narrow, precision=highest))
        return live_tiles[:, None, None] * (middle + feed_sum + vectors[5])
    result, pullback = jax.vjp(forward, tokens.astype(jnp.float32), *working)
    gradients = pullback(cotangent.astype(jnp.float32))
    input_grad = gradients[0]
    grad_attend, grad_project, grad_widen, grad_narrow, grad_heads, grad_hidden, grad_vectors = gradients[1:]
    correction = 1.0 - 0.5 ** STEP
    new_attend, first_attend, second_attend = adamw_update(attend_weight, attend_first, attend_second, grad_attend, (D // 2) ** (-0.5), DECAY, correction)
    new_project, first_project, second_project = adamw_update(project_weight, project_first, project_second, grad_project, (D // 16) ** (-0.5), DECAY, correction)
    new_widen, first_widen, second_widen = adamw_update(widen_weight, widen_first, widen_second, grad_widen, D ** (-0.5), DECAY, correction)
    new_narrow, first_narrow, second_narrow = adamw_update(narrow_weight, narrow_first, narrow_second, grad_narrow, FF ** (-0.5), DECAY, correction)
    new_heads, first_heads, second_heads = adamw_update(heads_offset, heads_first, heads_second, grad_heads, 0.1, 0.0, correction)
    new_hidden, first_hidden, second_hidden = adamw_update(hidden_offset, hidden_first, hidden_second, grad_hidden, 0.1, 0.0, correction)
    new_vectors, first_vectors, second_vectors = adamw_update(layer_vectors, vectors_first, vectors_second, grad_vectors, 0.15, 0.0, correction)
    return (result.astype(jnp.bfloat16), input_grad, grad_attend, grad_project, grad_widen, grad_narrow, grad_heads, grad_hidden, grad_vectors, new_attend, new_project, new_widen, new_narrow, new_heads, new_hidden, new_vectors, first_attend, first_project, first_widen, first_narrow, first_heads, first_hidden, first_vectors, second_attend, second_project, second_widen, second_narrow, second_heads, second_hidden, second_vectors, new_attend.astype(jnp.bfloat16), new_project.astype(jnp.bfloat16), new_widen.astype(jnp.bfloat16), new_narrow.astype(jnp.bfloat16), new_heads.astype(jnp.bfloat16), new_hidden.astype(jnp.bfloat16), new_vectors.astype(jnp.bfloat16))
```

```python
import functools
import math

import jax
import jax.numpy as jnp
import numpy as np
from jax import lax
from jax.experimental import pallas as pl
from jax.experimental.pallas import tpu as pltpu
from jax.sharding import PartitionSpec as P

D = 768
FF = 3072
GRID = 14
STEP = 3


LN_EPS = 1e-06
BETA_ONE = 0.5
BETA_TWO = 0.5
ADAM_EPS = 1e-08
DECAY = 0.05


def cut_along(x, dim, size):
    dims = x.shape
    parts = x.reshape(*dims[:dim], size, dims[dim] // size, *dims[dim + 1 :])
    return jnp.moveaxis(parts, dim, 0)


def summed_on_arrival(x, axis, dim):
    size = lax.axis_size(axis)
    parts = lax.all_to_all(cut_along(x, dim, size), axis, 0, 0, tiled=True)
    return jnp.sum(parts.astype(jnp.float32), axis=0)


def sine_table(places, feature_width):
    half_width = feature_width // 2
    spread = jnp.arange(half_width, dtype=jnp.float32) / half_width
    frequency = jnp.exp(-math.log(10000.0) * spread)
    angles = places[..., None] * frequency
    return jnp.concatenate([jnp.sin(angles), jnp.cos(angles)], axis=-1)


def position_table(visible, feature_width):
    plane_size = GRID * GRID
    frame_place = (visible // plane_size).astype(jnp.float32)
    within = visible % plane_size
    row_place = (within // GRID).astype(jnp.float32)
    column_place = (within % GRID).astype(jnp.float32)
    time_width = feature_width // 16 * 4
    space_width = feature_width // 16 * 6
    return jnp.concatenate(
        [
            sine_table(frame_place, time_width),
            sine_table(row_place, space_width),
            sine_table(column_place, space_width),
        ],
        axis=-1,
    )


def normalize(values):
    center = values - jnp.mean(values, axis=-1, keepdims=True)
    inverse = lax.rsqrt(jnp.mean(center * center, axis=-1, keepdims=True) + LN_EPS)
    return (center * inverse, inverse)


def norm_back(grad_normed, normed, inverse):
    return inverse * (
        grad_normed
        - jnp.mean(grad_normed, axis=-1, keepdims=True)
        - normed * jnp.mean(grad_normed * normed, axis=-1, keepdims=True)
    )


def over_rows(former, latter):
    return lax.dot_general(
        former, latter, (((0,), (0,)), ((), ())), preferred_element_type=jnp.float32
    )


def over_cols(former, latter):
    return lax.dot_general(
        former, latter, (((1,), (1,)), ((), ())), preferred_element_type=jnp.float32
    )


def exact_gelu(values):
    return jax.nn.gelu(values, approximate=False)


def adamw_update(
    master, first_moment, second_moment, gradient, step_rate, weight_decay, correction
):
    first_new = BETA_ONE * first_moment + (1.0 - BETA_ONE) * gradient
    second_new = BETA_TWO * second_moment + (1.0 - BETA_TWO) * gradient * gradient
    ratio = first_new / correction / (jnp.sqrt(second_new / correction) + ADAM_EPS)
    master_new = master - step_rate * (ratio + weight_decay * master)
    return (master_new, first_new, second_new)


def shards(
    tokens,
    cotangent,
    visible,
    tile_counts,
    attend_weight,
    project_weight,
    widen_weight,
    narrow_weight,
    heads_offset,
    hidden_offset,
    layer_vectors,
    attend_first,
    project_first,
    widen_first,
    narrow_first,
    heads_first,
    hidden_first,
    vectors_first,
    attend_second,
    project_second,
    widen_second,
    narrow_second,
    heads_second,
    hidden_second,
    vectors_second,
):
    fore_attend, fore_project, fore_widen, fore_narrow, fore_heads, fore_hidden, fore_vectors = (
        lax.all_gather(attend_weight.astype(jnp.bfloat16), "dp", axis=0, tiled=True),
        lax.all_gather(project_weight.astype(jnp.bfloat16), "dp", axis=1, tiled=True),
        lax.all_gather(widen_weight.astype(jnp.bfloat16), "dp", axis=0, tiled=True),
        lax.all_gather(narrow_weight.astype(jnp.bfloat16), "dp", axis=1, tiled=True),
        lax.all_gather(heads_offset.astype(jnp.bfloat16), "dp", axis=2, tiled=True),
        lax.all_gather(hidden_offset.astype(jnp.bfloat16), "dp", axis=1, tiled=True),
        lax.all_gather(layer_vectors.astype(jnp.bfloat16), "dp", axis=1, tiled=True),
    )
    tile_count, seq_length, model_width = tokens.shape
    row_count = tile_count * seq_length
    local_width = fore_attend.shape[2]
    heads_local = fore_heads.shape[1]
    head_size = fore_heads.shape[2]
    score_scale = 1.0 / math.sqrt(head_size)
    live_tiles = (jnp.arange(tile_count, dtype=jnp.int32) < tile_counts[0]).astype(jnp.float32)
    live_rows = jnp.broadcast_to(live_tiles[:, None], (tile_count, seq_length)).reshape(
        row_count, 1
    )
    vectors = fore_vectors.astype(jnp.float32)
    summed = (tokens.astype(jnp.float32) + position_table(visible, model_width)).reshape(
        row_count, model_width
    )
    normed_one, inverse_one = normalize(summed)
    attend_low = (normed_one * vectors[0] + vectors[1]).astype(jnp.bfloat16)
    linear = jnp.dot(
        attend_low,
        fore_attend.reshape(model_width, 3 * local_width),
        preferred_element_type=jnp.float32,
    ).reshape(row_count, 3, local_width)
    offsets = fore_heads.astype(jnp.float32).reshape(2, local_width)
    head_shape = (tile_count, seq_length, heads_local, head_size)
    query_low = (linear[:, 0] + offsets[0]).astype(jnp.bfloat16).reshape(head_shape)
    key_low = linear[:, 1].astype(jnp.bfloat16).reshape(head_shape)
    value_low = (linear[:, 2] + offsets[1]).astype(jnp.bfloat16).reshape(head_shape)
    scores = (
        jnp.einsum("tqhd,tkhd->thqk", query_low, key_low, preferred_element_type=jnp.float32)
        * score_scale
    )
    row_top = jnp.max(scores, axis=-1, keepdims=True)
    log_total = row_top + jnp.log(jnp.sum(jnp.exp(scores - row_top), axis=-1, keepdims=True))
    weights_low = jnp.exp(scores - log_total).astype(jnp.bfloat16)
    context = jnp.einsum(
        "thqk,tkhd->tqhd", weights_low, value_low, preferred_element_type=jnp.float32
    )
    context_low = context.reshape(row_count, local_width).astype(jnp.bfloat16)
    attention_part = jnp.dot(context_low, fore_project, preferred_element_type=jnp.float32)
    attention = lax.psum(attention_part.astype(jnp.bfloat16), "mp").astype(jnp.float32)
    middle = summed + attention + vectors[4]
    normed_two, inverse_two = normalize(middle)
    widen_low = (normed_two * vectors[2] + vectors[3]).astype(jnp.bfloat16)
    hidden = jnp.dot(
        widen_low, fore_widen, preferred_element_type=jnp.float32
    ) + fore_hidden.astype(jnp.float32).reshape(-1)
    active_low = exact_gelu(hidden).astype(jnp.bfloat16)
    feed_part = jnp.dot(active_low, fore_narrow, preferred_element_type=jnp.float32)
    feed_sum = lax.psum(feed_part.astype(jnp.bfloat16), "mp").astype(jnp.float32)
    result = (middle + feed_sum + vectors[5]) * live_rows
    output_low = result.astype(jnp.bfloat16)
    back_attend, back_project, back_widen, back_narrow, back_vectors = (
        fore_attend,
        fore_project,
        fore_widen,
        fore_narrow,
        fore_vectors,
    )
    vectors_back = back_vectors.astype(jnp.float32)
    grad_out = cotangent.astype(jnp.float32).reshape(row_count, model_width) * live_rows
    grad_out_low = grad_out.astype(jnp.bfloat16)
    grad_narrow = over_rows(active_low, grad_out_low)
    grad_active = over_cols(grad_out_low, back_narrow)
    gelu_back = jax.vjp(exact_gelu, hidden)[1]
    grad_hidden_low = gelu_back(grad_active)[0].astype(jnp.bfloat16)
    grad_widen = over_rows(widen_low, grad_hidden_low)
    grad_hidden = jnp.sum(grad_hidden_low.astype(jnp.float32), axis=0).reshape(fore_hidden.shape)
    normed_two_part = over_cols(grad_hidden_low, back_widen)
    grad_normed_two = lax.psum(normed_two_part.astype(jnp.bfloat16), "mp").astype(jnp.float32)
    grad_middle = grad_out + norm_back(grad_normed_two * vectors_back[2], normed_two, inverse_two)
    grad_middle_low = grad_middle.astype(jnp.bfloat16)
    grad_project = over_rows(context_low, grad_middle_low)
    grad_context_low = (
        over_cols(grad_middle_low, back_project).astype(jnp.bfloat16).reshape(head_shape)
    )
    scores_again = (
        jnp.einsum("tqhd,tkhd->thqk", query_low, key_low, preferred_element_type=jnp.float32)
        * score_scale
    )
    weights_full = jnp.exp(scores_again - log_total)
    weights_again_low = weights_full.astype(jnp.bfloat16)
    grad_weights = jnp.einsum(
        "tqhd,tkhd->thqk", grad_context_low, value_low, preferred_element_type=jnp.float32
    )
    grad_value = jnp.einsum(
        "thqk,tqhd->tkhd", weights_again_low, grad_context_low, preferred_element_type=jnp.float32
    )
    row_dot = jnp.sum(grad_weights * weights_full, axis=-1, keepdims=True)
    grad_scores_low = (weights_full * (grad_weights - row_dot)).astype(jnp.bfloat16)
    grad_query = (
        jnp.einsum("thqk,tkhd->tqhd", grad_scores_low, key_low, preferred_element_type=jnp.float32)
        * score_scale
    )
    grad_key = (
        jnp.einsum(
            "thqk,tqhd->tkhd", grad_scores_low, query_low, preferred_element_type=jnp.float32
        )
        * score_scale
    )
    grad_qkv_low = jnp.stack(
        [
            grad_query.reshape(row_count, local_width),
            grad_key.reshape(row_count, local_width),
            grad_value.reshape(row_count, local_width),
        ],
        axis=1,
    ).astype(jnp.bfloat16)
    grad_offsets = jnp.sum(grad_qkv_low.astype(jnp.float32), axis=0)
    grad_heads = jnp.stack([grad_offsets[0], grad_offsets[2]]).reshape(2, heads_local, head_size)
    flat_qkv = grad_qkv_low.reshape(row_count, 3 * local_width)
    grad_attend = over_rows(attend_low, flat_qkv).reshape(model_width, 3, local_width)
    normed_one_part = over_cols(flat_qkv, back_attend.reshape(model_width, 3 * local_width))
    grad_normed_one = lax.psum(normed_one_part.astype(jnp.bfloat16), "mp").astype(jnp.float32)
    grad_inputs = grad_middle + norm_back(
        grad_normed_one * vectors_back[0], normed_one, inverse_one
    )
    grad_vectors = jnp.stack(
        [
            jnp.sum(grad_normed_one * normed_one, axis=0),
            jnp.sum(grad_normed_one, axis=0),
            jnp.sum(grad_normed_two * normed_two, axis=0),
            jnp.sum(grad_normed_two, axis=0),
            jnp.sum(grad_middle, axis=0),
            jnp.sum(grad_out, axis=0),
        ]
    )
    output = output_low.reshape(tile_count, seq_length, model_width)
    input_grad = grad_inputs.reshape(tile_count, seq_length, model_width)
    (
        shard_attend,
        shard_project,
        shard_widen,
        shard_narrow,
        shard_heads,
        shard_hidden,
        shard_vectors,
    ) = (
        summed_on_arrival(grad_attend.astype(jnp.bfloat16), "dp", 0),
        summed_on_arrival(grad_project.astype(jnp.bfloat16), "dp", 1),
        summed_on_arrival(grad_widen.astype(jnp.bfloat16), "dp", 0),
        summed_on_arrival(grad_narrow.astype(jnp.bfloat16), "dp", 1),
        summed_on_arrival(grad_heads.astype(jnp.bfloat16), "dp", 2),
        summed_on_arrival(grad_hidden.astype(jnp.bfloat16), "dp", 1),
        summed_on_arrival(grad_vectors.astype(jnp.bfloat16), "dp", 1),
    )
    correction = 1.0 - 0.5**STEP
    new_attend, first_attend, second_attend = adamw_update(
        attend_weight,
        attend_first,
        attend_second,
        shard_attend,
        (D // 2) ** (-0.5),
        DECAY,
        correction,
    )
    new_project, first_project, second_project = adamw_update(
        project_weight,
        project_first,
        project_second,
        shard_project,
        (D // 16) ** (-0.5),
        DECAY,
        correction,
    )
    new_widen, first_widen, second_widen = adamw_update(
        widen_weight, widen_first, widen_second, shard_widen, D ** (-0.5), DECAY, correction
    )
    new_narrow, first_narrow, second_narrow = adamw_update(
        narrow_weight, narrow_first, narrow_second, shard_narrow, FF ** (-0.5), DECAY, correction
    )
    new_heads, first_heads, second_heads = adamw_update(
        heads_offset, heads_first, heads_second, shard_heads, 0.1, 0.0, correction
    )
    new_hidden, first_hidden, second_hidden = adamw_update(
        hidden_offset, hidden_first, hidden_second, shard_hidden, 0.1, 0.0, correction
    )
    new_vectors, first_vectors, second_vectors = adamw_update(
        layer_vectors, vectors_first, vectors_second, shard_vectors, 0.15, 0.0, correction
    )
    return (
        output,
        input_grad,
        shard_attend,
        shard_project,
        shard_widen,
        shard_narrow,
        shard_heads,
        shard_hidden,
        shard_vectors,
        new_attend,
        new_project,
        new_widen,
        new_narrow,
        new_heads,
        new_hidden,
        new_vectors,
        first_attend,
        first_project,
        first_widen,
        first_narrow,
        first_heads,
        first_hidden,
        first_vectors,
        second_attend,
        second_project,
        second_widen,
        second_narrow,
        second_heads,
        second_hidden,
        second_vectors,
        new_attend.astype(jnp.bfloat16),
        new_project.astype(jnp.bfloat16),
        new_widen.astype(jnp.bfloat16),
        new_narrow.astype(jnp.bfloat16),
        new_heads.astype(jnp.bfloat16),
        new_hidden.astype(jnp.bfloat16),
        new_vectors.astype(jnp.bfloat16),
    )


F32 = jnp.float32
BF16 = jnp.bfloat16
MESH = pl.DeviceIdType.MESH
ANY = pl.ANY


def nn(former, latter):
    return lax.dot_general(former, latter, (((1,), (0,)), ((), ())), preferred_element_type=F32)


def nt(former, latter):
    return lax.dot_general(former, latter, (((1,), (1,)), ((), ())), preferred_element_type=F32)


def tn(former, latter):
    return lax.dot_general(former, latter, (((0,), (0,)), ((), ())), preferred_element_type=F32)


def iota(shape, dim):
    return lax.broadcasted_iota(jnp.int32, shape, dim)


def whole(ref_shape):
    rank = len(ref_shape)
    return pl.BlockSpec(ref_shape, lambda *_: (0,) * rank)


def pick_vector(d):
    shape = (128, D)
    lane, column = iota(shape, 0), iota(shape, 1)
    return ((column - lane == 96 * d) & (lane < 96)).astype(F32).astype(BF16)


def pick_head(d):
    shape = (128, D)
    lane, column = iota(shape, 0), iota(shape, 1)
    same = (lax.shift_right_logical(column, 6) == lax.shift_right_logical(lane, 3)) & ((column & 7) == (lane & 7))
    return (same & ((lax.shift_right_logical(column, 3) & 7) == d) & (lane < 24)).astype(F32).astype(BF16)


def pick_row():
    shape = (128, D)
    return (lax.shift_right_logical(iota(shape, 1), 6) == iota(shape, 0)).astype(F32).astype(BF16)


def hidden_places(d):
    shape = (8, D)
    column = iota(shape, 1)
    return ((column & 7) == iota(shape, 0)) & ((lax.shift_right_logical(column, 3) & 7) == d)


def pack_kernel(attend, project, widen, narrow, heads, hidden, vectors, w_out, s_out, scratch):
    w_out[0] = jnp.concatenate([attend[0], attend[1], attend[2], project[...].T], axis=1).astype(BF16)
    w_out[1] = widen[...].astype(BF16)
    w_out[2] = narrow[...].astype(BF16)
    scratch[...] = jnp.zeros_like(scratch)
    scratch[0:6, 0:96] = vectors[...]
    for r in range(3):
        scratch[6:8, 8 * r : 8 * r + 8] = heads[r]
    scratch[8:16, 0:12] = hidden[...]
    s_out[...] = scratch[...].astype(BF16)


def spread_kernel(s_ref, vec_out, off_out):
    row_pick = pick_row()
    vec = jnp.zeros((16, D), F32)
    heads = [jnp.zeros((16, D), F32) for _ in range(4)]
    hidden = [jnp.zeros((1, D), F32) for _ in range(4)]
    for d in range(8):
        vec += nn(s_ref[0, d], pick_vector(d))
        head_pick, places = pick_head(d), hidden_places(d)
        for m in range(4):
            heads[m] += nn(s_ref[m, d], head_pick)
            spread = nn(s_ref[m, d], row_pick)[8:16]
            hidden[m] += jnp.sum(jnp.where(places, spread, 0.0), axis=0, keepdims=True)
    vec_out[...] = vec
    for m in range(4):
        off_out[m, 0:2, :] = heads[m][6:8]
        off_out[m, 2:3, :] = hidden[m]
        off_out[m, 3:8, :] = jnp.zeros((5, D), F32)


def squeeze_kernel(fore_ref, back_ref, hid_ref, heads_ref, out_ref, rows):
    rows[...] = jnp.zeros_like(rows)
    rows[0:2, :] = back_ref[0:2, :]
    rows[2:6, :] = fore_ref[0:4, :]
    row_pick = pick_row()
    shape = (8, 128)
    for m in range(4):
        rows[6:7, 0:192] = heads_ref[m, 0:1, 0:192]
        rows[7:8, 0:192] = heads_ref[m, 1:2, 0:192]
        block = rows[...].astype(BF16)
        wide = jnp.broadcast_to(hid_ref[m, 0:1, :], (8, D))
        for d in range(8):
            upper = jnp.where(iota(shape, 0) < 6, nt(block, pick_vector(d)), nt(block, pick_head(d)))
            lower = nt(jnp.where(hidden_places(d), wide, 0.0).astype(BF16), row_pick)
            out_ref[m, d] = jnp.concatenate([upper, lower], axis=0).astype(BF16)


def ln(values):
    center = values - jnp.mean(values, axis=-1, keepdims=True)
    inverse = lax.rsqrt(jnp.mean(center * center, axis=-1, keepdims=True) + LN_EPS)
    return center * inverse, inverse


def ln_back(grad, normed, inverse):
    return inverse * (
        grad
        - jnp.mean(grad, axis=-1, keepdims=True)
        - normed * jnp.mean(grad * normed, axis=-1, keepdims=True)
    )


def position_rows():
    plane = np.zeros((128, D), np.float32)
    time_width, space_width = D // 16 * 4, D // 16 * 6

    def sines(count, width):
        half = width // 2
        spread = np.arange(half, dtype=np.float32) / np.float32(half)
        frequency = np.exp(np.float32(-math.log(10000.0)) * spread).astype(np.float32)
        angles = np.arange(count, dtype=np.float32)[:, None] * frequency
        return np.concatenate([np.sin(angles), np.cos(angles)], axis=-1).astype(np.float32)

    plane[0:3, 0:time_width] = sines(3, time_width)
    plane[3 : 3 + GRID, time_width : time_width + space_width] = sines(GRID, space_width)
    plane[3 + GRID : 3 + 2 * GRID, time_width + space_width :] = sines(GRID, space_width)
    parts, rest = [], plane
    for _ in range(3):
        part = rest.astype(jnp.bfloat16)
        parts.append(part)
        rest = rest - part.astype(np.float32)
    return np.stack(parts)


def spread_lanes(ref, wide):
    for g in range(D // 128):
        part = ref[:, :, 128 * g : 128 * g + 128].astype(F32)
        wide[g] = part.reshape(part.shape[0] * 8, 128)


def place_rows(places):
    frame = (places >= GRID * GRID).astype(jnp.int32) + (places >= 2 * GRID * GRID).astype(jnp.int32)
    within = places - frame * (GRID * GRID)
    row = jnp.floor((within.astype(F32) + 0.5) * (1.0 / GRID)).astype(jnp.int32)
    column = within - row * GRID
    lane = iota((places.shape[0], 128), 1)
    hot = (lane == frame) | (lane == 3 + row) | (lane == 3 + GRID + column)
    return hot.astype(F32).astype(BF16)


def attend_kernel(seq, pad, tiles, who, tok_ref, vis_ref, tab_ref, vec_ref, off_ref, w_ref,
                  x_out, h_out, qkv_out, p_out, o_out, wide, low):
    m = pl.program_id(0)
    rows_of = lambda t: pl.ds(pl.multiple_of(t * pad, 16), pad)

    @pl.when(m == 0)
    def _():
        spread_lanes(tok_ref, wide)
        at = (who[0] & 1) * tiles
        tail = pad - seq
        for t in range(tiles):
            hot = place_rows(vis_ref[:, t : t + 1])
            table = nn(hot, tab_ref[0]) + nn(hot, tab_ref[1]) + nn(hot, tab_ref[2])
            x_out[t * pad + seq - seq % 8 : (t + 1) * pad, :] = jnp.zeros((tail + seq % 8, D), F32)
            for g in range(D // 128):
                lanes = slice(128 * g, 128 * g + 128)
                x_out[t * pad : t * pad + seq, lanes] = wide[g, pl.ds(at + t, seq, stride=8), :] + table[:, lanes]

        @pl.loop(0, tiles)
        def _(t):
            x = x_out[rows_of(t), :]
            normed, _ = ln(x)
            low[rows_of(t), :] = (normed * vec_ref[0:1, :] + vec_ref[1:2, :]).astype(BF16)
            h_out[rows_of(t), :] = x + vec_ref[4:5, :]

    linear = nn(low[...], w_ref[0, :, 0:576])
    zero = jnp.zeros((1, 192), F32)
    offset = jnp.concatenate([off_ref[0, 0:1, 0:192], zero, off_ref[0, 1:2, 0:192]], axis=1)
    qkv_out[0] = (linear + offset).astype(BF16)

    @pl.loop(0, tiles)
    def _(t):
        rows = rows_of(t)
        qkv = qkv_out[0, rows, :]
        parts = []
        for h in range(3):
            q, k, v = (qkv[:, 192 * j + 64 * h : 192 * j + 64 * h + 64] for j in range(3))
            s = nt(q, k) * 0.125
            s = jnp.where(iota(s.shape, 1) < seq, s, -1e30)
            e = jnp.exp(s - jnp.max(s, axis=-1, keepdims=True))
            low_p = (e * (1.0 / jnp.sum(e, axis=-1, keepdims=True))).astype(BF16)
            p_out[0, h, rows, :] = low_p
            parts.append(nn(low_p, v))
        o_out[0, rows, :] = jnp.concatenate(parts, axis=1).astype(BF16)

    h_out[...] += nt(o_out[0], w_ref[0, :, 576:768])


def feed_kernel(seq, pad, tiles, who, cot_ref, h_ref, vec_ref, off_ref, w2_ref, w3_ref,
                out_out, dh_out, sum_out, hid_out, g2_out, g3_out,
                wide, c, c_t, dy, dy_t, y, dc):
    m = pl.program_id(0)
    rows_of = lambda t: pl.ds(pl.multiple_of(t * pad, 16), pad)
    at = (who[0] & 1) * tiles
    first = who[0] * tiles

    @pl.when(m == 0)
    def _():
        spread_lanes(cot_ref, wide)
        y[...] = jnp.zeros_like(y)
        for t in range(tiles):
            live = (first + t < who[1]).astype(F32)
            for g in range(D // 128):
                lanes = slice(128 * g, 128 * g + 128)
                y[t * pad : t * pad + seq, lanes] = wide[g, pl.ds(at + t, seq, stride=8), :] * live
        sum_out[...] = jnp.zeros_like(sum_out)

        @pl.loop(0, tiles)
        def _(t):
            grad = y[rows_of(t), :]
            sum_out[3:4, :] += jnp.sum(grad, axis=0, keepdims=True)
            dy[rows_of(t), :] = grad.astype(BF16)
            normed, _ = ln(h_ref[rows_of(t), :])
            c[rows_of(t), :] = (normed * vec_ref[2:3, :] + vec_ref[3:4, :]).astype(BF16)

        dy_t[...] = dy[...].T
        c_t[...] = c[...].T
        y[...] = jnp.zeros_like(y)
        dc[...] = jnp.zeros_like(dc)

    @pl.loop(0, 3)
    def _(n):
        cols = pl.ds(pl.multiple_of(n * 256, 256), 256)
        u = nn(c[...], w2_ref[0, :, cols]) + off_ref[0, 2:3, cols]
        cdf = 0.5 * (1.0 + lax.erf(u * math.sqrt(0.5)))
        r = (u * cdf).astype(BF16)
        slope = cdf + u * (jnp.exp(-0.5 * u * u) * (1.0 / math.sqrt(2.0 * math.pi)))
        g3_out[0, :, cols] = nn(dy_t[...], r).astype(BF16)
        du = (nn(dy[...], w3_ref[0, :, cols]) * slope).astype(BF16)
        hid_out[0, 0:1, cols] = jnp.sum(du.astype(F32), axis=0, keepdims=True)
        g2_out[0, :, cols] = nn(c_t[...], du).astype(BF16)
        y[...] += nt(r, w3_ref[0, :, cols])
        dc[...] += nt(du, w2_ref[0, :, cols])

    @pl.when(m == pl.num_programs(0) - 1)
    def _():
        @pl.loop(0, tiles)
        def _(t):
            rows = rows_of(t)
            live = (first + t < who[1]).astype(F32)
            h = h_ref[rows, :]
            out_out[rows, :] = ((h + y[rows, :] + vec_ref[5:6, :]) * live).astype(BF16)
            normed, inverse = ln(h)
            grad = dc[rows, :]
            dh = dy[rows, :].astype(F32) + ln_back(grad * vec_ref[2:3, :], normed, inverse)
            dh_out[rows, :] = dh
            sum_out[0:1, :] += jnp.sum(grad * normed, axis=0, keepdims=True)
            sum_out[1:2, :] += jnp.sum(grad, axis=0, keepdims=True)
            sum_out[2:3, :] += jnp.sum(dh, axis=0, keepdims=True)


def back_kernel(seq, pad, tiles, x_ref, dh_ref, vec_ref, w_ref, qkv_ref, p_ref, o_ref,
                in_out, sum_out, head_out, g1_out, a_t, dh_low, dh_t, do, dqkv, da):
    m = pl.program_id(0)
    rows_of = lambda t: pl.ds(pl.multiple_of(t * pad, 16), pad)

    @pl.when(m == 0)
    def _():
        @pl.loop(0, tiles)
        def _(t):
            rows = rows_of(t)
            normed, _ = ln(x_ref[rows, :])
            dh_low[rows, :] = (normed * vec_ref[0:1, :] + vec_ref[1:2, :]).astype(BF16)

        a_t[...] = dh_low[...].T
        dh_low[...] = dh_ref[...].astype(BF16)
        dh_t[...] = dh_low[...].T
        da[...] = jnp.zeros_like(da)
        sum_out[...] = jnp.zeros_like(sum_out)

    do[...] = nn(dh_low[...], w_ref[0, :, 576:768]).astype(BF16)
    g1_out[0, :, 576:768] = nn(dh_t[...], o_ref[0]).astype(BF16)

    @pl.loop(0, tiles)
    def _(t):
        rows = rows_of(t)
        qkv = qkv_ref[0, rows, :]
        grad = do[rows, :]
        parts = [[], [], []]
        for h in range(3):
            q, k, v = (qkv[:, 192 * j + 64 * h : 192 * j + 64 * h + 64] for j in range(3))
            g = grad[:, 64 * h : 64 * h + 64]
            low_p = p_ref[0, h, rows, :]
            p = low_p.astype(F32)
            dp = nt(g, v)
            ds = (p * (dp - jnp.sum(dp * p, axis=-1, keepdims=True))).astype(BF16)
            parts[0].append(nn(ds, k) * 0.125)
            parts[1].append(tn(ds, q) * 0.125)
            parts[2].append(tn(low_p, g))
        dqkv[rows, :] = jnp.concatenate(parts[0] + parts[1] + parts[2], axis=1).astype(BF16)

    sums = jnp.sum(dqkv[...].astype(F32), axis=0, keepdims=True)
    head_out[0, 0:1, 0:192] = sums[:, 0:192]
    head_out[0, 1:2, 0:192] = sums[:, 384:576]
    g1_out[0, :, 0:576] = nn(a_t[...], dqkv[...]).astype(BF16)
    da[...] += nt(dqkv[...], w_ref[0, :, 0:576])

    @pl.when(m == pl.num_programs(0) - 1)
    def _():
        @pl.loop(0, tiles)
        def _(t):
            rows = rows_of(t)
            normed, inverse = ln(x_ref[rows, :])
            grad = da[rows, :]
            back = ln_back(grad * vec_ref[0:1, :], normed, inverse)
            in_out[rows, :] = (dh_ref[rows, :] + back).astype(BF16)
            sum_out[0:1, :] += jnp.sum(grad * normed, axis=0, keepdims=True)
            sum_out[1:2, :] += jnp.sum(grad, axis=0, keepdims=True)


def lay_kernel(seq, pad, count, out_ref, in_ref, out_out, in_out, wide):
    for t in range(count):
        wide[pl.ds(t, seq, stride=count), :] = out_ref[t, 0:seq, :].astype(F32)
        in_out[pl.ds(t, seq, stride=count), :] = in_ref[t, 0:seq, :].astype(F32)
    out_out[...] = wide[...].astype(BF16)


def update_kernel(*refs):
    grad_ref, small_ref = refs[:2]
    state, outs = refs[2:23], refs[23:]
    correction = 1.0 - 0.5**STEP
    rates = ((D // 2) ** -0.5, (D // 16) ** -0.5, D**-0.5, FF**-0.5, 0.1, 0.1, 0.15)

    def update(i, at, gradient):
        master, first, second = (state[i + 7 * j][at] for j in range(3))
        decay = DECAY if i < 4 else 0.0
        values = adamw_update(master, first, second, gradient, rates[i], decay, correction)
        for j, value in enumerate((gradient,) + values + (values[0].astype(BF16),)):
            outs[i + 7 * j][at] = value

    every = (slice(None), slice(None))
    for j in range(3):
        update(0, (j,) + every, grad_ref[0, :, 192 * j : 192 * j + 192])
    update(1, every, grad_ref[0, :, 576:768].T)
    update(2, every, grad_ref[1])
    update(3, every, grad_ref[2])
    for r in range(3):
        update(4, (r,) + every, small_ref[6:8, 8 * r : 8 * r + 8])
    update(5, every, small_ref[8:16, 0:12])
    update(6, every, small_ref[0:6, 0:96])


class Place:
    def __init__(self):
        dp, mp = lax.axis_index("dp"), lax.axis_index("mp")
        self.z, self.y = dp // 2, dp % 2
        self.x, self.c = mp // 2, mp % 2

    def id(self, z=None, y=None, x=None, c=None):
        z, y, x, c = (own if new is None else new for own, new in ((self.z, z), (self.y, y), (self.x, x), (self.c, c)))
        return (2 * z + y, 2 * x + c)

    def neighbours(self):
        return [
            *(self.id(z=(self.z + k) % 4) for k in (1, 2, 3)),
            self.id(y=1 - self.y),
            self.id(x=1 - self.x),
            self.id(c=1 - self.c),
        ]

    def greet(self):
        barrier = pltpu.get_barrier_semaphore()
        for device in self.neighbours():
            pl.semaphore_signal(barrier, inc=1, device_id=device, device_id_type=MESH)
        pl.semaphore_wait(barrier, 6)


class Sends:
    def __init__(self, send, recv):
        self.send, self.recv, self.count, self.all = send, recv, 0, []

    def start(self, src, dst, device):
        copy = pltpu.make_async_remote_copy(
            src_ref=src,
            dst_ref=dst,
            send_sem=self.send.at[self.count],
            recv_sem=self.recv.at[self.count],
            device_id=device,
            device_id_type=MESH,
        )
        self.count += 1
        copy.start()
        self.all.append(copy)
        return copy

    def finish(self):
        for copy in self.all:
            copy.wait_send()


def arrived(copies):
    for copy in copies:
        copy.wait_recv()


class Gather:
    def __init__(self, place, sends, own, full, split):
        self.p, self.s, self.own, self.full, self.split = place, sends, own, full, split
        self.core = []

    def along_z(self):
        p = self.p
        slot = self.full.at[p.x, p.c, p.z, p.y]
        self.wait = [self.s.start(self.own, slot, p.id(z=(p.z + k) % 4)) for k in (1, 2, 3)]

    def second(self):
        p, f, s = self.p, self.full, self.s
        arrived(self.wait)
        upper, lower = pl.ds(0, self.split), pl.ds(self.split, f.shape[4] - self.split)
        part = f.at[p.x, p.c, :, p.y, upper]
        self.wait = [s.start(part, part, p.id(y=1 - p.y))]
        if self.split < f.shape[4]:
            part = f.at[p.x, p.c, :, p.y, lower]
            self.wait.append(s.start(part, part, p.id(x=1 - p.x)))
        part = f.at[p.x, p.c, :, p.y]
        self.core.append(s.start(part, part, p.id(c=1 - p.c)))

    def third(self):
        p, f, s = self.p, self.full, self.s
        arrived(self.wait)
        upper, lower = pl.ds(0, self.split), pl.ds(self.split, f.shape[4] - self.split)
        part = f.at[p.x, p.c, :, :, upper]
        self.wait = [s.start(part, part, p.id(x=1 - p.x))]
        core = [f.at[p.x, p.c, :, 1 - p.y, upper]]
        if self.split < f.shape[4]:
            for x in (0, 1):
                part = f.at[x, p.c, :, p.y, lower]
                self.wait.append(s.start(part, part, p.id(y=1 - p.y)))
            core.append(f.at[1 - p.x, p.c, :, p.y, lower])
        self.core += [s.start(part, part, p.id(c=1 - p.c)) for part in core]

    def last(self):
        p, f, s = self.p, self.full, self.s
        arrived(self.wait)
        upper, lower = pl.ds(0, self.split), pl.ds(self.split, f.shape[4] - self.split)
        core = [f.at[1 - p.x, p.c, :, :, upper]]
        if self.split < f.shape[4]:
            core += [f.at[x, p.c, :, 1 - p.y, lower] for x in (0, 1)]
        self.core += [s.start(part, part, p.id(c=1 - p.c)) for part in core]

    def done(self):
        arrived(self.core)

    COUNT = 14
    COUNT_WHOLE = 8


def gather_kernel(w_ref, s_ref, f1, f2, f3, fs, send, recv, local):
    p = Place()
    p.greet()
    s = Sends(send, recv)
    fulls = [(s_ref, fs, 16), (w_ref.at[0], f1, 48), (w_ref.at[1], f2, 48), (w_ref.at[2], f3, 48)]
    gathers = [Gather(p, s, own, full, split) for own, full, split in fulls]
    for g in gathers:
        g.along_z()
    copies = []
    for i, (own, full, _) in enumerate(fulls):
        copies.append(pltpu.make_async_copy(own, full.at[p.x, p.c, p.z, p.y], local.at[i]))
        copies[-1].start()
    for copy in copies:
        copy.wait()
    stages = [("second", 0), ("second", 1), ("third", 0), ("second", 2), ("third", 1), ("last", 0), ("second", 3),
              ("third", 2), ("last", 1), ("third", 3), ("last", 2), ("last", 3)]
    for name, i in stages:
        getattr(gathers[i], name)()
    for g in gathers:
        g.done()
    s.finish()


def add_into(target, other, lead):
    total = math.prod(lead)

    @pl.loop(0, total)
    def _(i):
        index = []
        for size in reversed(lead):
            index.append(i % size)
            i = i // size
        index = tuple(reversed(index))
        target[index] = (target[index].astype(F32) + other(*index).astype(F32)).astype(BF16)


class Reduce:
    def __init__(self, place, sends, parts, r0, r1a, r1b, r2a, r2b, r3a, r3b, split):
        self.p, self.s, self.parts, self.split = place, sends, parts, split
        self.r0, self.r1a, self.r1b, self.r2a, self.r2b, self.r3a, self.r3b = r0, r1a, r1b, r2a, r2b, r3a, r3b
        self.both = r1b is not None

    def cores(self):
        p = self.p
        self.wait = [self.s.start(self.parts.at[:, 1 - p.c], self.r0, p.id(c=1 - p.c))]

    def first(self):
        p, s, h = self.p, self.s, self.split
        arrived(self.wait)
        add_into(self.r0, lambda x, z, y: self.parts[x, p.c, z, y], self.r0.shape[:3])
        self.wait = [s.start(self.r0.at[1 - p.x, :, :, pl.ds(0, h)], self.r1a, p.id(x=1 - p.x))]
        if self.both:
            low = pl.ds(h, self.r0.shape[3] - h)
            self.wait.append(s.start(self.r0.at[:, :, 1 - p.y, low], self.r1b, p.id(y=1 - p.y)))

    def second(self):
        p, s, h = self.p, self.s, self.split
        arrived(self.wait)
        add_into(self.r1a, lambda z, y: self.r0[p.x, z, y, 0:h], self.r1a.shape[:2])
        self.wait = [s.start(self.r1a.at[:, 1 - p.y], self.r2a, p.id(y=1 - p.y))]
        if self.both:
            add_into(self.r1b, lambda x, z: self.r0[x, z, p.y, h:], self.r1b.shape[:2])
            self.wait.append(s.start(self.r1b.at[1 - p.x], self.r2b, p.id(x=1 - p.x)))

    def third(self):
        p, s = self.p, self.s
        arrived(self.wait)
        add_into(self.r2a, lambda z: self.r1a[z, p.y], self.r2a.shape[:1])
        if self.both:
            add_into(self.r2b, lambda z: self.r1b[p.x, z], self.r2b.shape[:1])
        self.wait = []
        for k in (1, 2, 3):
            to = (p.z + k) % 4
            self.wait.append(s.start(self.r2a.at[to], self.r3a.at[k - 1], p.id(z=to)))
            if self.both:
                self.wait.append(s.start(self.r2b.at[to], self.r3b.at[k - 1], p.id(z=to)))

    def last(self, out):
        p = self.p
        arrived(self.wait)
        sum_of = lambda r2, r3: r2[p.z].astype(F32) + r3[0].astype(F32) + r3[1].astype(F32) + r3[2].astype(F32)
        out[0 : self.split] = sum_of(self.r2a, self.r3a)
        if self.both:
            out[self.split :] = sum_of(self.r2b, self.r3b)

    @staticmethod
    def scratch(rows, columns, split):
        shapes = [(2, 4, 2, rows), (4, 2, split), (2, 4, rows - split), (4, split), (4, rows - split), (3, split), (3, rows - split)]
        return [pltpu.VMEM(shape + (columns,), BF16) for shape in shapes if shape[-1] > 0]


def reduce_kernel(g1, g2, g3, gs, own_out, own_in, total, small, all_out, all_in, *scratch):
    *buffers, send, recv, local = scratch
    p = Place()
    p.greet()
    s = Sends(send, recv)
    reduces = [Reduce(p, s, part, *buffers[7 * i : 7 * i + 7], 48) for i, part in enumerate((g3, g2, g1))]
    b = buffers[21:]
    reduces.append(Reduce(p, s, gs, b[0], b[1], None, b[2], None, b[3], None, 16))
    outs = [total.at[2], total.at[1], total.at[0], small]
    for r in reduces:
        r.cores()
    trades, copies = [], []
    for i, (own, full) in enumerate(((own_out, all_out), (own_in, all_in))):
        slot = full.at[p.x, p.c]
        copies.append(pltpu.make_async_copy(own, slot, local.at[i]))
        copies[-1].start()
    for i in range(4):
        reduces[i].first()
        if i > 0:
            reduces[i - 1].second()
        if i > 1:
            reduces[i - 2].third()
    for own, full in ((own_out, all_out), (own_in, all_in)):
        slot = full.at[p.x, p.c]
        trades.append([s.start(own, slot, p.id(x=1 - p.x)), s.start(own, slot, p.id(c=1 - p.c))])
    reduces[3].second()
    reduces[2].third()
    reduces[3].third()
    for r, out in zip(reduces, outs):
        r.last(out)
    for trade, full in zip(trades, (all_out, all_in)):
        arrived(trade[:1])
        slot = full.at[1 - p.x, p.c]
        trade.append(s.start(slot, slot, p.id(c=1 - p.c)))
    for trade in trades:
        arrived(trade[1:])
    for copy in copies:
        copy.wait()
    s.finish()


def fast_shards(*args):
    (tokens, cotangent, visible, tile_counts, *state) = args
    tile_count, seq, width = tokens.shape
    mp_size = lax.axis_size("mp")
    tiles = tile_count // mp_size
    pad = -(-seq // 16) * 16
    rows = tiles * pad
    native = lambda i, a: a.transpose(1, 0, 2) if i in (0, 4) else a.T if i in (3, 5) else a
    state = [native(i % 7, a) for i, a in enumerate(state)]
    params = lambda limit=None, **kw: pltpu.CompilerParams(vmem_limit_bytes=60 << 20, **kw)
    shape = jax.ShapeDtypeStruct
    me = lax.axis_index("mp").astype(jnp.int32)
    who = jnp.stack([me, tile_counts[0]])

    own, own_small = pl.pallas_call(
        pack_kernel,
        out_shape=(shape((3, 96, D), BF16), shape((16, 128), BF16)),
        scratch_shapes=[pltpu.VMEM((16, 128), F32)],
        compiler_params=params(),
        name="pack",
    )(*state[:7])

    full = shape((2, 2, 4, 2, 96, D), BF16)
    copies = 3 * Gather.COUNT + Gather.COUNT_WHOLE
    f1, f2, f3, fs = pl.pallas_call(
        gather_kernel,
        out_shape=(full, full, full, shape((2, 2, 4, 2, 16, 128), BF16)),
        in_specs=[pl.BlockSpec(memory_space=pltpu.VMEM)] * 2,
        out_specs=(pl.BlockSpec(memory_space=ANY),) * 4,
        scratch_shapes=[
            pltpu.SemaphoreType.DMA((copies,)),
            pltpu.SemaphoreType.DMA((copies,)),
            pltpu.SemaphoreType.DMA((4,)),
        ],
        compiler_params=params(collective_id=0, has_side_effects=True),
        name="gather",
    )(own, own_small)
    w1, w2, w3 = (f.reshape(4, D, D) for f in (f1, f2, f3))

    vec, off = pl.pallas_call(
        spread_kernel,
        out_shape=(shape((16, D), F32), shape((4, 8, D), F32)),
        compiler_params=params(),
        name="spread",
    )(fs.reshape(4, 8, 16, 128))

    by_place = lambda a: a.transpose(1, 0, 2)
    half = pl.BlockSpec((seq, 8, D), lambda m, who: (0, who[0] // 2, 0))
    of_group = lambda *shape: pl.BlockSpec((1,) + shape, lambda m, who: (m,) + (0,) * len(shape))
    all_of = lambda *shape: pl.BlockSpec(shape, lambda m, who: (0,) * len(shape))
    places = lax.dynamic_slice(visible, (me * tiles, 0), (tiles, seq)).T
    table = jnp.asarray(position_rows())

    x, h, qkv, probs, o = pl.pallas_call(
        functools.partial(attend_kernel, seq, pad, tiles),
        out_shape=(
            shape((rows, D), F32),
            shape((rows, D), F32),
            shape((4, rows, 576), BF16),
            shape((4, 3, rows, pad), BF16),
            shape((4, rows, 192), BF16),
        ),
        grid_spec=pltpu.PrefetchScalarGridSpec(
            num_scalar_prefetch=1,
            grid=(4,),
            in_specs=[half, all_of(seq, tiles), all_of(3, 128, D), all_of(16, D), of_group(8, D), of_group(D, D)],
            out_specs=(all_of(rows, D), all_of(rows, D), of_group(rows, 576), of_group(3, rows, pad), of_group(rows, 192)),
            scratch_shapes=[pltpu.VMEM((D // 128, seq * 8, 128), F32), pltpu.VMEM((rows, D), BF16)],
        ),
        compiler_params=params(),
        name="attend",
    )(who, by_place(tokens), places, table, vec, off, w1)

    out_own, dh, sum_two, sum_hid, g2, g3 = pl.pallas_call(
        functools.partial(feed_kernel, seq, pad, tiles),
        out_shape=(
            shape((rows, D), BF16),
            shape((rows, D), F32),
            shape((8, D), F32),
            shape((4, 8, D), F32),
            shape((4, D, D), BF16),
            shape((4, D, D), BF16),
        ),
        grid_spec=pltpu.PrefetchScalarGridSpec(
            num_scalar_prefetch=1,
            grid=(4,),
            in_specs=[half, all_of(rows, D), all_of(16, D), of_group(8, D), of_group(D, D), of_group(D, D)],
            out_specs=(all_of(rows, D), all_of(rows, D), all_of(8, D), of_group(8, D), of_group(D, D), of_group(D, D)),
            scratch_shapes=[
                pltpu.VMEM((D // 128, seq * 8, 128), F32),
                pltpu.VMEM((rows, D), BF16),
                pltpu.VMEM((D, rows), BF16),
                pltpu.VMEM((rows, D), BF16),
                pltpu.VMEM((D, rows), BF16),
                pltpu.VMEM((rows, D), F32),
                pltpu.VMEM((rows, D), F32),
            ],
        ),
        compiler_params=params(),
        name="feed",
    )(who, by_place(cotangent), h, vec, off, w2, w3)

    of_group1 = lambda *shape: pl.BlockSpec((1,) + shape, lambda m: (m,) + (0,) * len(shape))
    all_of1 = lambda *shape: pl.BlockSpec(shape, lambda m: (0,) * len(shape))
    in_own, sum_one, sum_head, g1 = pl.pallas_call(
        functools.partial(back_kernel, seq, pad, tiles),
        out_shape=(
            shape((rows, D), BF16),
            shape((8, D), F32),
            shape((4, 8, D), F32),
            shape((4, D, D), BF16),
        ),
        grid=(4,),
        in_specs=[all_of1(rows, D), all_of1(rows, D), all_of1(16, D), of_group1(D, D), of_group1(rows, 576),
                  of_group1(3, rows, pad), of_group1(rows, 192)],
        out_specs=(all_of1(rows, D), all_of1(8, D), of_group1(8, D), of_group1(D, D)),
        scratch_shapes=[
            pltpu.VMEM((D, rows), BF16),
            pltpu.VMEM((rows, D), BF16),
            pltpu.VMEM((D, rows), BF16),
            pltpu.VMEM((rows, 192), BF16),
            pltpu.VMEM((rows, 576), BF16),
            pltpu.VMEM((rows, D), F32),
        ],
        compiler_params=params(),
        name="back",
    )(x, dh, vec, w1, qkv, probs, o)

    gs = pl.pallas_call(
        squeeze_kernel,
        out_shape=shape((4, 8, 16, 128), BF16),
        scratch_shapes=[pltpu.VMEM((8, D), F32)],
        compiler_params=params(),
        name="squeeze",
    )(sum_two, sum_one, sum_hid, sum_head)

    copies = 3 * 11 + 6 + 6
    everyone = shape((2, 2, rows, D), BF16)
    total, small, all_out, all_in = pl.pallas_call(
        reduce_kernel,
        out_shape=(shape((3, 96, D), F32), shape((16, 128), F32), everyone, everyone),
        in_specs=[pl.BlockSpec(memory_space=pltpu.VMEM)] * 4 + [pl.BlockSpec(memory_space=ANY)] * 2,
        out_specs=(pl.BlockSpec(memory_space=pltpu.VMEM),) * 2 + (pl.BlockSpec(memory_space=ANY),) * 2,
        scratch_shapes=[
            *(3 * Reduce.scratch(96, D, 48)),
            *Reduce.scratch(16, 128, 16),
            pltpu.SemaphoreType.DMA((copies,)),
            pltpu.SemaphoreType.DMA((copies,)),
            pltpu.SemaphoreType.DMA((2,)),
        ],
        compiler_params=params(collective_id=1, has_side_effects=True),
        name="reduce",
    )(*(g.reshape(2, 2, 4, 2, 96, D) for g in (g1, g2, g3)), gs.reshape(2, 2, 4, 2, 16, 128), out_own, in_own)

    flat = seq * tile_count
    block = pl.BlockSpec((tile_count, pad, 128), lambda n: (0, 0, n))
    output, input_grad = pl.pallas_call(
        functools.partial(lay_kernel, seq, pad, tile_count),
        out_shape=(shape((flat, D), BF16), shape((flat, D), F32)),
        grid=(D // 128,),
        in_specs=[block, block],
        out_specs=(pl.BlockSpec((flat, 128), lambda n: (0, n)),) * 2,
        scratch_shapes=[pltpu.VMEM((flat, 128), F32)],
        compiler_params=params(),
        name="lay",
    )(*(a.reshape(tile_count, pad, D) for a in (all_out, all_in)))
    output, input_grad = (a.reshape(seq, tile_count, D).transpose(1, 0, 2) for a in (output, input_grad))

    kinds = [shape(a.shape, F32) for a in state[:7]]
    results = pl.pallas_call(
        update_kernel,
        out_shape=tuple(kinds * 4 + [shape(a.shape, BF16) for a in kinds]),
        compiler_params=params(),
        name="update",
    )(total, small, *state)
    return (output, input_grad) + tuple(native(i % 7, a) for i, a in enumerate(results))


def solution(mesh):
    in_specs = (
        P("dp", None, None),
        P("dp", None, None),
        P("dp", None),
        P("dp"),
        P("dp", None, "mp"),
        P("mp", "dp"),
        P("dp", "mp"),
        P("mp", "dp"),
        P(None, "mp", "dp"),
        P("mp", "dp"),
        P(None, "dp"),
        P("dp", None, "mp"),
        P("mp", "dp"),
        P("dp", "mp"),
        P("mp", "dp"),
        P(None, "mp", "dp"),
        P("mp", "dp"),
        P(None, "dp"),
        P("dp", None, "mp"),
        P("mp", "dp"),
        P("dp", "mp"),
        P("mp", "dp"),
        P(None, "mp", "dp"),
        P("mp", "dp"),
        P(None, "dp"),
    )
    out_specs = (
        P("dp", None, None),
        P("dp", None, None),
        P("dp", None, "mp"),
        P("mp", "dp"),
        P("dp", "mp"),
        P("mp", "dp"),
        P(None, "mp", "dp"),
        P("mp", "dp"),
        P(None, "dp"),
        P("dp", None, "mp"),
        P("mp", "dp"),
        P("dp", "mp"),
        P("mp", "dp"),
        P(None, "mp", "dp"),
        P("mp", "dp"),
        P(None, "dp"),
        P("dp", None, "mp"),
        P("mp", "dp"),
        P("dp", "mp"),
        P("mp", "dp"),
        P(None, "mp", "dp"),
        P("mp", "dp"),
        P(None, "dp"),
        P("dp", None, "mp"),
        P("mp", "dp"),
        P("dp", "mp"),
        P("mp", "dp"),
        P(None, "mp", "dp"),
        P("mp", "dp"),
        P(None, "dp"),
        P("dp", None, "mp"),
        P("mp", "dp"),
        P("dp", "mp"),
        P("mp", "dp"),
        P(None, "mp", "dp"),
        P("mp", "dp"),
        P(None, "dp"),
    )
    sizes = (mesh.shape["dp"], mesh.shape["mp"])
    body = fast_shards if sizes == (8, 4) else shards
    return jax.shard_map(body, mesh=mesh, in_specs=in_specs, out_specs=out_specs, check_vma=False)
```

```python
import functools
import math

import jax
import jax.numpy as jnp
import numpy as np
from jax import lax
from jax.experimental import pallas as pl
from jax.experimental.pallas import tpu as pltpu
from jax.sharding import PartitionSpec as P

D = 768
FF = 3072
GRID = 14
STEP = 3


LN_EPS = 1e-06
BETA_ONE = 0.5
BETA_TWO = 0.5
ADAM_EPS = 1e-08
DECAY = 0.05


def cut_along(x, dim, size):
    dims = x.shape
    parts = x.reshape(*dims[:dim], size, dims[dim] // size, *dims[dim + 1 :])
    return jnp.moveaxis(parts, dim, 0)


def summed_on_arrival(x, axis, dim):
    size = lax.axis_size(axis)
    parts = lax.all_to_all(cut_along(x, dim, size), axis, 0, 0, tiled=True)
    return jnp.sum(parts.astype(jnp.float32), axis=0)


def sine_table(places, feature_width):
    half_width = feature_width // 2
    spread = jnp.arange(half_width, dtype=jnp.float32) / half_width
    frequency = jnp.exp(-math.log(10000.0) * spread)
    angles = places[..., None] * frequency
    return jnp.concatenate([jnp.sin(angles), jnp.cos(angles)], axis=-1)


def position_table(visible, feature_width):
    plane_size = GRID * GRID
    frame_place = (visible // plane_size).astype(jnp.float32)
    within = visible % plane_size
    row_place = (within // GRID).astype(jnp.float32)
    column_place = (within % GRID).astype(jnp.float32)
    time_width = feature_width // 16 * 4
    space_width = feature_width // 16 * 6
    return jnp.concatenate(
        [
            sine_table(frame_place, time_width),
            sine_table(row_place, space_width),
            sine_table(column_place, space_width),
        ],
        axis=-1,
    )


def normalize(values):
    center = values - jnp.mean(values, axis=-1, keepdims=True)
    inverse = lax.rsqrt(jnp.mean(center * center, axis=-1, keepdims=True) + LN_EPS)
    return (center * inverse, inverse)


def norm_back(grad_normed, normed, inverse):
    return inverse * (
        grad_normed
        - jnp.mean(grad_normed, axis=-1, keepdims=True)
        - normed * jnp.mean(grad_normed * normed, axis=-1, keepdims=True)
    )


def over_rows(former, latter):
    return lax.dot_general(
        former, latter, (((0,), (0,)), ((), ())), preferred_element_type=jnp.float32
    )


def over_cols(former, latter):
    return lax.dot_general(
        former, latter, (((1,), (1,)), ((), ())), preferred_element_type=jnp.float32
    )


def exact_gelu(values):
    return jax.nn.gelu(values, approximate=False)


def adamw_update(
    master, first_moment, second_moment, gradient, step_rate, weight_decay, correction
):
    first_new = BETA_ONE * first_moment + (1.0 - BETA_ONE) * gradient
    second_new = BETA_TWO * second_moment + (1.0 - BETA_TWO) * gradient * gradient
    ratio = first_new / correction / (jnp.sqrt(second_new / correction) + ADAM_EPS)
    master_new = master - step_rate * (ratio + weight_decay * master)
    return (master_new, first_new, second_new)


def shards(
    tokens,
    cotangent,
    visible,
    tile_counts,
    attend_weight,
    project_weight,
    widen_weight,
    narrow_weight,
    heads_offset,
    hidden_offset,
    layer_vectors,
    attend_first,
    project_first,
    widen_first,
    narrow_first,
    heads_first,
    hidden_first,
    vectors_first,
    attend_second,
    project_second,
    widen_second,
    narrow_second,
    heads_second,
    hidden_second,
    vectors_second,
):
    fore_attend, fore_project, fore_widen, fore_narrow, fore_heads, fore_hidden, fore_vectors = (
        lax.all_gather(attend_weight.astype(jnp.bfloat16), "dp", axis=0, tiled=True),
        lax.all_gather(project_weight.astype(jnp.bfloat16), "dp", axis=1, tiled=True),
        lax.all_gather(widen_weight.astype(jnp.bfloat16), "dp", axis=0, tiled=True),
        lax.all_gather(narrow_weight.astype(jnp.bfloat16), "dp", axis=1, tiled=True),
        lax.all_gather(heads_offset.astype(jnp.bfloat16), "dp", axis=2, tiled=True),
        lax.all_gather(hidden_offset.astype(jnp.bfloat16), "dp", axis=1, tiled=True),
        lax.all_gather(layer_vectors.astype(jnp.bfloat16), "dp", axis=1, tiled=True),
    )
    tile_count, seq_length, model_width = tokens.shape
    row_count = tile_count * seq_length
    local_width = fore_attend.shape[2]
    heads_local = fore_heads.shape[1]
    head_size = fore_heads.shape[2]
    score_scale = 1.0 / math.sqrt(head_size)
    live_tiles = (jnp.arange(tile_count, dtype=jnp.int32) < tile_counts[0]).astype(jnp.float32)
    live_rows = jnp.broadcast_to(live_tiles[:, None], (tile_count, seq_length)).reshape(
        row_count, 1
    )
    vectors = fore_vectors.astype(jnp.float32)
    summed = (tokens.astype(jnp.float32) + position_table(visible, model_width)).reshape(
        row_count, model_width
    )
    normed_one, inverse_one = normalize(summed)
    attend_low = (normed_one * vectors[0] + vectors[1]).astype(jnp.bfloat16)
    linear = jnp.dot(
        attend_low,
        fore_attend.reshape(model_width, 3 * local_width),
        preferred_element_type=jnp.float32,
    ).reshape(row_count, 3, local_width)
    offsets = fore_heads.astype(jnp.float32).reshape(2, local_width)
    head_shape = (tile_count, seq_length, heads_local, head_size)
    query_low = (linear[:, 0] + offsets[0]).astype(jnp.bfloat16).reshape(head_shape)
    key_low = linear[:, 1].astype(jnp.bfloat16).reshape(head_shape)
    value_low = (linear[:, 2] + offsets[1]).astype(jnp.bfloat16).reshape(head_shape)
    scores = (
        jnp.einsum("tqhd,tkhd->thqk", query_low, key_low, preferred_element_type=jnp.float32)
        * score_scale
    )
    row_top = jnp.max(scores, axis=-1, keepdims=True)
    log_total = row_top + jnp.log(jnp.sum(jnp.exp(scores - row_top), axis=-1, keepdims=True))
    weights_low = jnp.exp(scores - log_total).astype(jnp.bfloat16)
    context = jnp.einsum(
        "thqk,tkhd->tqhd", weights_low, value_low, preferred_element_type=jnp.float32
    )
    context_low = context.reshape(row_count, local_width).astype(jnp.bfloat16)
    attention_part = jnp.dot(context_low, fore_project, preferred_element_type=jnp.float32)
    attention = lax.psum(attention_part.astype(jnp.bfloat16), "mp").astype(jnp.float32)
    middle = summed + attention + vectors[4]
    normed_two, inverse_two = normalize(middle)
    widen_low = (normed_two * vectors[2] + vectors[3]).astype(jnp.bfloat16)
    hidden = jnp.dot(
        widen_low, fore_widen, preferred_element_type=jnp.float32
    ) + fore_hidden.astype(jnp.float32).reshape(-1)
    active_low = exact_gelu(hidden).astype(jnp.bfloat16)
    feed_part = jnp.dot(active_low, fore_narrow, preferred_element_type=jnp.float32)
    feed_sum = lax.psum(feed_part.astype(jnp.bfloat16), "mp").astype(jnp.float32)
    result = (middle + feed_sum + vectors[5]) * live_rows
    output_low = result.astype(jnp.bfloat16)
    back_attend, back_project, back_widen, back_narrow, back_vectors = (
        fore_attend,
        fore_project,
        fore_widen,
        fore_narrow,
        fore_vectors,
    )
    vectors_back = back_vectors.astype(jnp.float32)
    grad_out = cotangent.astype(jnp.float32).reshape(row_count, model_width) * live_rows
    grad_out_low = grad_out.astype(jnp.bfloat16)
    grad_narrow = over_rows(active_low, grad_out_low)
    grad_active = over_cols(grad_out_low, back_narrow)
    gelu_back = jax.vjp(exact_gelu, hidden)[1]
    grad_hidden_low = gelu_back(grad_active)[0].astype(jnp.bfloat16)
    grad_widen = over_rows(widen_low, grad_hidden_low)
    grad_hidden = jnp.sum(grad_hidden_low.astype(jnp.float32), axis=0).reshape(fore_hidden.shape)
    normed_two_part = over_cols(grad_hidden_low, back_widen)
    grad_normed_two = lax.psum(normed_two_part.astype(jnp.bfloat16), "mp").astype(jnp.float32)
    grad_middle = grad_out + norm_back(grad_normed_two * vectors_back[2], normed_two, inverse_two)
    grad_middle_low = grad_middle.astype(jnp.bfloat16)
    grad_project = over_rows(context_low, grad_middle_low)
    grad_context_low = (
        over_cols(grad_middle_low, back_project).astype(jnp.bfloat16).reshape(head_shape)
    )
    scores_again = (
        jnp.einsum("tqhd,tkhd->thqk", query_low, key_low, preferred_element_type=jnp.float32)
        * score_scale
    )
    weights_full = jnp.exp(scores_again - log_total)
    weights_again_low = weights_full.astype(jnp.bfloat16)
    grad_weights = jnp.einsum(
        "tqhd,tkhd->thqk", grad_context_low, value_low, preferred_element_type=jnp.float32
    )
    grad_value = jnp.einsum(
        "thqk,tqhd->tkhd", weights_again_low, grad_context_low, preferred_element_type=jnp.float32
    )
    row_dot = jnp.sum(grad_weights * weights_full, axis=-1, keepdims=True)
    grad_scores_low = (weights_full * (grad_weights - row_dot)).astype(jnp.bfloat16)
    grad_query = (
        jnp.einsum("thqk,tkhd->tqhd", grad_scores_low, key_low, preferred_element_type=jnp.float32)
        * score_scale
    )
    grad_key = (
        jnp.einsum(
            "thqk,tqhd->tkhd", grad_scores_low, query_low, preferred_element_type=jnp.float32
        )
        * score_scale
    )
    grad_qkv_low = jnp.stack(
        [
            grad_query.reshape(row_count, local_width),
            grad_key.reshape(row_count, local_width),
            grad_value.reshape(row_count, local_width),
        ],
        axis=1,
    ).astype(jnp.bfloat16)
    grad_offsets = jnp.sum(grad_qkv_low.astype(jnp.float32), axis=0)
    grad_heads = jnp.stack([grad_offsets[0], grad_offsets[2]]).reshape(2, heads_local, head_size)
    flat_qkv = grad_qkv_low.reshape(row_count, 3 * local_width)
    grad_attend = over_rows(attend_low, flat_qkv).reshape(model_width, 3, local_width)
    normed_one_part = over_cols(flat_qkv, back_attend.reshape(model_width, 3 * local_width))
    grad_normed_one = lax.psum(normed_one_part.astype(jnp.bfloat16), "mp").astype(jnp.float32)
    grad_inputs = grad_middle + norm_back(
        grad_normed_one * vectors_back[0], normed_one, inverse_one
    )
    grad_vectors = jnp.stack(
        [
            jnp.sum(grad_normed_one * normed_one, axis=0),
            jnp.sum(grad_normed_one, axis=0),
            jnp.sum(grad_normed_two * normed_two, axis=0),
            jnp.sum(grad_normed_two, axis=0),
            jnp.sum(grad_middle, axis=0),
            jnp.sum(grad_out, axis=0),
        ]
    )
    output = output_low.reshape(tile_count, seq_length, model_width)
    input_grad = grad_inputs.reshape(tile_count, seq_length, model_width)
    (
        shard_attend,
        shard_project,
        shard_widen,
        shard_narrow,
        shard_heads,
        shard_hidden,
        shard_vectors,
    ) = (
        summed_on_arrival(grad_attend.astype(jnp.bfloat16), "dp", 0),
        summed_on_arrival(grad_project.astype(jnp.bfloat16), "dp", 1),
        summed_on_arrival(grad_widen.astype(jnp.bfloat16), "dp", 0),
        summed_on_arrival(grad_narrow.astype(jnp.bfloat16), "dp", 1),
        summed_on_arrival(grad_heads.astype(jnp.bfloat16), "dp", 2),
        summed_on_arrival(grad_hidden.astype(jnp.bfloat16), "dp", 1),
        summed_on_arrival(grad_vectors.astype(jnp.bfloat16), "dp", 1),
    )
    correction = 1.0 - 0.5**STEP
    new_attend, first_attend, second_attend = adamw_update(
        attend_weight,
        attend_first,
        attend_second,
        shard_attend,
        (D // 2) ** (-0.5),
        DECAY,
        correction,
    )
    new_project, first_project, second_project = adamw_update(
        project_weight,
        project_first,
        project_second,
        shard_project,
        (D // 16) ** (-0.5),
        DECAY,
        correction,
    )
    new_widen, first_widen, second_widen = adamw_update(
        widen_weight, widen_first, widen_second, shard_widen, D ** (-0.5), DECAY, correction
    )
    new_narrow, first_narrow, second_narrow = adamw_update(
        narrow_weight, narrow_first, narrow_second, shard_narrow, FF ** (-0.5), DECAY, correction
    )
    new_heads, first_heads, second_heads = adamw_update(
        heads_offset, heads_first, heads_second, shard_heads, 0.1, 0.0, correction
    )
    new_hidden, first_hidden, second_hidden = adamw_update(
        hidden_offset, hidden_first, hidden_second, shard_hidden, 0.1, 0.0, correction
    )
    new_vectors, first_vectors, second_vectors = adamw_update(
        layer_vectors, vectors_first, vectors_second, shard_vectors, 0.15, 0.0, correction
    )
    return (
        output,
        input_grad,
        shard_attend,
        shard_project,
        shard_widen,
        shard_narrow,
        shard_heads,
        shard_hidden,
        shard_vectors,
        new_attend,
        new_project,
        new_widen,
        new_narrow,
        new_heads,
        new_hidden,
        new_vectors,
        first_attend,
        first_project,
        first_widen,
        first_narrow,
        first_heads,
        first_hidden,
        first_vectors,
        second_attend,
        second_project,
        second_widen,
        second_narrow,
        second_heads,
        second_hidden,
        second_vectors,
        new_attend.astype(jnp.bfloat16),
        new_project.astype(jnp.bfloat16),
        new_widen.astype(jnp.bfloat16),
        new_narrow.astype(jnp.bfloat16),
        new_heads.astype(jnp.bfloat16),
        new_hidden.astype(jnp.bfloat16),
        new_vectors.astype(jnp.bfloat16),
    )


F32 = jnp.float32
BF16 = jnp.bfloat16
MESH = pl.DeviceIdType.MESH
ANY = pl.ANY


def nn(former, latter):
    return lax.dot_general(former, latter, (((1,), (0,)), ((), ())), preferred_element_type=F32)


def nt(former, latter):
    return lax.dot_general(former, latter, (((1,), (1,)), ((), ())), preferred_element_type=F32)


def tn(former, latter):
    return lax.dot_general(former, latter, (((0,), (0,)), ((), ())), preferred_element_type=F32)


def iota(shape, dim):
    return lax.broadcasted_iota(jnp.int32, shape, dim)


def whole(ref_shape):
    rank = len(ref_shape)
    return pl.BlockSpec(ref_shape, lambda *_: (0,) * rank)


def pick_vector(d):
    shape = (128, D)
    lane, column = iota(shape, 0), iota(shape, 1)
    return ((column - lane == 96 * d) & (lane < 96)).astype(F32).astype(BF16)


def pick_head(d):
    shape = (128, D)
    lane, column = iota(shape, 0), iota(shape, 1)
    same = (lax.shift_right_logical(column, 6) == lax.shift_right_logical(lane, 3)) & ((column & 7) == (lane & 7))
    return (same & ((lax.shift_right_logical(column, 3) & 7) == d) & (lane < 24)).astype(F32).astype(BF16)


def pick_row():
    shape = (128, D)
    return (lax.shift_right_logical(iota(shape, 1), 6) == iota(shape, 0)).astype(F32).astype(BF16)


def hidden_places(d):
    shape = (8, D)
    column = iota(shape, 1)
    return ((column & 7) == iota(shape, 0)) & ((lax.shift_right_logical(column, 3) & 7) == d)


def pack_kernel(attend, project, widen, narrow, heads, hidden, vectors, w_out, s_out, scratch):
    w_out[0] = jnp.concatenate([attend[0], attend[1], attend[2], project[...].T], axis=1).astype(BF16)
    w_out[1] = widen[...].astype(BF16)
    w_out[2] = narrow[...].astype(BF16)
    scratch[...] = jnp.zeros_like(scratch)
    scratch[0:6, 0:96] = vectors[...]
    for r in range(3):
        scratch[6:8, 8 * r : 8 * r + 8] = heads[r]
    scratch[8:16, 0:12] = hidden[...]
    s_out[...] = scratch[...].astype(BF16)


def spread_kernel(s_ref, vec_out, off_out):
    row_pick = pick_row()
    vec = jnp.zeros((16, D), F32)
    heads = [jnp.zeros((16, D), F32) for _ in range(4)]
    hidden = [jnp.zeros((1, D), F32) for _ in range(4)]
    for d in range(8):
        vec += nn(s_ref[0, d], pick_vector(d))
        head_pick, places = pick_head(d), hidden_places(d)
        for m in range(4):
            heads[m] += nn(s_ref[m, d], head_pick)
            spread = nn(s_ref[m, d], row_pick)[8:16]
            hidden[m] += jnp.sum(jnp.where(places, spread, 0.0), axis=0, keepdims=True)
    vec_out[...] = vec
    for m in range(4):
        off_out[m, 0:2, :] = heads[m][6:8]
        off_out[m, 2:3, :] = hidden[m]
        off_out[m, 3:8, :] = jnp.zeros((5, D), F32)


def squeeze_kernel(fore_ref, back_ref, hid_ref, heads_ref, out_ref, rows):
    rows[...] = jnp.zeros_like(rows)
    rows[0:2, :] = back_ref[0:2, :]
    rows[2:6, :] = fore_ref[0:4, :]
    row_pick = pick_row()
    shape = (8, 128)
    for m in range(4):
        rows[6:7, 0:192] = heads_ref[m, 0:1, 0:192]
        rows[7:8, 0:192] = heads_ref[m, 1:2, 0:192]
        block = rows[...].astype(BF16)
        wide = jnp.broadcast_to(hid_ref[m, 0:1, :], (8, D))
        for d in range(8):
            upper = jnp.where(iota(shape, 0) < 6, nt(block, pick_vector(d)), nt(block, pick_head(d)))
            lower = nt(jnp.where(hidden_places(d), wide, 0.0).astype(BF16), row_pick)
            out_ref[m, d] = jnp.concatenate([upper, lower], axis=0).astype(BF16)


def ln(values):
    center = values - jnp.mean(values, axis=-1, keepdims=True)
    inverse = lax.rsqrt(jnp.mean(center * center, axis=-1, keepdims=True) + LN_EPS)
    return center * inverse, inverse


def ln_back(grad, normed, inverse):
    return inverse * (
        grad
        - jnp.mean(grad, axis=-1, keepdims=True)
        - normed * jnp.mean(grad * normed, axis=-1, keepdims=True)
    )


def position_rows():
    plane = np.zeros((128, D), np.float32)
    time_width, space_width = D // 16 * 4, D // 16 * 6

    def sines(count, width):
        half = width // 2
        spread = np.arange(half, dtype=np.float32) / np.float32(half)
        frequency = np.exp(np.float32(-math.log(10000.0)) * spread).astype(np.float32)
        angles = np.arange(count, dtype=np.float32)[:, None] * frequency
        return np.concatenate([np.sin(angles), np.cos(angles)], axis=-1).astype(np.float32)

    plane[0:3, 0:time_width] = sines(3, time_width)
    plane[3 : 3 + GRID, time_width : time_width + space_width] = sines(GRID, space_width)
    plane[3 + GRID : 3 + 2 * GRID, time_width + space_width :] = sines(GRID, space_width)
    parts, rest = [], plane
    for _ in range(3):
        part = rest.astype(jnp.bfloat16)
        parts.append(part)
        rest = rest - part.astype(np.float32)
    return np.stack(parts)


def spread_lanes(ref, wide):
    for g in range(D // 128):
        part = ref[:, :, 128 * g : 128 * g + 128].astype(F32)
        wide[g] = part.reshape(part.shape[0] * 8, 128)


def place_rows(places):
    frame = (places >= GRID * GRID).astype(jnp.int32) + (places >= 2 * GRID * GRID).astype(jnp.int32)
    within = places - frame * (GRID * GRID)
    row = jnp.floor((within.astype(F32) + 0.5) * (1.0 / GRID)).astype(jnp.int32)
    column = within - row * GRID
    lane = iota((places.shape[0], 128), 1)
    hot = (lane == frame) | (lane == 3 + row) | (lane == 3 + GRID + column)
    return hot.astype(F32).astype(BF16)


def prep_kernel(seq, pad, tiles, who, tok_ref, cot_ref, vis_ref, tab_ref, x_out, dy_out, wide, grad):
    at = (who[0] & 1) * tiles
    first = who[0] * tiles
    head = seq - seq % 8
    spread_lanes(tok_ref, wide)
    for t in range(tiles):
        hot = place_rows(vis_ref[:, t : t + 1])
        table = nn(hot, tab_ref[0]) + nn(hot, tab_ref[1]) + nn(hot, tab_ref[2])
        x_out[t * pad + head : (t + 1) * pad, :] = jnp.zeros((pad - head, D), F32)
        for g in range(D // 128):
            lanes = slice(128 * g, 128 * g + 128)
            x_out[t * pad : t * pad + seq, lanes] = wide[g, pl.ds(at + t, seq, stride=8), :] + table[:, lanes]
    spread_lanes(cot_ref, wide)
    for t in range(tiles):
        live = (first + t < who[1]).astype(F32)
        grad[t * pad + head : (t + 1) * pad, :] = jnp.zeros((pad - head, D), F32)
        for g in range(D // 128):
            lanes = slice(128 * g, 128 * g + 128)
            grad[t * pad : t * pad + seq, lanes] = wide[g, pl.ds(at + t, seq, stride=8), :] * live
    dy_out[...] = grad[...].astype(BF16)


def attend_kernel(seq, pad, tiles, x_ref, vec_ref, off_ref, w_ref, col2, own3,
                  h_out, qkv_out, p_out, o_out, f2, f3, low, send, recv, local):
    m = pl.program_id(0)
    rows_of = lambda t: pl.ds(pl.multiple_of(t * pad, 16), pad)
    p = Place()
    s = Sends(send, recv)
    g2 = Gather(p, s, f2, 48, column=col2)
    g3 = Gather(p, s, f3, 48, own=own3)
    mine = [
        pltpu.make_async_copy(col2, f2.at[p.x, p.c, :, p.y], local.at[0]),
        pltpu.make_async_copy(own3, f3.at[p.x, p.c, p.z, p.y], local.at[1]),
    ]

    @pl.when(m == 0)
    def _():
        p.greet()
        g2.second()
        g3.along_z()
        for copy in mine:
            copy.start()

        @pl.loop(0, tiles)
        def _(t):
            x = x_ref[rows_of(t), :]
            normed, _ = ln(x)
            low[rows_of(t), :] = (normed * vec_ref[0:1, :] + vec_ref[1:2, :]).astype(BF16)
            h_out[rows_of(t), :] = x + vec_ref[4:5, :]

    linear = nn(low[...], w_ref[0, :, 0:576])
    zero = jnp.zeros((1, 192), F32)
    offset = jnp.concatenate([off_ref[0, 0:1, 0:192], zero, off_ref[0, 1:2, 0:192]], axis=1)
    qkv_out[0] = (linear + offset).astype(BF16)

    @pl.loop(0, tiles)
    def _(t):
        rows = rows_of(t)
        qkv = qkv_out[0, rows, :]
        parts = []
        for h in range(3):
            q, k, v = (qkv[:, 192 * j + 64 * h : 192 * j + 64 * h + 64] for j in range(3))
            s = nt(q, k) * 0.125
            s = jnp.where(iota(s.shape, 1) < seq, s, -1e30)
            e = jnp.exp(s - jnp.max(s, axis=-1, keepdims=True))
            low_p = (e * (1.0 / jnp.sum(e, axis=-1, keepdims=True))).astype(BF16)
            p_out[0, h, rows, :] = low_p
            parts.append(nn(low_p, v))
        o_out[0, rows, :] = jnp.concatenate(parts, axis=1).astype(BF16)

    h_out[...] += nt(o_out[0], w_ref[0, :, 576:768])

    @pl.when(m == 0)
    def _():
        for copy in mine:
            copy.wait()
        g2.third()

    @pl.when(m == 1)
    def _():
        g3.second()

    @pl.when(m == 2)
    def _():
        g2.last()

    @pl.when(m == 3)
    def _():
        g3.third()
        g3.last()
        g2.done()
        g3.done()
        s.finish()


def feed_kernel(seq, pad, tiles, who, dy, h_ref, vec_ref, off_ref, w2_ref, w3_ref,
                out_out, dh_out, sum_out, hid_out, g2_out, g3_out, c, c_t, dy_t, y, dc):
    m = pl.program_id(0)
    rows_of = lambda t: pl.ds(pl.multiple_of(t * pad, 16), pad)
    first = who[0] * tiles

    @pl.when(m == 0)
    def _():
        sum_out[...] = jnp.zeros_like(sum_out)

        @pl.loop(0, tiles)
        def _(t):
            sum_out[3:4, :] += jnp.sum(dy[rows_of(t), :].astype(F32), axis=0, keepdims=True)
            normed, _ = ln(h_ref[rows_of(t), :])
            c[rows_of(t), :] = (normed * vec_ref[2:3, :] + vec_ref[3:4, :]).astype(BF16)

        dy_t[...] = dy[...].T
        c_t[...] = c[...].T
        y[...] = jnp.zeros_like(y)
        dc[...] = jnp.zeros_like(dc)

    @pl.loop(0, 3)
    def _(n):
        cols = pl.ds(pl.multiple_of(n * 256, 256), 256)
        u = nn(c[...], w2_ref[0, :, cols]) + off_ref[0, 2:3, cols]
        cdf = 0.5 * (1.0 + lax.erf(u * math.sqrt(0.5)))
        r = (u * cdf).astype(BF16)
        slope = cdf + u * (jnp.exp(-0.5 * u * u) * (1.0 / math.sqrt(2.0 * math.pi)))
        g3_out[0, :, cols] = nn(dy_t[...], r).astype(BF16)
        du = (nn(dy[...], w3_ref[0, :, cols]) * slope).astype(BF16)
        hid_out[0, 0:1, cols] = jnp.sum(du.astype(F32), axis=0, keepdims=True)
        g2_out[0, :, cols] = nn(c_t[...], du).astype(BF16)
        y[...] += nt(r, w3_ref[0, :, cols])
        dc[...] += nt(du, w2_ref[0, :, cols])

    @pl.when(m == pl.num_programs(0) - 1)
    def _():
        @pl.loop(0, tiles)
        def _(t):
            rows = rows_of(t)
            live = (first + t < who[1]).astype(F32)
            h = h_ref[rows, :]
            out_out[rows, :] = ((h + y[rows, :] + vec_ref[5:6, :]) * live).astype(BF16)
            normed, inverse = ln(h)
            grad = dc[rows, :]
            dh = dy[rows, :].astype(F32) + ln_back(grad * vec_ref[2:3, :], normed, inverse)
            dh_out[rows, :] = dh
            sum_out[0:1, :] += jnp.sum(grad * normed, axis=0, keepdims=True)
            sum_out[1:2, :] += jnp.sum(grad, axis=0, keepdims=True)
            sum_out[2:3, :] += jnp.sum(dh, axis=0, keepdims=True)


def back_kernel(seq, pad, tiles, x_ref, dh_ref, vec_ref, w_ref, qkv_ref, p_ref, o_ref,
                in_out, sum_out, head_out, g1_out, a_t, dh_low, dh_t, do, dqkv, da):
    m = pl.program_id(0)
    rows_of = lambda t: pl.ds(pl.multiple_of(t * pad, 16), pad)

    @pl.when(m == 0)
    def _():
        @pl.loop(0, tiles)
        def _(t):
            rows = rows_of(t)
            normed, _ = ln(x_ref[rows, :])
            dh_low[rows, :] = (normed * vec_ref[0:1, :] + vec_ref[1:2, :]).astype(BF16)

        a_t[...] = dh_low[...].T
        dh_low[...] = dh_ref[...].astype(BF16)
        dh_t[...] = dh_low[...].T
        da[...] = jnp.zeros_like(da)
        sum_out[...] = jnp.zeros_like(sum_out)

    do[...] = nn(dh_low[...], w_ref[0, :, 576:768]).astype(BF16)
    g1_out[0, :, 576:768] = nn(dh_t[...], o_ref[0]).astype(BF16)

    @pl.loop(0, tiles)
    def _(t):
        rows = rows_of(t)
        qkv = qkv_ref[0, rows, :]
        grad = do[rows, :]
        parts = [[], [], []]
        for h in range(3):
            q, k, v = (qkv[:, 192 * j + 64 * h : 192 * j + 64 * h + 64] for j in range(3))
            g = grad[:, 64 * h : 64 * h + 64]
            low_p = p_ref[0, h, rows, :]
            p = low_p.astype(F32)
            dp = nt(g, v)
            ds = (p * (dp - jnp.sum(dp * p, axis=-1, keepdims=True))).astype(BF16)
            parts[0].append(nn(ds, k) * 0.125)
            parts[1].append(tn(ds, q) * 0.125)
            parts[2].append(tn(low_p, g))
        dqkv[rows, :] = jnp.concatenate(parts[0] + parts[1] + parts[2], axis=1).astype(BF16)

    sums = jnp.sum(dqkv[...].astype(F32), axis=0, keepdims=True)
    head_out[0, 0:1, 0:192] = sums[:, 0:192]
    head_out[0, 1:2, 0:192] = sums[:, 384:576]
    g1_out[0, :, 0:576] = nn(a_t[...], dqkv[...]).astype(BF16)
    da[...] += nt(dqkv[...], w_ref[0, :, 0:576])

    @pl.when(m == pl.num_programs(0) - 1)
    def _():
        @pl.loop(0, tiles)
        def _(t):
            rows = rows_of(t)
            normed, inverse = ln(x_ref[rows, :])
            grad = da[rows, :]
            back = ln_back(grad * vec_ref[0:1, :], normed, inverse)
            in_out[rows, :] = (dh_ref[rows, :] + back).astype(BF16)
            sum_out[0:1, :] += jnp.sum(grad * normed, axis=0, keepdims=True)
            sum_out[1:2, :] += jnp.sum(grad, axis=0, keepdims=True)


def lay_kernel(seq, pad, count, out_ref, in_ref, out_out, in_out, wide):
    for t in range(count):
        wide[pl.ds(t, seq, stride=count), :] = out_ref[t, 0:seq, :].astype(F32)
        in_out[pl.ds(t, seq, stride=count), :] = in_ref[t, 0:seq, :].astype(F32)
    out_out[...] = wide[...].astype(BF16)


def update_kernel(*refs):
    grad_ref, small_ref = refs[:2]
    state, outs = refs[2:23], refs[23:]
    correction = 1.0 - 0.5**STEP
    rates = ((D // 2) ** -0.5, (D // 16) ** -0.5, D**-0.5, FF**-0.5, 0.1, 0.1, 0.15)

    def update(i, at, gradient):
        master, first, second = (state[i + 7 * j][at] for j in range(3))
        decay = DECAY if i < 4 else 0.0
        values = adamw_update(master, first, second, gradient, rates[i], decay, correction)
        for j, value in enumerate((gradient,) + values + (values[0].astype(BF16),)):
            outs[i + 7 * j][at] = value

    every = (slice(None), slice(None))
    for j in range(3):
        update(0, (j,) + every, grad_ref[0, :, 192 * j : 192 * j + 192])
    update(1, every, grad_ref[0, :, 576:768].T)
    update(2, every, grad_ref[1])
    update(3, every, grad_ref[2])
    for r in range(3):
        update(4, (r,) + every, small_ref[6:8, 8 * r : 8 * r + 8])
    update(5, every, small_ref[8:16, 0:12])
    update(6, every, small_ref[0:6, 0:96])


ALL = slice(None)


class Place:
    def __init__(self):
        dp, mp = lax.axis_index("dp"), lax.axis_index("mp")
        self.z, self.y = dp // 2, dp % 2
        self.x, self.c = mp // 2, mp % 2
        self.zs = [(self.z + k) % 4 for k in (1, 2, 3)]
        self.oy, self.ox, self.oc = 1 - self.y, 1 - self.x, 1 - self.c
        self.to_z = [self.id(z=z) for z in self.zs]
        self.to_y, self.to_x, self.to_c = self.id(y=self.oy), self.id(x=self.ox), self.id(c=self.oc)

    def id(self, z=None, y=None, x=None, c=None):
        z, y, x, c = (own if new is None else new for own, new in ((self.z, z), (self.y, y), (self.x, x), (self.c, c)))
        return (2 * z + y, 2 * x + c)

    def greet(self):
        barrier = pltpu.get_barrier_semaphore()
        for device in (*self.to_z, self.to_y, self.to_x, self.to_c):
            pl.semaphore_signal(barrier, inc=1, device_id=device, device_id_type=MESH)
        pl.semaphore_wait(barrier, 6)


class Sends:
    def __init__(self, send, recv):
        self.send, self.recv, self.all = send, recv, []

    def copy(self, src, dst, device):
        i = len(self.all)
        self.all.append(
            pltpu.make_async_remote_copy(
                src_ref=src,
                dst_ref=dst,
                send_sem=self.send.at[i],
                recv_sem=self.recv.at[i],
                device_id=device,
                device_id_type=MESH,
            )
        )
        return self.all[-1]

    def start(self, src, dst, device):
        copy = self.copy(src, dst, device)
        copy.start()
        return copy

    def finish(self):
        for copy in self.all:
            copy.wait_send()


def start(copies):
    for copy in copies:
        copy.start()


def arrived(copies):
    for copy in copies:
        copy.wait_recv()


class Gather:
    def __init__(self, p, s, full, split, cols=ALL, own=None, column=None):
        every = full.shape[4]
        at = lambda x, c, z, y, rows: full.at[x, c, z, y, rows, cols]
        col = lambda rows: at(p.x, p.c, ALL, p.y, rows) if column is None else column.at[:, rows, cols]
        both = lambda view, device: s.copy(view, view, device)
        high, low = pl.ds(0, split), pl.ds(split, every - split)
        here = at(p.x, p.c, p.z, p.y, ALL)
        self.z = [s.copy(own, here, device) for device in p.to_z] if column is None else []
        self.two = [s.copy(col(high), at(p.x, p.c, ALL, p.y, high), p.to_y)]
        self.three = [both(at(p.x, p.c, ALL, ALL, high), p.to_x)]
        self.core_two = [s.copy(col(ALL), at(p.x, p.c, ALL, p.y, ALL), p.to_c)]
        self.core_three = [both(at(p.x, p.c, ALL, p.oy, high), p.to_c)]
        self.core_last = [both(at(p.ox, p.c, ALL, ALL, high), p.to_c)]
        if split < every:
            self.two.append(s.copy(col(low), at(p.x, p.c, ALL, p.y, low), p.to_x))
            self.three += [both(at(x, p.c, ALL, p.y, low), p.to_y) for x in (0, 1)]
            self.core_three.append(both(at(p.ox, p.c, ALL, p.y, low), p.to_c))
            self.core_last += [both(at(x, p.c, ALL, p.oy, low), p.to_c) for x in (0, 1)]

    def along_z(self):
        start(self.z)

    def second(self):
        arrived(self.z)
        start(self.two)
        start(self.core_two)

    def third(self):
        arrived(self.two)
        start(self.three)
        start(self.core_three)

    def last(self):
        arrived(self.three)
        start(self.core_last)

    def done(self):
        arrived(self.core_two + self.core_three + self.core_last)

    COPIES = 14
    COPIES_WHOLE = 8


def gather_kernel(w_ref, s_ref, f1, col2, fs, send, recv, local):
    p = Place()
    p.greet()
    s = Sends(send, recv)
    half = pl.ds(0, 384), pl.ds(384, 384)
    gathers = [
        Gather(p, s, fs, 16, own=s_ref),
        *(Gather(p, s, f1, 48, cols, own=w_ref.at[0, :, cols]) for cols in half),
    ]
    for g in gathers:
        g.along_z()
    ahead = [s.copy(w_ref.at[1], col2.at[p.z], device) for device in p.to_z]
    start(ahead)
    mine = [
        pltpu.make_async_copy(s_ref, fs.at[p.x, p.c, p.z, p.y], local.at[0]),
        pltpu.make_async_copy(w_ref.at[0], f1.at[p.x, p.c, p.z, p.y], local.at[1]),
        pltpu.make_async_copy(w_ref.at[1], col2.at[p.z], local.at[2]),
    ]
    start(mine)
    for copy in mine:
        copy.wait()
    stages = [("second", 0), ("second", 1), ("third", 0), ("last", 0), ("second", 2), ("third", 1), ("third", 2),
              ("last", 1), ("last", 2)]
    for name, i in stages:
        getattr(gathers[i], name)()
    for g in gathers:
        g.done()
    arrived(ahead)
    s.finish()


def add_into(target, other, lead):
    total = math.prod(lead)

    @pl.loop(0, total)
    def _(i):
        index = []
        for size in reversed(lead):
            index.append(i % size)
            i = i // size
        index = tuple(reversed(index))
        target[index] = (target[index].astype(F32) + other(*index).astype(F32)).astype(BF16)


class Reduce:
    def __init__(self, place, sends, parts, r0, r1a, r1b, r2a, r2b, r3a, r3b, split):
        self.p, self.s, self.parts, self.split = place, sends, parts, split
        self.r0, self.r1a, self.r1b, self.r2a, self.r2b, self.r3a, self.r3b = r0, r1a, r1b, r2a, r2b, r3a, r3b
        self.both = r1b is not None

    def cores(self):
        p = self.p
        self.wait = [self.s.start(self.parts.at[:, 1 - p.c], self.r0, p.id(c=1 - p.c))]

    def first(self):
        p, s, h = self.p, self.s, self.split
        arrived(self.wait)
        add_into(self.r0, lambda x, z, y: self.parts[x, p.c, z, y], self.r0.shape[:3])
        self.wait = [s.start(self.r0.at[1 - p.x, :, :, pl.ds(0, h)], self.r1a, p.id(x=1 - p.x))]
        if self.both:
            low = pl.ds(h, self.r0.shape[3] - h)
            self.wait.append(s.start(self.r0.at[:, :, 1 - p.y, low], self.r1b, p.id(y=1 - p.y)))

    def second(self):
        p, s, h = self.p, self.s, self.split
        arrived(self.wait)
        add_into(self.r1a, lambda z, y: self.r0[p.x, z, y, 0:h], self.r1a.shape[:2])
        self.wait = [s.start(self.r1a.at[:, 1 - p.y], self.r2a, p.id(y=1 - p.y))]
        if self.both:
            add_into(self.r1b, lambda x, z: self.r0[x, z, p.y, h:], self.r1b.shape[:2])
            self.wait.append(s.start(self.r1b.at[1 - p.x], self.r2b, p.id(x=1 - p.x)))

    def third(self):
        p, s = self.p, self.s
        arrived(self.wait)
        add_into(self.r2a, lambda z: self.r1a[z, p.y], self.r2a.shape[:1])
        if self.both:
            add_into(self.r2b, lambda z: self.r1b[p.x, z], self.r2b.shape[:1])
        self.wait = []
        for k in (1, 2, 3):
            to = (p.z + k) % 4
            self.wait.append(s.start(self.r2a.at[to], self.r3a.at[k - 1], p.id(z=to)))
            if self.both:
                self.wait.append(s.start(self.r2b.at[to], self.r3b.at[k - 1], p.id(z=to)))

    def last(self, out):
        p = self.p
        arrived(self.wait)
        sum_of = lambda r2, r3: r2[p.z].astype(F32) + r3[0].astype(F32) + r3[1].astype(F32) + r3[2].astype(F32)
        out[0 : self.split] = sum_of(self.r2a, self.r3a)
        if self.both:
            out[self.split :] = sum_of(self.r2b, self.r3b)

    @staticmethod
    def scratch(rows, columns, split):
        shapes = [(2, 4, 2, rows), (4, 2, split), (2, 4, rows - split), (4, split), (4, rows - split), (3, split), (3, rows - split)]
        return [pltpu.VMEM(shape + (columns,), BF16) for shape in shapes if shape[-1] > 0]


def reduce_kernel(g1, g2, g3, gs, own_out, own_in, total, small, all_out, all_in, *scratch):
    *buffers, send, recv, local = scratch
    p = Place()
    p.greet()
    s = Sends(send, recv)
    reduces = [Reduce(p, s, part, *buffers[7 * i : 7 * i + 7], 48) for i, part in enumerate((g3, g2, g1))]
    b = buffers[21:]
    reduces.append(Reduce(p, s, gs, b[0], b[1], None, b[2], None, b[3], None, 16))
    outs = [total.at[2], total.at[1], total.at[0], small]
    for r in reduces:
        r.cores()
    trades, copies = [], []
    for i, (own, full) in enumerate(((own_out, all_out), (own_in, all_in))):
        slot = full.at[p.x, p.c]
        copies.append(pltpu.make_async_copy(own, slot, local.at[i]))
        copies[-1].start()
    for i in range(4):
        reduces[i].first()
        if i > 0:
            reduces[i - 1].second()
        if i > 1:
            reduces[i - 2].third()
    for own, full in ((own_out, all_out), (own_in, all_in)):
        slot = full.at[p.x, p.c]
        trades.append([s.start(own, slot, p.id(x=1 - p.x)), s.start(own, slot, p.id(c=1 - p.c))])
    reduces[3].second()
    reduces[2].third()
    reduces[3].third()
    for r, out in zip(reduces, outs):
        r.last(out)
    for trade, full in zip(trades, (all_out, all_in)):
        arrived(trade[:1])
        slot = full.at[1 - p.x, p.c]
        trade.append(s.start(slot, slot, p.id(c=1 - p.c)))
    for trade in trades:
        arrived(trade[1:])
    for copy in copies:
        copy.wait()
    s.finish()


def fast_shards(*args):
    (tokens, cotangent, visible, tile_counts, *state) = args
    tile_count, seq, width = tokens.shape
    mp_size = lax.axis_size("mp")
    tiles = tile_count // mp_size
    pad = -(-seq // 16) * 16
    rows = tiles * pad
    native = lambda i, a: a.transpose(1, 0, 2) if i in (0, 4) else a.T if i in (3, 5) else a
    state = [native(i % 7, a) for i, a in enumerate(state)]
    params = lambda limit=None, **kw: pltpu.CompilerParams(vmem_limit_bytes=60 << 20, **kw)
    shape = jax.ShapeDtypeStruct
    me = lax.axis_index("mp").astype(jnp.int32)
    who = jnp.stack([me, tile_counts[0]])

    own, own_small = pl.pallas_call(
        pack_kernel,
        out_shape=(shape((3, 96, D), BF16), shape((16, 128), BF16)),
        scratch_shapes=[pltpu.VMEM((16, 128), F32)],
        compiler_params=params(),
        name="pack",
    )(*state[:7])

    full = shape((2, 2, 4, 2, 96, D), BF16)
    dma = lambda count: pltpu.SemaphoreType.DMA((count,))
    copies = 2 * Gather.COPIES + Gather.COPIES_WHOLE + 3
    f1, col2, fs = pl.pallas_call(
        gather_kernel,
        out_shape=(full, shape((4, 96, D), BF16), shape((2, 2, 4, 2, 16, 128), BF16)),
        in_specs=[pl.BlockSpec(memory_space=pltpu.VMEM)] * 2,
        out_specs=(pl.BlockSpec(memory_space=ANY),) * 3,
        scratch_shapes=[dma(copies), dma(copies), dma(3)],
        compiler_params=params(collective_id=0, has_side_effects=True),
        name="gather",
    )(own, own_small)
    w1 = f1.reshape(4, D, D)

    vec, off = pl.pallas_call(
        spread_kernel,
        out_shape=(shape((16, D), F32), shape((4, 8, D), F32)),
        compiler_params=params(),
        name="spread",
    )(fs.reshape(4, 8, 16, 128))

    by_place = lambda a: a.transpose(1, 0, 2)
    half = pl.BlockSpec((seq, 8, D), lambda m, who: (0, who[0] // 2, 0))
    of_group = lambda *shape: pl.BlockSpec((1,) + shape, lambda m, who: (m,) + (0,) * len(shape))
    all_of = lambda *shape: pl.BlockSpec(shape, lambda m, who: (0,) * len(shape))
    places = lax.dynamic_slice(visible, (me * tiles, 0), (tiles, seq)).T
    table = jnp.asarray(position_rows())

    x, dy = pl.pallas_call(
        functools.partial(prep_kernel, seq, pad, tiles),
        out_shape=(shape((rows, D), F32), shape((rows, D), BF16)),
        grid_spec=pltpu.PrefetchScalarGridSpec(
            num_scalar_prefetch=1,
            grid=(1,),
            in_specs=[half, half, all_of(seq, tiles), all_of(3, 128, D)],
            out_specs=(all_of(rows, D),) * 2,
            scratch_shapes=[pltpu.VMEM((D // 128, seq * 8, 128), F32), pltpu.VMEM((rows, D), F32)],
        ),
        compiler_params=params(),
        name="prep",
    )(who, by_place(tokens), by_place(cotangent), places, table)

    of_group1 = lambda *shape: pl.BlockSpec((1,) + shape, lambda m: (m,) + (0,) * len(shape))
    all_of1 = lambda *shape: pl.BlockSpec(shape, lambda m: (0,) * len(shape))
    copies = Gather.COPIES * 2 - 3
    h, qkv, probs, o, f2, f3 = pl.pallas_call(
        functools.partial(attend_kernel, seq, pad, tiles),
        out_shape=(
            shape((rows, D), F32),
            shape((4, rows, 576), BF16),
            shape((4, 3, rows, pad), BF16),
            shape((4, rows, 192), BF16),
            full,
            full,
        ),
        grid=(4,),
        in_specs=[all_of1(rows, D), all_of1(16, D), of_group1(8, D), of_group1(D, D), all_of1(4, 96, D), all_of1(96, D)],
        out_specs=(all_of1(rows, D), of_group1(rows, 576), of_group1(3, rows, pad), of_group1(rows, 192))
        + (pl.BlockSpec(memory_space=ANY),) * 2,
        scratch_shapes=[pltpu.VMEM((rows, D), BF16), dma(copies), dma(copies), dma(2)],
        compiler_params=params(collective_id=2, has_side_effects=True),
        name="attend",
    )(x, vec, off, w1, col2, own[2])
    w2, w3 = (f.reshape(4, D, D) for f in (f2, f3))

    out_own, dh, sum_two, sum_hid, g2, g3 = pl.pallas_call(
        functools.partial(feed_kernel, seq, pad, tiles),
        out_shape=(
            shape((rows, D), BF16),
            shape((rows, D), F32),
            shape((8, D), F32),
            shape((4, 8, D), F32),
            shape((4, D, D), BF16),
            shape((4, D, D), BF16),
        ),
        grid_spec=pltpu.PrefetchScalarGridSpec(
            num_scalar_prefetch=1,
            grid=(4,),
            in_specs=[all_of(rows, D), all_of(rows, D), all_of(16, D), of_group(8, D), of_group(D, D), of_group(D, D)],
            out_specs=(all_of(rows, D), all_of(rows, D), all_of(8, D), of_group(8, D), of_group(D, D), of_group(D, D)),
            scratch_shapes=[
                pltpu.VMEM((rows, D), BF16),
                pltpu.VMEM((D, rows), BF16),
                pltpu.VMEM((D, rows), BF16),
                pltpu.VMEM((rows, D), F32),
                pltpu.VMEM((rows, D), F32),
            ],
        ),
        compiler_params=params(),
        name="feed",
    )(who, dy, h, vec, off, w2, w3)

    in_own, sum_one, sum_head, g1 = pl.pallas_call(
        functools.partial(back_kernel, seq, pad, tiles),
        out_shape=(
            shape((rows, D), BF16),
            shape((8, D), F32),
            shape((4, 8, D), F32),
            shape((4, D, D), BF16),
        ),
        grid=(4,),
        in_specs=[all_of1(rows, D), all_of1(rows, D), all_of1(16, D), of_group1(D, D), of_group1(rows, 576),
                  of_group1(3, rows, pad), of_group1(rows, 192)],
        out_specs=(all_of1(rows, D), all_of1(8, D), of_group1(8, D), of_group1(D, D)),
        scratch_shapes=[
            pltpu.VMEM((D, rows), BF16),
            pltpu.VMEM((rows, D), BF16),
            pltpu.VMEM((D, rows), BF16),
            pltpu.VMEM((rows, 192), BF16),
            pltpu.VMEM((rows, 576), BF16),
            pltpu.VMEM((rows, D), F32),
        ],
        compiler_params=params(),
        name="back",
    )(x, dh, vec, w1, qkv, probs, o)

    gs = pl.pallas_call(
        squeeze_kernel,
        out_shape=shape((4, 8, 16, 128), BF16),
        scratch_shapes=[pltpu.VMEM((8, D), F32)],
        compiler_params=params(),
        name="squeeze",
    )(sum_two, sum_one, sum_hid, sum_head)

    copies = 3 * 11 + 6 + 6
    everyone = shape((2, 2, rows, D), BF16)
    total, small, all_out, all_in = pl.pallas_call(
        reduce_kernel,
        out_shape=(shape((3, 96, D), F32), shape((16, 128), F32), everyone, everyone),
        in_specs=[pl.BlockSpec(memory_space=pltpu.VMEM)] * 4 + [pl.BlockSpec(memory_space=ANY)] * 2,
        out_specs=(pl.BlockSpec(memory_space=pltpu.VMEM),) * 2 + (pl.BlockSpec(memory_space=ANY),) * 2,
        scratch_shapes=[
            *(3 * Reduce.scratch(96, D, 48)),
            *Reduce.scratch(16, 128, 16),
            pltpu.SemaphoreType.DMA((copies,)),
            pltpu.SemaphoreType.DMA((copies,)),
            pltpu.SemaphoreType.DMA((2,)),
        ],
        compiler_params=params(collective_id=1, has_side_effects=True),
        name="reduce",
    )(*(g.reshape(2, 2, 4, 2, 96, D) for g in (g1, g2, g3)), gs.reshape(2, 2, 4, 2, 16, 128), out_own, in_own)

    flat = seq * tile_count
    block = pl.BlockSpec((tile_count, pad, 128), lambda n: (0, 0, n))
    output, input_grad = pl.pallas_call(
        functools.partial(lay_kernel, seq, pad, tile_count),
        out_shape=(shape((flat, D), BF16), shape((flat, D), F32)),
        grid=(D // 128,),
        in_specs=[block, block],
        out_specs=(pl.BlockSpec((flat, 128), lambda n: (0, n)),) * 2,
        scratch_shapes=[pltpu.VMEM((flat, 128), F32)],
        compiler_params=params(),
        name="lay",
    )(*(a.reshape(tile_count, pad, D) for a in (all_out, all_in)))
    output, input_grad = (a.reshape(seq, tile_count, D).transpose(1, 0, 2) for a in (output, input_grad))

    kinds = [shape(a.shape, F32) for a in state[:7]]
    results = pl.pallas_call(
        update_kernel,
        out_shape=tuple(kinds * 4 + [shape(a.shape, BF16) for a in kinds]),
        compiler_params=params(),
        name="update",
    )(total, small, *state)
    return (output, input_grad) + tuple(native(i % 7, a) for i, a in enumerate(results))


def solution(mesh):
    in_specs = (
        P("dp", None, None),
        P("dp", None, None),
        P("dp", None),
        P("dp"),
        P("dp", None, "mp"),
        P("mp", "dp"),
        P("dp", "mp"),
        P("mp", "dp"),
        P(None, "mp", "dp"),
        P("mp", "dp"),
        P(None, "dp"),
        P("dp", None, "mp"),
        P("mp", "dp"),
        P("dp", "mp"),
        P("mp", "dp"),
        P(None, "mp", "dp"),
        P("mp", "dp"),
        P(None, "dp"),
        P("dp", None, "mp"),
        P("mp", "dp"),
        P("dp", "mp"),
        P("mp", "dp"),
        P(None, "mp", "dp"),
        P("mp", "dp"),
        P(None, "dp"),
    )
    out_specs = (
        P("dp", None, None),
        P("dp", None, None),
        P("dp", None, "mp"),
        P("mp", "dp"),
        P("dp", "mp"),
        P("mp", "dp"),
        P(None, "mp", "dp"),
        P("mp", "dp"),
        P(None, "dp"),
        P("dp", None, "mp"),
        P("mp", "dp"),
        P("dp", "mp"),
        P("mp", "dp"),
        P(None, "mp", "dp"),
        P("mp", "dp"),
        P(None, "dp"),
        P("dp", None, "mp"),
        P("mp", "dp"),
        P("dp", "mp"),
        P("mp", "dp"),
        P(None, "mp", "dp"),
        P("mp", "dp"),
        P(None, "dp"),
        P("dp", None, "mp"),
        P("mp", "dp"),
        P("dp", "mp"),
        P("mp", "dp"),
        P(None, "mp", "dp"),
        P("mp", "dp"),
        P(None, "dp"),
        P("dp", None, "mp"),
        P("mp", "dp"),
        P("dp", "mp"),
        P("mp", "dp"),
        P(None, "mp", "dp"),
        P("mp", "dp"),
        P(None, "dp"),
    )
    sizes = (mesh.shape["dp"], mesh.shape["mp"])
    body = fast_shards if sizes == (8, 4) else shards
    return jax.shard_map(body, mesh=mesh, in_specs=in_specs, out_specs=out_specs, check_vma=False)
```

```python
import functools
import math

import jax
import jax.numpy as jnp
import numpy as np
from jax import lax
from jax.experimental import pallas as pl
from jax.experimental.pallas import tpu as pltpu
from jax.sharding import PartitionSpec as P

D = 768
FF = 3072
GRID = 14
STEP = 3


LN_EPS = 1e-06
BETA_ONE = 0.5
BETA_TWO = 0.5
ADAM_EPS = 1e-08
DECAY = 0.05


def cut_along(x, dim, size):
    dims = x.shape
    parts = x.reshape(*dims[:dim], size, dims[dim] // size, *dims[dim + 1 :])
    return jnp.moveaxis(parts, dim, 0)


def summed_on_arrival(x, axis, dim):
    size = lax.axis_size(axis)
    parts = lax.all_to_all(cut_along(x, dim, size), axis, 0, 0, tiled=True)
    return jnp.sum(parts.astype(jnp.float32), axis=0)


def sine_table(places, feature_width):
    half_width = feature_width // 2
    spread = jnp.arange(half_width, dtype=jnp.float32) / half_width
    frequency = jnp.exp(-math.log(10000.0) * spread)
    angles = places[..., None] * frequency
    return jnp.concatenate([jnp.sin(angles), jnp.cos(angles)], axis=-1)


def position_table(visible, feature_width):
    plane_size = GRID * GRID
    frame_place = (visible // plane_size).astype(jnp.float32)
    within = visible % plane_size
    row_place = (within // GRID).astype(jnp.float32)
    column_place = (within % GRID).astype(jnp.float32)
    time_width = feature_width // 16 * 4
    space_width = feature_width // 16 * 6
    return jnp.concatenate(
        [
            sine_table(frame_place, time_width),
            sine_table(row_place, space_width),
            sine_table(column_place, space_width),
        ],
        axis=-1,
    )


def normalize(values):
    center = values - jnp.mean(values, axis=-1, keepdims=True)
    inverse = lax.rsqrt(jnp.mean(center * center, axis=-1, keepdims=True) + LN_EPS)
    return (center * inverse, inverse)


def norm_back(grad_normed, normed, inverse):
    return inverse * (
        grad_normed
        - jnp.mean(grad_normed, axis=-1, keepdims=True)
        - normed * jnp.mean(grad_normed * normed, axis=-1, keepdims=True)
    )


def over_rows(former, latter):
    return lax.dot_general(
        former, latter, (((0,), (0,)), ((), ())), preferred_element_type=jnp.float32
    )


def over_cols(former, latter):
    return lax.dot_general(
        former, latter, (((1,), (1,)), ((), ())), preferred_element_type=jnp.float32
    )


def exact_gelu(values):
    return jax.nn.gelu(values, approximate=False)


def adamw_update(
    master, first_moment, second_moment, gradient, step_rate, weight_decay, correction
):
    first_new = BETA_ONE * first_moment + (1.0 - BETA_ONE) * gradient
    second_new = BETA_TWO * second_moment + (1.0 - BETA_TWO) * gradient * gradient
    ratio = first_new / correction / (jnp.sqrt(second_new / correction) + ADAM_EPS)
    master_new = master - step_rate * (ratio + weight_decay * master)
    return (master_new, first_new, second_new)


def shards(
    tokens,
    cotangent,
    visible,
    tile_counts,
    attend_weight,
    project_weight,
    widen_weight,
    narrow_weight,
    heads_offset,
    hidden_offset,
    layer_vectors,
    attend_first,
    project_first,
    widen_first,
    narrow_first,
    heads_first,
    hidden_first,
    vectors_first,
    attend_second,
    project_second,
    widen_second,
    narrow_second,
    heads_second,
    hidden_second,
    vectors_second,
):
    fore_attend, fore_project, fore_widen, fore_narrow, fore_heads, fore_hidden, fore_vectors = (
        lax.all_gather(attend_weight.astype(jnp.bfloat16), "dp", axis=0, tiled=True),
        lax.all_gather(project_weight.astype(jnp.bfloat16), "dp", axis=1, tiled=True),
        lax.all_gather(widen_weight.astype(jnp.bfloat16), "dp", axis=0, tiled=True),
        lax.all_gather(narrow_weight.astype(jnp.bfloat16), "dp", axis=1, tiled=True),
        lax.all_gather(heads_offset.astype(jnp.bfloat16), "dp", axis=2, tiled=True),
        lax.all_gather(hidden_offset.astype(jnp.bfloat16), "dp", axis=1, tiled=True),
        lax.all_gather(layer_vectors.astype(jnp.bfloat16), "dp", axis=1, tiled=True),
    )
    tile_count, seq_length, model_width = tokens.shape
    row_count = tile_count * seq_length
    local_width = fore_attend.shape[2]
    heads_local = fore_heads.shape[1]
    head_size = fore_heads.shape[2]
    score_scale = 1.0 / math.sqrt(head_size)
    live_tiles = (jnp.arange(tile_count, dtype=jnp.int32) < tile_counts[0]).astype(jnp.float32)
    live_rows = jnp.broadcast_to(live_tiles[:, None], (tile_count, seq_length)).reshape(
        row_count, 1
    )
    vectors = fore_vectors.astype(jnp.float32)
    summed = (tokens.astype(jnp.float32) + position_table(visible, model_width)).reshape(
        row_count, model_width
    )
    normed_one, inverse_one = normalize(summed)
    attend_low = (normed_one * vectors[0] + vectors[1]).astype(jnp.bfloat16)
    linear = jnp.dot(
        attend_low,
        fore_attend.reshape(model_width, 3 * local_width),
        preferred_element_type=jnp.float32,
    ).reshape(row_count, 3, local_width)
    offsets = fore_heads.astype(jnp.float32).reshape(2, local_width)
    head_shape = (tile_count, seq_length, heads_local, head_size)
    query_low = (linear[:, 0] + offsets[0]).astype(jnp.bfloat16).reshape(head_shape)
    key_low = linear[:, 1].astype(jnp.bfloat16).reshape(head_shape)
    value_low = (linear[:, 2] + offsets[1]).astype(jnp.bfloat16).reshape(head_shape)
    scores = (
        jnp.einsum("tqhd,tkhd->thqk", query_low, key_low, preferred_element_type=jnp.float32)
        * score_scale
    )
    row_top = jnp.max(scores, axis=-1, keepdims=True)
    log_total = row_top + jnp.log(jnp.sum(jnp.exp(scores - row_top), axis=-1, keepdims=True))
    weights_low = jnp.exp(scores - log_total).astype(jnp.bfloat16)
    context = jnp.einsum(
        "thqk,tkhd->tqhd", weights_low, value_low, preferred_element_type=jnp.float32
    )
    context_low = context.reshape(row_count, local_width).astype(jnp.bfloat16)
    attention_part = jnp.dot(context_low, fore_project, preferred_element_type=jnp.float32)
    attention = lax.psum(attention_part.astype(jnp.bfloat16), "mp").astype(jnp.float32)
    middle = summed + attention + vectors[4]
    normed_two, inverse_two = normalize(middle)
    widen_low = (normed_two * vectors[2] + vectors[3]).astype(jnp.bfloat16)
    hidden = jnp.dot(
        widen_low, fore_widen, preferred_element_type=jnp.float32
    ) + fore_hidden.astype(jnp.float32).reshape(-1)
    active_low = exact_gelu(hidden).astype(jnp.bfloat16)
    feed_part = jnp.dot(active_low, fore_narrow, preferred_element_type=jnp.float32)
    feed_sum = lax.psum(feed_part.astype(jnp.bfloat16), "mp").astype(jnp.float32)
    result = (middle + feed_sum + vectors[5]) * live_rows
    output_low = result.astype(jnp.bfloat16)
    back_attend, back_project, back_widen, back_narrow, back_vectors = (
        fore_attend,
        fore_project,
        fore_widen,
        fore_narrow,
        fore_vectors,
    )
    vectors_back = back_vectors.astype(jnp.float32)
    grad_out = cotangent.astype(jnp.float32).reshape(row_count, model_width) * live_rows
    grad_out_low = grad_out.astype(jnp.bfloat16)
    grad_narrow = over_rows(active_low, grad_out_low)
    grad_active = over_cols(grad_out_low, back_narrow)
    gelu_back = jax.vjp(exact_gelu, hidden)[1]
    grad_hidden_low = gelu_back(grad_active)[0].astype(jnp.bfloat16)
    grad_widen = over_rows(widen_low, grad_hidden_low)
    grad_hidden = jnp.sum(grad_hidden_low.astype(jnp.float32), axis=0).reshape(fore_hidden.shape)
    normed_two_part = over_cols(grad_hidden_low, back_widen)
    grad_normed_two = lax.psum(normed_two_part.astype(jnp.bfloat16), "mp").astype(jnp.float32)
    grad_middle = grad_out + norm_back(grad_normed_two * vectors_back[2], normed_two, inverse_two)
    grad_middle_low = grad_middle.astype(jnp.bfloat16)
    grad_project = over_rows(context_low, grad_middle_low)
    grad_context_low = (
        over_cols(grad_middle_low, back_project).astype(jnp.bfloat16).reshape(head_shape)
    )
    scores_again = (
        jnp.einsum("tqhd,tkhd->thqk", query_low, key_low, preferred_element_type=jnp.float32)
        * score_scale
    )
    weights_full = jnp.exp(scores_again - log_total)
    weights_again_low = weights_full.astype(jnp.bfloat16)
    grad_weights = jnp.einsum(
        "tqhd,tkhd->thqk", grad_context_low, value_low, preferred_element_type=jnp.float32
    )
    grad_value = jnp.einsum(
        "thqk,tqhd->tkhd", weights_again_low, grad_context_low, preferred_element_type=jnp.float32
    )
    row_dot = jnp.sum(grad_weights * weights_full, axis=-1, keepdims=True)
    grad_scores_low = (weights_full * (grad_weights - row_dot)).astype(jnp.bfloat16)
    grad_query = (
        jnp.einsum("thqk,tkhd->tqhd", grad_scores_low, key_low, preferred_element_type=jnp.float32)
        * score_scale
    )
    grad_key = (
        jnp.einsum(
            "thqk,tqhd->tkhd", grad_scores_low, query_low, preferred_element_type=jnp.float32
        )
        * score_scale
    )
    grad_qkv_low = jnp.stack(
        [
            grad_query.reshape(row_count, local_width),
            grad_key.reshape(row_count, local_width),
            grad_value.reshape(row_count, local_width),
        ],
        axis=1,
    ).astype(jnp.bfloat16)
    grad_offsets = jnp.sum(grad_qkv_low.astype(jnp.float32), axis=0)
    grad_heads = jnp.stack([grad_offsets[0], grad_offsets[2]]).reshape(2, heads_local, head_size)
    flat_qkv = grad_qkv_low.reshape(row_count, 3 * local_width)
    grad_attend = over_rows(attend_low, flat_qkv).reshape(model_width, 3, local_width)
    normed_one_part = over_cols(flat_qkv, back_attend.reshape(model_width, 3 * local_width))
    grad_normed_one = lax.psum(normed_one_part.astype(jnp.bfloat16), "mp").astype(jnp.float32)
    grad_inputs = grad_middle + norm_back(
        grad_normed_one * vectors_back[0], normed_one, inverse_one
    )
    grad_vectors = jnp.stack(
        [
            jnp.sum(grad_normed_one * normed_one, axis=0),
            jnp.sum(grad_normed_one, axis=0),
            jnp.sum(grad_normed_two * normed_two, axis=0),
            jnp.sum(grad_normed_two, axis=0),
            jnp.sum(grad_middle, axis=0),
            jnp.sum(grad_out, axis=0),
        ]
    )
    output = output_low.reshape(tile_count, seq_length, model_width)
    input_grad = grad_inputs.reshape(tile_count, seq_length, model_width)
    (
        shard_attend,
        shard_project,
        shard_widen,
        shard_narrow,
        shard_heads,
        shard_hidden,
        shard_vectors,
    ) = (
        summed_on_arrival(grad_attend.astype(jnp.bfloat16), "dp", 0),
        summed_on_arrival(grad_project.astype(jnp.bfloat16), "dp", 1),
        summed_on_arrival(grad_widen.astype(jnp.bfloat16), "dp", 0),
        summed_on_arrival(grad_narrow.astype(jnp.bfloat16), "dp", 1),
        summed_on_arrival(grad_heads.astype(jnp.bfloat16), "dp", 2),
        summed_on_arrival(grad_hidden.astype(jnp.bfloat16), "dp", 1),
        summed_on_arrival(grad_vectors.astype(jnp.bfloat16), "dp", 1),
    )
    correction = 1.0 - 0.5**STEP
    new_attend, first_attend, second_attend = adamw_update(
        attend_weight,
        attend_first,
        attend_second,
        shard_attend,
        (D // 2) ** (-0.5),
        DECAY,
        correction,
    )
    new_project, first_project, second_project = adamw_update(
        project_weight,
        project_first,
        project_second,
        shard_project,
        (D // 16) ** (-0.5),
        DECAY,
        correction,
    )
    new_widen, first_widen, second_widen = adamw_update(
        widen_weight, widen_first, widen_second, shard_widen, D ** (-0.5), DECAY, correction
    )
    new_narrow, first_narrow, second_narrow = adamw_update(
        narrow_weight, narrow_first, narrow_second, shard_narrow, FF ** (-0.5), DECAY, correction
    )
    new_heads, first_heads, second_heads = adamw_update(
        heads_offset, heads_first, heads_second, shard_heads, 0.1, 0.0, correction
    )
    new_hidden, first_hidden, second_hidden = adamw_update(
        hidden_offset, hidden_first, hidden_second, shard_hidden, 0.1, 0.0, correction
    )
    new_vectors, first_vectors, second_vectors = adamw_update(
        layer_vectors, vectors_first, vectors_second, shard_vectors, 0.15, 0.0, correction
    )
    return (
        output,
        input_grad,
        shard_attend,
        shard_project,
        shard_widen,
        shard_narrow,
        shard_heads,
        shard_hidden,
        shard_vectors,
        new_attend,
        new_project,
        new_widen,
        new_narrow,
        new_heads,
        new_hidden,
        new_vectors,
        first_attend,
        first_project,
        first_widen,
        first_narrow,
        first_heads,
        first_hidden,
        first_vectors,
        second_attend,
        second_project,
        second_widen,
        second_narrow,
        second_heads,
        second_hidden,
        second_vectors,
        new_attend.astype(jnp.bfloat16),
        new_project.astype(jnp.bfloat16),
        new_widen.astype(jnp.bfloat16),
        new_narrow.astype(jnp.bfloat16),
        new_heads.astype(jnp.bfloat16),
        new_hidden.astype(jnp.bfloat16),
        new_vectors.astype(jnp.bfloat16),
    )


F32 = jnp.float32
BF16 = jnp.bfloat16
MESH = pl.DeviceIdType.MESH
ANY = pl.ANY


def nn(former, latter):
    return lax.dot_general(former, latter, (((1,), (0,)), ((), ())), preferred_element_type=F32)


def nt(former, latter):
    return lax.dot_general(former, latter, (((1,), (1,)), ((), ())), preferred_element_type=F32)


def tn(former, latter):
    return lax.dot_general(former, latter, (((0,), (0,)), ((), ())), preferred_element_type=F32)


def iota(shape, dim):
    return lax.broadcasted_iota(jnp.int32, shape, dim)


def whole(ref_shape):
    rank = len(ref_shape)
    return pl.BlockSpec(ref_shape, lambda *_: (0,) * rank)


def pick_vector(d):
    shape = (128, D)
    lane, column = iota(shape, 0), iota(shape, 1)
    return ((column - lane == 96 * d) & (lane < 96)).astype(F32).astype(BF16)


def pick_head(d):
    shape = (128, D)
    lane, column = iota(shape, 0), iota(shape, 1)
    same = (lax.shift_right_logical(column, 6) == lax.shift_right_logical(lane, 3)) & ((column & 7) == (lane & 7))
    return (same & ((lax.shift_right_logical(column, 3) & 7) == d) & (lane < 24)).astype(F32).astype(BF16)


def pick_row():
    shape = (128, D)
    return (lax.shift_right_logical(iota(shape, 1), 6) == iota(shape, 0)).astype(F32).astype(BF16)


def hidden_places(d):
    shape = (8, D)
    column = iota(shape, 1)
    return ((column & 7) == iota(shape, 0)) & ((lax.shift_right_logical(column, 3) & 7) == d)


def pack_kernel(attend, project, widen, narrow, heads, hidden, vectors, w_out, s_out, scratch):
    w_out[0] = jnp.concatenate([attend[0], attend[1], attend[2], project[...].T], axis=1).astype(BF16)
    w_out[1] = widen[...].astype(BF16)
    w_out[2] = narrow[...].astype(BF16)
    scratch[...] = jnp.zeros_like(scratch)
    scratch[0:6, 0:96] = vectors[...]
    for r in range(3):
        scratch[6:8, 8 * r : 8 * r + 8] = heads[r]
    scratch[8:16, 0:12] = hidden[...]
    s_out[...] = scratch[...].astype(BF16)


def spread_small(s_ref, vec_out, off_out):
    row_pick = pick_row()
    vec = jnp.zeros((16, D), F32)
    heads = [jnp.zeros((16, D), F32) for _ in range(4)]
    hidden = [jnp.zeros((1, D), F32) for _ in range(4)]
    for d in range(8):
        vec += nn(s_ref[0, 0, d // 2, d % 2], pick_vector(d))
        head_pick, places = pick_head(d), hidden_places(d)
        for m in range(4):
            block = s_ref[m // 2, m % 2, d // 2, d % 2]
            heads[m] += nn(block, head_pick)
            spread = nn(block, row_pick)[8:16]
            hidden[m] += jnp.sum(jnp.where(places, spread, 0.0), axis=0, keepdims=True)
    vec_out[...] = vec
    for m in range(4):
        off_out[m, 0:2, :] = heads[m][6:8]
        off_out[m, 2:3, :] = hidden[m]
        off_out[m, 3:8, :] = jnp.zeros((5, D), F32)


def squeeze_small(fore_ref, back_ref, hid_ref, heads_ref, out_ref, rows):
    rows[...] = jnp.zeros_like(rows)
    rows[0:2, :] = back_ref[0:2, :]
    rows[2:6, :] = fore_ref[0:4, :]
    row_pick = pick_row()
    shape = (8, 128)
    for m in range(4):
        rows[6:7, 0:192] = heads_ref[m, 0:1, 0:192]
        rows[7:8, 0:192] = heads_ref[m, 1:2, 0:192]
        block = rows[...].astype(BF16)
        wide = jnp.broadcast_to(hid_ref[m, 0:1, :], (8, D))
        for d in range(8):
            upper = jnp.where(iota(shape, 0) < 6, nt(block, pick_vector(d)), nt(block, pick_head(d)))
            lower = nt(jnp.where(hidden_places(d), wide, 0.0).astype(BF16), row_pick)
            out_ref[m // 2, m % 2, d // 2, d % 2] = jnp.concatenate([upper, lower], axis=0).astype(BF16)


def ln(values):
    center = values - jnp.mean(values, axis=-1, keepdims=True)
    inverse = lax.rsqrt(jnp.mean(center * center, axis=-1, keepdims=True) + LN_EPS)
    return center * inverse, inverse


def ln_back(grad, normed, inverse):
    return inverse * (
        grad
        - jnp.mean(grad, axis=-1, keepdims=True)
        - normed * jnp.mean(grad * normed, axis=-1, keepdims=True)
    )


def position_rows():
    plane = np.zeros((128, D), np.float32)
    time_width, space_width = D // 16 * 4, D // 16 * 6

    def sines(count, width):
        half = width // 2
        spread = np.arange(half, dtype=np.float32) / np.float32(half)
        frequency = np.exp(np.float32(-math.log(10000.0)) * spread).astype(np.float32)
        angles = np.arange(count, dtype=np.float32)[:, None] * frequency
        return np.concatenate([np.sin(angles), np.cos(angles)], axis=-1).astype(np.float32)

    plane[0:3, 0:time_width] = sines(3, time_width)
    plane[3 : 3 + GRID, time_width : time_width + space_width] = sines(GRID, space_width)
    plane[3 + GRID : 3 + 2 * GRID, time_width + space_width :] = sines(GRID, space_width)
    parts, rest = [], plane
    for _ in range(3):
        part = rest.astype(jnp.bfloat16)
        parts.append(part)
        rest = rest - part.astype(np.float32)
    return np.stack(parts)


def spread_lanes(ref, wide):
    for g in range(D // 128):
        part = ref[:, :, 128 * g : 128 * g + 128].astype(F32)
        wide[g] = part.reshape(part.shape[0] * 8, 128)


def place_rows(places):
    frame = (places >= GRID * GRID).astype(jnp.int32) + (places >= 2 * GRID * GRID).astype(jnp.int32)
    within = places - frame * (GRID * GRID)
    row = jnp.floor((within.astype(F32) + 0.5) * (1.0 / GRID)).astype(jnp.int32)
    column = within - row * GRID
    lane = iota((places.shape[0], 128), 1)
    hot = (lane == frame) | (lane == 3 + row) | (lane == 3 + GRID + column)
    return hot.astype(F32).astype(BF16)


def lay_tokens(seq, pad, tiles, at, tok_ref, vis_ref, tab_ref, x_out, wide):
    head = seq - seq % 8
    spread_lanes(tok_ref, wide)
    for t in range(tiles):
        hot = place_rows(vis_ref[:, t : t + 1])
        table = nn(hot, tab_ref[0]) + nn(hot, tab_ref[1]) + nn(hot, tab_ref[2])
        x_out[t * pad + head : (t + 1) * pad, :] = jnp.zeros((pad - head, D), F32)
        for g in range(D // 128):
            lanes = slice(128 * g, 128 * g + 128)
            x_out[t * pad : t * pad + seq, lanes] = wide[g, pl.ds(at + t, seq, stride=8), :] + table[:, lanes]


def lay_cotangent(seq, pad, tiles, at, live_ref, cot_ref, dy_out, wide, grad):
    head = seq - seq % 8
    spread_lanes(cot_ref, wide)
    for t in range(tiles):
        live = live_ref[t : t + 1, :]
        grad[t * pad + head : (t + 1) * pad, :] = jnp.zeros((pad - head, D), F32)
        for g in range(D // 128):
            lanes = slice(128 * g, 128 * g + 128)
            grad[t * pad : t * pad + seq, lanes] = wide[g, pl.ds(at + t, seq, stride=8), :] * live
    dy_out[...] = grad[...].astype(BF16)


def attend_kernel(seq, pad, tiles, x_ref, vec_ref, off_ref, w_ref, col2, own3,
                  h_out, qkv_out, p_out, o_out, f2, f3, low, send, recv, local):
    m = pl.program_id(0)
    rows_of = lambda t: pl.ds(pl.multiple_of(t * pad, 16), pad)
    p = Place()
    s = Sends(send, recv)
    g2 = Gather(p, s, f2, 48, column=col2)
    g3 = Gather(p, s, f3, 48, own=own3.at[0])
    mine = [
        pltpu.make_async_copy(col2, f2.at[p.x, p.c, :, p.y], local.at[0]),
        pltpu.make_async_copy(own3.at[0], f3.at[p.x, p.c, p.z, p.y], local.at[1]),
    ]

    @pl.when(m == 0)
    def _():
        p.greet()
        g2.second()
        g3.along_z()
        for copy in mine:
            copy.start()

        @pl.loop(0, tiles)
        def _(t):
            x = x_ref[rows_of(t), :]
            normed, _ = ln(x)
            low[rows_of(t), :] = (normed * vec_ref[0:1, :] + vec_ref[1:2, :]).astype(BF16)
            h_out[rows_of(t), :] = x + vec_ref[4:5, :]

    linear = nn(low[...], w_ref[0, :, 0:576])
    zero = jnp.zeros((1, 192), F32)
    offset = jnp.concatenate([off_ref[0, 0:1, 0:192], zero, off_ref[0, 1:2, 0:192]], axis=1)
    qkv_out[0] = (linear + offset).astype(BF16)

    @pl.loop(0, tiles)
    def _(t):
        rows = rows_of(t)
        qkv = qkv_out[0, rows, :]
        parts = []
        for h in range(3):
            q, k, v = (qkv[:, 192 * j + 64 * h : 192 * j + 64 * h + 64] for j in range(3))
            s = nt(q, k) * 0.125
            s = jnp.where(iota(s.shape, 1) < seq, s, -1e30)
            e = jnp.exp(s - jnp.max(s, axis=-1, keepdims=True))
            low_p = (e * (1.0 / jnp.sum(e, axis=-1, keepdims=True))).astype(BF16)
            p_out[0, h, rows, :] = low_p
            parts.append(nn(low_p, v))
        o_out[0, rows, :] = jnp.concatenate(parts, axis=1).astype(BF16)

    h_out[...] += nt(o_out[0], w_ref[0, :, 576:768])

    @pl.when(m == 0)
    def _():
        for copy in mine:
            copy.wait()
        g2.third()

    @pl.when(m == 1)
    def _():
        g3.second()

    @pl.when(m == 2)
    def _():
        g2.last()

    @pl.when(m == 3)
    def _():
        g3.third()
        g3.last()
        g2.done()
        g3.done()
        s.finish()


def feed_kernel(seq, pad, tiles, live_ref, dy, h_ref, vec_ref, off_ref, w2_ref, w3_ref,
                out_out, dh_out, sum_out, hid_out, g2_out, g3_out, c, c_t, dy_t, y, dc):
    m = pl.program_id(0)
    rows_of = lambda t: pl.ds(pl.multiple_of(t * pad, 16), pad)

    @pl.when(m == 0)
    def _():
        sum_out[...] = jnp.zeros_like(sum_out)

        @pl.loop(0, tiles)
        def _(t):
            sum_out[3:4, :] += jnp.sum(dy[rows_of(t), :].astype(F32), axis=0, keepdims=True)
            normed, _ = ln(h_ref[rows_of(t), :])
            c[rows_of(t), :] = (normed * vec_ref[2:3, :] + vec_ref[3:4, :]).astype(BF16)

        dy_t[...] = dy[...].T
        c_t[...] = c[...].T
        y[...] = jnp.zeros_like(y)
        dc[...] = jnp.zeros_like(dc)

    @pl.loop(0, 3)
    def _(n):
        cols = pl.ds(pl.multiple_of(n * 256, 256), 256)
        u = nn(c[...], w2_ref[0, :, cols]) + off_ref[0, 2:3, cols]
        cdf = 0.5 * (1.0 + lax.erf(u * math.sqrt(0.5)))
        r = (u * cdf).astype(BF16)
        slope = cdf + u * (jnp.exp(-0.5 * u * u) * (1.0 / math.sqrt(2.0 * math.pi)))
        g3_out[0, :, cols] = nn(dy_t[...], r).astype(BF16)
        du = (nn(dy[...], w3_ref[0, :, cols]) * slope).astype(BF16)
        hid_out[0, 0:1, cols] = jnp.sum(du.astype(F32), axis=0, keepdims=True)
        g2_out[0, :, cols] = nn(c_t[...], du).astype(BF16)
        y[...] += nt(r, w3_ref[0, :, cols])
        dc[...] += nt(du, w2_ref[0, :, cols])

    @pl.when(m == pl.num_programs(0) - 1)
    def _():
        @pl.loop(0, tiles)
        def _(t):
            rows = rows_of(t)
            live = live_ref[pl.ds(t, 1), 0:1]
            h = h_ref[rows, :]
            out_out[rows, :] = ((h + y[rows, :] + vec_ref[5:6, :]) * live).astype(BF16)
            normed, inverse = ln(h)
            grad = dc[rows, :]
            dh = dy[rows, :].astype(F32) + ln_back(grad * vec_ref[2:3, :], normed, inverse)
            dh_out[rows, :] = dh
            sum_out[0:1, :] += jnp.sum(grad * normed, axis=0, keepdims=True)
            sum_out[1:2, :] += jnp.sum(grad, axis=0, keepdims=True)
            sum_out[2:3, :] += jnp.sum(dh, axis=0, keepdims=True)


def back_kernel(seq, pad, tiles, x_ref, dh_ref, vec_ref, w_ref, qkv_ref, p_ref, o_ref, g2, g3, own_out,
                in_out, sum_out, head_out, g1_out, part_out, all_out, a_t, dh_low, dh_t, do, dqkv, da, *scratch):
    *buffers, send, recv, local = scratch
    m = pl.program_id(0)
    rows_of = lambda t: pl.ds(pl.multiple_of(t * pad, 16), pad)
    p = Place()
    s = Sends(send, recv)
    halves = pl.ds(0, 384), pl.ds(384, 384)
    reduces = [
        Reduce(p, s, g, [*buffers[4 * i : 4 * i + 4], None], None, cols, local.at[i])
        for i, (g, cols) in enumerate((g, cols) for g in (g2, g3) for cols in halves)
    ]
    trade = Trade(p, s, own_out, all_out, local.at[4])

    @pl.when(m == 0)
    def _():
        p.greet()
        for r in reduces:
            r.cores()
        trade.begin()

        @pl.loop(0, tiles)
        def _(t):
            rows = rows_of(t)
            normed, _ = ln(x_ref[rows, :])
            dh_low[rows, :] = (normed * vec_ref[0:1, :] + vec_ref[1:2, :]).astype(BF16)

        a_t[...] = dh_low[...].T
        dh_low[...] = dh_ref[...].astype(BF16)
        dh_t[...] = dh_low[...].T
        da[...] = jnp.zeros_like(da)
        sum_out[...] = jnp.zeros_like(sum_out)
        reduces[0].first()
        reduces[1].first()

    do[...] = nn(dh_low[...], w_ref[0, :, 576:768]).astype(BF16)
    g1_out[0, :, 576:768] = nn(dh_t[...], o_ref[0]).astype(BF16)

    @pl.loop(0, tiles)
    def _(t):
        rows = rows_of(t)
        qkv = qkv_ref[0, rows, :]
        grad = do[rows, :]
        parts = [[], [], []]
        for h in range(3):
            q, k, v = (qkv[:, 192 * j + 64 * h : 192 * j + 64 * h + 64] for j in range(3))
            g = grad[:, 64 * h : 64 * h + 64]
            low_p = p_ref[0, h, rows, :]
            prob = low_p.astype(F32)
            dp = nt(g, v)
            ds = (prob * (dp - jnp.sum(dp * prob, axis=-1, keepdims=True))).astype(BF16)
            parts[0].append(nn(ds, k) * 0.125)
            parts[1].append(tn(ds, q) * 0.125)
            parts[2].append(tn(low_p, g))
        dqkv[rows, :] = jnp.concatenate(parts[0] + parts[1] + parts[2], axis=1).astype(BF16)

    sums = jnp.sum(dqkv[...].astype(F32), axis=0, keepdims=True)
    head_out[0, 0:1, 0:192] = sums[:, 0:192]
    head_out[0, 1:2, 0:192] = sums[:, 384:576]
    g1_out[0, :, 0:576] = nn(a_t[...], dqkv[...]).astype(BF16)
    da[...] += nt(dqkv[...], w_ref[0, :, 0:576])

    @pl.when(m == 0)
    def _():
        reduces[2].first()
        reduces[3].first()

    @pl.when(m == 1)
    def _():
        reduces[0].second()

    @pl.when(m == 2)
    def _():
        trade.relay()
        reduces[1].second()

    @pl.when(m == pl.num_programs(0) - 1)
    def _():
        @pl.loop(0, tiles)
        def _(t):
            rows = rows_of(t)
            normed, inverse = ln(x_ref[rows, :])
            grad = da[rows, :]
            back = ln_back(grad * vec_ref[0:1, :], normed, inverse)
            in_out[rows, :] = (dh_ref[rows, :] + back).astype(BF16)
            sum_out[0:1, :] += jnp.sum(grad * normed, axis=0, keepdims=True)
            sum_out[1:2, :] += jnp.sum(grad, axis=0, keepdims=True)

        reduces[2].second()
        reduces[3].second()
        for i, r in enumerate(reduces):
            r.hand_on(part_out, i // 2, halves[i % 2])
        trade.done()
        s.finish()


def lay_kernel(seq, pad, count, out_ref, in_ref, out_out, in_out, wide):
    for t in range(count):
        wide[pl.ds(t, seq, stride=count), :] = out_ref[t, 0:seq, :].astype(F32)
        in_out[pl.ds(t, seq, stride=count), :] = in_ref[t, 0:seq, :].astype(F32)
    out_out[...] = wide[...].astype(BF16)


def update_kernel(*refs):
    attend_ref, feed_ref, small_ref = refs[:3]
    state, outs = refs[3:24], refs[24:]
    correction = 1.0 - 0.5**STEP
    rates = ((D // 2) ** -0.5, (D // 16) ** -0.5, D**-0.5, FF**-0.5, 0.1, 0.1, 0.15)

    def update(i, at, gradient):
        master, first, second = (state[i + 7 * j][at] for j in range(3))
        decay = DECAY if i < 4 else 0.0
        values = adamw_update(master, first, second, gradient, rates[i], decay, correction)
        for j, value in enumerate((gradient,) + values + (values[0].astype(BF16),)):
            outs[i + 7 * j][at] = value

    every = (slice(None), slice(None))
    for j in range(3):
        update(0, (j,) + every, attend_ref[:, 192 * j : 192 * j + 192])
    update(1, every, attend_ref[:, 576:768].T)
    update(2, every, feed_ref[0])
    update(3, every, feed_ref[1])
    for r in range(3):
        update(4, (r,) + every, small_ref[6:8, 8 * r : 8 * r + 8])
    update(5, every, small_ref[8:16, 0:12])
    update(6, every, small_ref[0:6, 0:96])


ALL = slice(None)


class Place:
    def __init__(self):
        dp, mp = lax.axis_index("dp"), lax.axis_index("mp")
        self.z, self.y = dp // 2, dp % 2
        self.x, self.c = mp // 2, mp % 2
        self.zs = [(self.z + k) % 4 for k in (1, 2, 3)]
        self.oy, self.ox, self.oc = 1 - self.y, 1 - self.x, 1 - self.c
        self.to_z = [self.id(z=z) for z in self.zs]
        self.to_y, self.to_x, self.to_c = self.id(y=self.oy), self.id(x=self.ox), self.id(c=self.oc)

    def id(self, z=None, y=None, x=None, c=None):
        z, y, x, c = (own if new is None else new for own, new in ((self.z, z), (self.y, y), (self.x, x), (self.c, c)))
        return (2 * z + y, 2 * x + c)

    def greet(self):
        barrier = pltpu.get_barrier_semaphore()
        for device in (*self.to_z, self.to_y, self.to_x, self.to_c):
            pl.semaphore_signal(barrier, inc=1, device_id=device, device_id_type=MESH)
        pl.semaphore_wait(barrier, 6)


class Sends:
    def __init__(self, send, recv):
        self.send, self.recv, self.all = send, recv, []

    def copy(self, src, dst, device):
        i = len(self.all)
        self.all.append(
            pltpu.make_async_remote_copy(
                src_ref=src,
                dst_ref=dst,
                send_sem=self.send.at[i],
                recv_sem=self.recv.at[i],
                device_id=device,
                device_id_type=MESH,
            )
        )
        return self.all[-1]

    def start(self, src, dst, device):
        copy = self.copy(src, dst, device)
        copy.start()
        return copy

    def finish(self):
        for copy in self.all:
            copy.wait_send()


def start(copies):
    for copy in copies:
        copy.start()


def arrived(copies):
    for copy in copies:
        copy.wait_recv()


class Gather:
    def __init__(self, p, s, full, split, cols=ALL, own=None, column=None):
        every = full.shape[4]
        at = lambda x, c, z, y, rows: full.at[x, c, z, y, rows, cols]
        col = lambda rows: at(p.x, p.c, ALL, p.y, rows) if column is None else column.at[:, rows, cols]
        both = lambda view, device: s.copy(view, view, device)
        high, low = pl.ds(0, split), pl.ds(split, every - split)
        here = at(p.x, p.c, p.z, p.y, ALL)
        self.z = [s.copy(own, here, device) for device in p.to_z] if column is None else []
        self.two = [s.copy(col(high), at(p.x, p.c, ALL, p.y, high), p.to_y)]
        self.three = [both(at(p.x, p.c, ALL, ALL, high), p.to_x)]
        self.core_two = [s.copy(col(ALL), at(p.x, p.c, ALL, p.y, ALL), p.to_c)]
        self.core_three = [both(at(p.x, p.c, ALL, p.oy, high), p.to_c)]
        self.core_last = [both(at(p.ox, p.c, ALL, ALL, high), p.to_c)]
        if split < every:
            self.two.append(s.copy(col(low), at(p.x, p.c, ALL, p.y, low), p.to_x))
            self.three += [both(at(x, p.c, ALL, p.y, low), p.to_y) for x in (0, 1)]
            self.core_three.append(both(at(p.ox, p.c, ALL, p.y, low), p.to_c))
            self.core_last += [both(at(x, p.c, ALL, p.oy, low), p.to_c) for x in (0, 1)]

    def along_z(self):
        start(self.z)

    def second(self):
        arrived(self.z)
        start(self.two)
        start(self.core_two)

    def third(self):
        arrived(self.two)
        start(self.three)
        start(self.core_three)

    def last(self):
        arrived(self.three)
        start(self.core_last)

    def done(self):
        arrived(self.core_two + self.core_three + self.core_last)

    COPIES = 14
    COPIES_WHOLE = 8


def gather_kernel(seq, pad, tiles, w_ref, s_ref, tok, cot, vis_ref, tab_ref, live_ref,
                  f1, col2, x_out, dy_out, vec_out, off_out, fs, tok_ref, cot_ref, wide, grad, send, recv, local):
    p = Place()
    s = Sends(send, recv)
    half = pl.ds(0, 384), pl.ds(384, 384)
    gathers = [
        Gather(p, s, fs, 16, own=s_ref),
        *(Gather(p, s, f1, 48, cols, own=w_ref.at[0, :, cols]) for cols in half),
    ]
    ahead = [s.copy(w_ref.at[1], col2.at[p.z], device) for device in p.to_z]
    group = pl.ds(pl.multiple_of(8 * p.x, 8), 8)
    rows_in = [
        pltpu.make_async_copy(tok.at[:, group], tok_ref, local.at[3]),
        pltpu.make_async_copy(cot.at[:, group], cot_ref, local.at[4]),
    ]
    mine = [
        pltpu.make_async_copy(s_ref, fs.at[p.x, p.c, p.z, p.y], local.at[0]),
        pltpu.make_async_copy(w_ref.at[0], f1.at[p.x, p.c, p.z, p.y], local.at[1]),
        pltpu.make_async_copy(w_ref.at[1], col2.at[p.z], local.at[2]),
    ]
    p.greet()
    for g in gathers:
        g.along_z()
    start(ahead)
    start(mine)
    start(rows_in)
    rows_in[0].wait()
    lay_tokens(seq, pad, tiles, p.c * tiles, tok_ref, vis_ref, tab_ref, x_out, wide)
    for copy in mine:
        copy.wait()
    gathers[0].second()
    gathers[1].second()
    rows_in[1].wait()
    lay_cotangent(seq, pad, tiles, p.c * tiles, live_ref, cot_ref, dy_out, wide, grad)
    stages = [("third", 0), ("second", 2), ("third", 1), ("last", 0), ("third", 2), ("done", 0)]
    for name, i in stages:
        getattr(gathers[i], name)()
    spread_small(fs, vec_out, off_out)
    for name, i in [("last", 1), ("last", 2), ("done", 1), ("done", 2)]:
        getattr(gathers[i], name)()
    arrived(ahead)
    s.finish()


def add_into(target, other, lead):
    total = math.prod(lead)

    @pl.loop(0, total)
    def _(i):
        index = []
        for size in reversed(lead):
            index.append(i % size)
            i = i // size
        index = tuple(reversed(index))
        target[index] = (target[index].astype(F32) + other(*index).astype(F32)).astype(BF16)


class Reduce:
    COPIES = 6

    def __init__(self, p, s, parts, buffers, out, cols, load):
        own, r0, r1, r2, r3 = buffers
        self.p, self.out, self.own, self.r0, self.r1, self.r2, self.r3 = p, out, own, r0, r1, r2, r3
        self.load = pltpu.make_async_copy(parts.at[:, p.c, :, :, :, cols], own, load)
        self.core = [s.copy(parts.at[:, p.oc, :, :, :, cols], r0, p.to_c)]
        self.over_y = [s.copy(r0.at[:, :, p.oy], r1, p.to_y)]
        self.over_x = [s.copy(r1.at[p.ox], r2, p.to_x)]
        if r3 is not None:
            self.over_z = [s.copy(r2.at[z], r3.at[k], device) for k, (z, device) in enumerate(zip(p.zs, p.to_z))]

    def cores(self):
        start(self.core)
        self.load.start()

    def first(self):
        self.load.wait()
        arrived(self.core)
        add_into(self.r0, lambda x, z, y: self.own[x, z, y], self.r0.shape[:3])
        start(self.over_y)

    def second(self):
        arrived(self.over_y)
        add_into(self.r1, lambda x, z: self.r0[x, z, self.p.y], self.r1.shape[:2])
        start(self.over_x)

    def third(self):
        arrived(self.over_x)
        add_into(self.r2, lambda z: self.r1[self.p.x, z], self.r2.shape[:1])
        start(self.over_z)

    def hand_on(self, out, i, cols):
        arrived(self.over_x)
        for z in range(4):
            out[z, i, :, cols] = (self.r2[z].astype(F32) + self.r1[self.p.x, z].astype(F32)).astype(BF16)

    def last(self):
        arrived(self.over_z)
        r2, r3 = self.r2, self.r3
        self.out[...] = r2[self.p.z].astype(F32) + r3[0].astype(F32) + r3[1].astype(F32) + r3[2].astype(F32)

    @staticmethod
    def scratch(rows, columns):
        lead = (2, 4, 2), (2, 4, 2), (2, 4), (4,), (3,)
        return [pltpu.VMEM(shape + (rows, columns), BF16) for shape in lead]


class Trade:
    COPIES = 3

    def __init__(self, p, s, own, full, local):
        here, there = full.at[p.x, p.c], full.at[p.ox, p.c]
        self.mine = pltpu.make_async_copy(own, here, local)
        self.x, self.c = [s.copy(own, here, p.to_x)], [s.copy(own, here, p.to_c)]
        self.further = [s.copy(there, there, p.to_c)]

    def begin(self):
        start(self.x)
        start(self.c)
        self.mine.start()

    def relay(self):
        arrived(self.x)
        start(self.further)

    def done(self):
        arrived(self.c + self.further)
        self.mine.wait()


def reduce_kernel(g1, own_in, part, sum_two, sum_one, sum_hid, sum_head, total, feed, small, all_in,
                  part_z, gs, lines, *scratch):
    *buffers, send, recv, local = scratch
    p = Place()
    s = Sends(send, recv)
    thirds = [pl.ds(256 * i, 256) for i in range(3)]
    reduces = [
        Reduce(p, s, g1, buffers[5 * i : 5 * i + 5], total.at[:, cols], cols, local.at[i])
        for i, cols in enumerate(thirds)
    ]
    reduces.append(Reduce(p, s, gs, buffers[15:20], small, ALL, local.at[3]))
    over_z = [s.copy(part.at[z], part_z.at[k], device) for k, (z, device) in enumerate(zip(p.zs, p.to_z))]
    trade = Trade(p, s, own_in, all_in, local.at[4])
    p.greet()
    for r in reduces[:3]:
        r.cores()
    trade.begin()
    start(over_z)
    squeeze_small(sum_two, sum_one, sum_hid, sum_head, gs, lines)
    reduces[3].cores()
    for r in reduces:
        r.first()
    reduces[0].second()
    reduces[1].second()
    reduces[0].third()
    reduces[2].second()
    reduces[1].third()
    reduces[3].second()
    trade.relay()
    reduces[2].third()
    reduces[3].third()
    arrived(over_z)
    for i in range(2):
        feed[i] = part[p.z, i].astype(F32) + sum(part_z[k, i].astype(F32) for k in range(3))
    for r in reduces:
        r.last()
    trade.done()
    s.finish()


def fast_shards(*args):
    (tokens, cotangent, visible, tile_counts, *state) = args
    tile_count, seq, width = tokens.shape
    mp_size = lax.axis_size("mp")
    tiles = tile_count // mp_size
    pad = -(-seq // 16) * 16
    rows = tiles * pad
    native = lambda i, a: a.transpose(1, 0, 2) if i in (0, 4) else a.T if i in (3, 5) else a
    state = [native(i % 7, a) for i, a in enumerate(state)]
    params = lambda limit=None, **kw: pltpu.CompilerParams(vmem_limit_bytes=60 << 20, **kw)
    shape = jax.ShapeDtypeStruct
    me = lax.axis_index("mp").astype(jnp.int32)
    place = me * tiles + jnp.arange(tiles, dtype=jnp.int32)
    live = jnp.broadcast_to((place < tile_counts[0]).astype(F32)[:, None], (tiles, 128))
    by_place = lambda a: a.transpose(1, 0, 2)
    places = lax.dynamic_slice(visible, (me * tiles, 0), (tiles, seq)).T
    table = jnp.asarray(position_rows())
    vmem, anywhere = pl.BlockSpec(memory_space=pltpu.VMEM), pl.BlockSpec(memory_space=ANY)

    own, own_small = pl.pallas_call(
        pack_kernel,
        out_shape=(shape((3, 96, D), BF16), shape((16, 128), BF16)),
        scratch_shapes=[pltpu.VMEM((16, 128), F32)],
        compiler_params=params(),
        name="pack",
    )(*state[:7])

    full = shape((2, 2, 4, 2, 96, D), BF16)
    dma = lambda count: pltpu.SemaphoreType.DMA((count,))
    copies = 2 * Gather.COPIES + Gather.COPIES_WHOLE + 3
    f1, col2, x, dy, vec, off = pl.pallas_call(
        functools.partial(gather_kernel, seq, pad, tiles),
        out_shape=(
            full,
            shape((4, 96, D), BF16),
            shape((rows, D), F32),
            shape((rows, D), BF16),
            shape((16, D), F32),
            shape((4, 8, D), F32),
        ),
        in_specs=[vmem] * 2 + [anywhere] * 2 + [vmem] * 3,
        out_specs=[anywhere] * 2 + [vmem] * 4,
        scratch_shapes=[
            pltpu.VMEM((2, 2, 4, 2, 16, 128), BF16),
            pltpu.VMEM((seq, 8, D), BF16),
            pltpu.VMEM((seq, 8, D), BF16),
            pltpu.VMEM((D // 128, seq * 8, 128), F32),
            pltpu.VMEM((rows, D), F32),
            dma(copies),
            dma(copies),
            dma(5),
        ],
        compiler_params=params(collective_id=0, has_side_effects=True),
        name="gather",
    )(own, own_small, by_place(tokens), by_place(cotangent), places, table, live)
    w1 = f1.reshape(4, D, D)

    of_group1 = lambda *shape: pl.BlockSpec((1,) + shape, lambda m: (m,) + (0,) * len(shape))
    all_of1 = lambda *shape: pl.BlockSpec(shape, lambda m: (0,) * len(shape))
    copies = Gather.COPIES * 2 - 3
    h, qkv, probs, o, f2, f3 = pl.pallas_call(
        functools.partial(attend_kernel, seq, pad, tiles),
        out_shape=(
            shape((rows, D), F32),
            shape((4, rows, 576), BF16),
            shape((4, 3, rows, pad), BF16),
            shape((4, rows, 192), BF16),
            full,
            full,
        ),
        grid=(4,),
        in_specs=[all_of1(rows, D), all_of1(16, D), of_group1(8, D), of_group1(D, D), all_of1(4, 96, D), pl.BlockSpec((1, 96, D), lambda m: (2, 0, 0))],
        out_specs=(all_of1(rows, D), of_group1(rows, 576), of_group1(3, rows, pad), of_group1(rows, 192))
        + (pl.BlockSpec(memory_space=ANY),) * 2,
        scratch_shapes=[pltpu.VMEM((rows, D), BF16), dma(copies), dma(copies), dma(2)],
        compiler_params=params(collective_id=2, has_side_effects=True),
        name="attend",
    )(x, vec, off, w1, col2, own)
    w2, w3 = (f.reshape(4, D, D) for f in (f2, f3))

    out_own, dh, sum_two, sum_hid, g2, g3 = pl.pallas_call(
        functools.partial(feed_kernel, seq, pad, tiles),
        out_shape=(
            shape((rows, D), BF16),
            shape((rows, D), F32),
            shape((8, D), F32),
            shape((4, 8, D), F32),
            shape((4, D, D), BF16),
            shape((4, D, D), BF16),
        ),
        grid=(4,),
        in_specs=[all_of1(tiles, 128), all_of1(rows, D), all_of1(rows, D), all_of1(16, D), of_group1(8, D),
                  of_group1(D, D), of_group1(D, D)],
        out_specs=(all_of1(rows, D), all_of1(rows, D), all_of1(8, D), of_group1(8, D), of_group1(D, D), of_group1(D, D)),
        scratch_shapes=[
            pltpu.VMEM((rows, D), BF16),
            pltpu.VMEM((D, rows), BF16),
            pltpu.VMEM((D, rows), BF16),
            pltpu.VMEM((rows, D), F32),
            pltpu.VMEM((rows, D), F32),
        ],
        compiler_params=params(),
        name="feed",
    )(live, dy, h, vec, off, w2, w3)

    by_device = lambda g: g.reshape(2, 2, 4, 2, 96, D)
    everyone = shape((2, 2, rows, D), BF16)
    copies = 4 * (Reduce.COPIES - 3) + Trade.COPIES
    in_own, sum_one, sum_head, g1, part, all_out = pl.pallas_call(
        functools.partial(back_kernel, seq, pad, tiles),
        out_shape=(
            shape((rows, D), BF16),
            shape((8, D), F32),
            shape((4, 8, D), F32),
            shape((4, D, D), BF16),
            shape((4, 2, 96, D), BF16),
            everyone,
        ),
        grid=(4,),
        in_specs=[all_of1(rows, D), all_of1(rows, D), all_of1(16, D), of_group1(D, D), of_group1(rows, 576),
                  of_group1(3, rows, pad), of_group1(rows, 192)] + [pl.BlockSpec(memory_space=ANY)] * 3,
        out_specs=(all_of1(rows, D), all_of1(8, D), of_group1(8, D), of_group1(D, D), all_of1(4, 2, 96, D),
                   pl.BlockSpec(memory_space=ANY)),
        scratch_shapes=[
            pltpu.VMEM((D, rows), BF16),
            pltpu.VMEM((rows, D), BF16),
            pltpu.VMEM((D, rows), BF16),
            pltpu.VMEM((rows, 192), BF16),
            pltpu.VMEM((rows, 576), BF16),
            pltpu.VMEM((rows, D), F32),
            *(4 * Reduce.scratch(96, 384)[:4]),
            dma(copies),
            dma(copies),
            dma(5),
        ],
        compiler_params=params(collective_id=3, has_side_effects=True),
        name="back",
    )(x, dh, vec, w1, qkv, probs, o, by_device(g2), by_device(g3), out_own)

    copies = 4 * Reduce.COPIES + 3 + Trade.COPIES
    total_attend, total_feed, small, all_in = pl.pallas_call(
        reduce_kernel,
        out_shape=(shape((96, D), F32), shape((2, 96, D), F32), shape((16, 128), F32), everyone),
        in_specs=[anywhere] * 2 + [vmem] * 5,
        out_specs=[vmem] * 3 + [anywhere],
        scratch_shapes=[
            pltpu.VMEM((3, 2, 96, D), BF16),
            pltpu.VMEM((2, 2, 4, 2, 16, 128), BF16),
            pltpu.VMEM((8, D), F32),
            *(3 * Reduce.scratch(96, 256)),
            *Reduce.scratch(16, 128),
            dma(copies),
            dma(copies),
            dma(5),
        ],
        compiler_params=params(collective_id=1, has_side_effects=True),
        name="reduce",
    )(by_device(g1), in_own, part, sum_two, sum_one, sum_hid, sum_head)

    flat = seq * tile_count
    block = pl.BlockSpec((tile_count, pad, 128), lambda n: (0, 0, n))
    output, input_grad = pl.pallas_call(
        functools.partial(lay_kernel, seq, pad, tile_count),
        out_shape=(shape((flat, D), BF16), shape((flat, D), F32)),
        grid=(D // 128,),
        in_specs=[block, block],
        out_specs=(pl.BlockSpec((flat, 128), lambda n: (0, n)),) * 2,
        scratch_shapes=[pltpu.VMEM((flat, 128), F32)],
        compiler_params=params(),
        name="lay",
    )(*(a.reshape(tile_count, pad, D) for a in (all_out, all_in)))
    output, input_grad = (a.reshape(seq, tile_count, D).transpose(1, 0, 2) for a in (output, input_grad))

    kinds = [shape(a.shape, F32) for a in state[:7]]
    results = pl.pallas_call(
        update_kernel,
        out_shape=tuple(kinds * 4 + [shape(a.shape, BF16) for a in kinds]),
        compiler_params=params(),
        name="update",
    )(total_attend, total_feed, small, *state)
    return (output, input_grad) + tuple(native(i % 7, a) for i, a in enumerate(results))


def solution(mesh):
    in_specs = (
        P("dp", None, None),
        P("dp", None, None),
        P("dp", None),
        P("dp"),
        P("dp", None, "mp"),
        P("mp", "dp"),
        P("dp", "mp"),
        P("mp", "dp"),
        P(None, "mp", "dp"),
        P("mp", "dp"),
        P(None, "dp"),
        P("dp", None, "mp"),
        P("mp", "dp"),
        P("dp", "mp"),
        P("mp", "dp"),
        P(None, "mp", "dp"),
        P("mp", "dp"),
        P(None, "dp"),
        P("dp", None, "mp"),
        P("mp", "dp"),
        P("dp", "mp"),
        P("mp", "dp"),
        P(None, "mp", "dp"),
        P("mp", "dp"),
        P(None, "dp"),
    )
    out_specs = (
        P("dp", None, None),
        P("dp", None, None),
        P("dp", None, "mp"),
        P("mp", "dp"),
        P("dp", "mp"),
        P("mp", "dp"),
        P(None, "mp", "dp"),
        P("mp", "dp"),
        P(None, "dp"),
        P("dp", None, "mp"),
        P("mp", "dp"),
        P("dp", "mp"),
        P("mp", "dp"),
        P(None, "mp", "dp"),
        P("mp", "dp"),
        P(None, "dp"),
        P("dp", None, "mp"),
        P("mp", "dp"),
        P("dp", "mp"),
        P("mp", "dp"),
        P(None, "mp", "dp"),
        P("mp", "dp"),
        P(None, "dp"),
        P("dp", None, "mp"),
        P("mp", "dp"),
        P("dp", "mp"),
        P("mp", "dp"),
        P(None, "mp", "dp"),
        P("mp", "dp"),
        P(None, "dp"),
        P("dp", None, "mp"),
        P("mp", "dp"),
        P("dp", "mp"),
        P("mp", "dp"),
        P(None, "mp", "dp"),
        P("mp", "dp"),
        P(None, "dp"),
    )
    sizes = (mesh.shape["dp"], mesh.shape["mp"])
    body = fast_shards if sizes == (8, 4) else shards
    return jax.shard_map(body, mesh=mesh, in_specs=in_specs, out_specs=out_specs, check_vma=False)
```

```python
import functools
import math

import jax
import jax.numpy as jnp
import numpy as np
from jax import lax
from jax.experimental import pallas as pl
from jax.experimental.pallas import tpu as pltpu
from jax.sharding import PartitionSpec as P

D = 768
FF = 3072
GRID = 14
STEP = 3


LN_EPS = 1e-06
BETA_ONE = 0.5
BETA_TWO = 0.5
ADAM_EPS = 1e-08
DECAY = 0.05


def cut_along(x, dim, size):
    dims = x.shape
    parts = x.reshape(*dims[:dim], size, dims[dim] // size, *dims[dim + 1 :])
    return jnp.moveaxis(parts, dim, 0)


def summed_on_arrival(x, axis, dim):
    size = lax.axis_size(axis)
    parts = lax.all_to_all(cut_along(x, dim, size), axis, 0, 0, tiled=True)
    return jnp.sum(parts.astype(jnp.float32), axis=0)


def sine_table(places, feature_width):
    half_width = feature_width // 2
    spread = jnp.arange(half_width, dtype=jnp.float32) / half_width
    frequency = jnp.exp(-math.log(10000.0) * spread)
    angles = places[..., None] * frequency
    return jnp.concatenate([jnp.sin(angles), jnp.cos(angles)], axis=-1)


def position_table(visible, feature_width):
    plane_size = GRID * GRID
    frame_place = (visible // plane_size).astype(jnp.float32)
    within = visible % plane_size
    row_place = (within // GRID).astype(jnp.float32)
    column_place = (within % GRID).astype(jnp.float32)
    time_width = feature_width // 16 * 4
    space_width = feature_width // 16 * 6
    return jnp.concatenate(
        [
            sine_table(frame_place, time_width),
            sine_table(row_place, space_width),
            sine_table(column_place, space_width),
        ],
        axis=-1,
    )


def normalize(values):
    center = values - jnp.mean(values, axis=-1, keepdims=True)
    inverse = lax.rsqrt(jnp.mean(center * center, axis=-1, keepdims=True) + LN_EPS)
    return (center * inverse, inverse)


def norm_back(grad_normed, normed, inverse):
    return inverse * (
        grad_normed
        - jnp.mean(grad_normed, axis=-1, keepdims=True)
        - normed * jnp.mean(grad_normed * normed, axis=-1, keepdims=True)
    )


def over_rows(former, latter):
    return lax.dot_general(
        former, latter, (((0,), (0,)), ((), ())), preferred_element_type=jnp.float32
    )


def over_cols(former, latter):
    return lax.dot_general(
        former, latter, (((1,), (1,)), ((), ())), preferred_element_type=jnp.float32
    )


def exact_gelu(values):
    return jax.nn.gelu(values, approximate=False)


def adamw_update(
    master, first_moment, second_moment, gradient, step_rate, weight_decay, correction
):
    first_new = BETA_ONE * first_moment + (1.0 - BETA_ONE) * gradient
    second_new = BETA_TWO * second_moment + (1.0 - BETA_TWO) * gradient * gradient
    ratio = first_new / correction / (jnp.sqrt(second_new / correction) + ADAM_EPS)
    master_new = master - step_rate * (ratio + weight_decay * master)
    return (master_new, first_new, second_new)


def shards(
    tokens,
    cotangent,
    visible,
    tile_counts,
    attend_weight,
    project_weight,
    widen_weight,
    narrow_weight,
    heads_offset,
    hidden_offset,
    layer_vectors,
    attend_first,
    project_first,
    widen_first,
    narrow_first,
    heads_first,
    hidden_first,
    vectors_first,
    attend_second,
    project_second,
    widen_second,
    narrow_second,
    heads_second,
    hidden_second,
    vectors_second,
):
    fore_attend, fore_project, fore_widen, fore_narrow, fore_heads, fore_hidden, fore_vectors = (
        lax.all_gather(attend_weight.astype(jnp.bfloat16), "dp", axis=0, tiled=True),
        lax.all_gather(project_weight.astype(jnp.bfloat16), "dp", axis=1, tiled=True),
        lax.all_gather(widen_weight.astype(jnp.bfloat16), "dp", axis=0, tiled=True),
        lax.all_gather(narrow_weight.astype(jnp.bfloat16), "dp", axis=1, tiled=True),
        lax.all_gather(heads_offset.astype(jnp.bfloat16), "dp", axis=2, tiled=True),
        lax.all_gather(hidden_offset.astype(jnp.bfloat16), "dp", axis=1, tiled=True),
        lax.all_gather(layer_vectors.astype(jnp.bfloat16), "dp", axis=1, tiled=True),
    )
    tile_count, seq_length, model_width = tokens.shape
    row_count = tile_count * seq_length
    local_width = fore_attend.shape[2]
    heads_local = fore_heads.shape[1]
    head_size = fore_heads.shape[2]
    score_scale = 1.0 / math.sqrt(head_size)
    live_tiles = (jnp.arange(tile_count, dtype=jnp.int32) < tile_counts[0]).astype(jnp.float32)
    live_rows = jnp.broadcast_to(live_tiles[:, None], (tile_count, seq_length)).reshape(
        row_count, 1
    )
    vectors = fore_vectors.astype(jnp.float32)
    summed = (tokens.astype(jnp.float32) + position_table(visible, model_width)).reshape(
        row_count, model_width
    )
    normed_one, inverse_one = normalize(summed)
    attend_low = (normed_one * vectors[0] + vectors[1]).astype(jnp.bfloat16)
    linear = jnp.dot(
        attend_low,
        fore_attend.reshape(model_width, 3 * local_width),
        preferred_element_type=jnp.float32,
    ).reshape(row_count, 3, local_width)
    offsets = fore_heads.astype(jnp.float32).reshape(2, local_width)
    head_shape = (tile_count, seq_length, heads_local, head_size)
    query_low = (linear[:, 0] + offsets[0]).astype(jnp.bfloat16).reshape(head_shape)
    key_low = linear[:, 1].astype(jnp.bfloat16).reshape(head_shape)
    value_low = (linear[:, 2] + offsets[1]).astype(jnp.bfloat16).reshape(head_shape)
    scores = (
        jnp.einsum("tqhd,tkhd->thqk", query_low, key_low, preferred_element_type=jnp.float32)
        * score_scale
    )
    row_top = jnp.max(scores, axis=-1, keepdims=True)
    log_total = row_top + jnp.log(jnp.sum(jnp.exp(scores - row_top), axis=-1, keepdims=True))
    weights_low = jnp.exp(scores - log_total).astype(jnp.bfloat16)
    context = jnp.einsum(
        "thqk,tkhd->tqhd", weights_low, value_low, preferred_element_type=jnp.float32
    )
    context_low = context.reshape(row_count, local_width).astype(jnp.bfloat16)
    attention_part = jnp.dot(context_low, fore_project, preferred_element_type=jnp.float32)
    attention = lax.psum(attention_part.astype(jnp.bfloat16), "mp").astype(jnp.float32)
    middle = summed + attention + vectors[4]
    normed_two, inverse_two = normalize(middle)
    widen_low = (normed_two * vectors[2] + vectors[3]).astype(jnp.bfloat16)
    hidden = jnp.dot(
        widen_low, fore_widen, preferred_element_type=jnp.float32
    ) + fore_hidden.astype(jnp.float32).reshape(-1)
    active_low = exact_gelu(hidden).astype(jnp.bfloat16)
    feed_part = jnp.dot(active_low, fore_narrow, preferred_element_type=jnp.float32)
    feed_sum = lax.psum(feed_part.astype(jnp.bfloat16), "mp").astype(jnp.float32)
    result = (middle + feed_sum + vectors[5]) * live_rows
    output_low = result.astype(jnp.bfloat16)
    back_attend, back_project, back_widen, back_narrow, back_vectors = (
        fore_attend,
        fore_project,
        fore_widen,
        fore_narrow,
        fore_vectors,
    )
    vectors_back = back_vectors.astype(jnp.float32)
    grad_out = cotangent.astype(jnp.float32).reshape(row_count, model_width) * live_rows
    grad_out_low = grad_out.astype(jnp.bfloat16)
    grad_narrow = over_rows(active_low, grad_out_low)
    grad_active = over_cols(grad_out_low, back_narrow)
    gelu_back = jax.vjp(exact_gelu, hidden)[1]
    grad_hidden_low = gelu_back(grad_active)[0].astype(jnp.bfloat16)
    grad_widen = over_rows(widen_low, grad_hidden_low)
    grad_hidden = jnp.sum(grad_hidden_low.astype(jnp.float32), axis=0).reshape(fore_hidden.shape)
    normed_two_part = over_cols(grad_hidden_low, back_widen)
    grad_normed_two = lax.psum(normed_two_part.astype(jnp.bfloat16), "mp").astype(jnp.float32)
    grad_middle = grad_out + norm_back(grad_normed_two * vectors_back[2], normed_two, inverse_two)
    grad_middle_low = grad_middle.astype(jnp.bfloat16)
    grad_project = over_rows(context_low, grad_middle_low)
    grad_context_low = (
        over_cols(grad_middle_low, back_project).astype(jnp.bfloat16).reshape(head_shape)
    )
    scores_again = (
        jnp.einsum("tqhd,tkhd->thqk", query_low, key_low, preferred_element_type=jnp.float32)
        * score_scale
    )
    weights_full = jnp.exp(scores_again - log_total)
    weights_again_low = weights_full.astype(jnp.bfloat16)
    grad_weights = jnp.einsum(
        "tqhd,tkhd->thqk", grad_context_low, value_low, preferred_element_type=jnp.float32
    )
    grad_value = jnp.einsum(
        "thqk,tqhd->tkhd", weights_again_low, grad_context_low, preferred_element_type=jnp.float32
    )
    row_dot = jnp.sum(grad_weights * weights_full, axis=-1, keepdims=True)
    grad_scores_low = (weights_full * (grad_weights - row_dot)).astype(jnp.bfloat16)
    grad_query = (
        jnp.einsum("thqk,tkhd->tqhd", grad_scores_low, key_low, preferred_element_type=jnp.float32)
        * score_scale
    )
    grad_key = (
        jnp.einsum(
            "thqk,tqhd->tkhd", grad_scores_low, query_low, preferred_element_type=jnp.float32
        )
        * score_scale
    )
    grad_qkv_low = jnp.stack(
        [
            grad_query.reshape(row_count, local_width),
            grad_key.reshape(row_count, local_width),
            grad_value.reshape(row_count, local_width),
        ],
        axis=1,
    ).astype(jnp.bfloat16)
    grad_offsets = jnp.sum(grad_qkv_low.astype(jnp.float32), axis=0)
    grad_heads = jnp.stack([grad_offsets[0], grad_offsets[2]]).reshape(2, heads_local, head_size)
    flat_qkv = grad_qkv_low.reshape(row_count, 3 * local_width)
    grad_attend = over_rows(attend_low, flat_qkv).reshape(model_width, 3, local_width)
    normed_one_part = over_cols(flat_qkv, back_attend.reshape(model_width, 3 * local_width))
    grad_normed_one = lax.psum(normed_one_part.astype(jnp.bfloat16), "mp").astype(jnp.float32)
    grad_inputs = grad_middle + norm_back(
        grad_normed_one * vectors_back[0], normed_one, inverse_one
    )
    grad_vectors = jnp.stack(
        [
            jnp.sum(grad_normed_one * normed_one, axis=0),
            jnp.sum(grad_normed_one, axis=0),
            jnp.sum(grad_normed_two * normed_two, axis=0),
            jnp.sum(grad_normed_two, axis=0),
            jnp.sum(grad_middle, axis=0),
            jnp.sum(grad_out, axis=0),
        ]
    )
    output = output_low.reshape(tile_count, seq_length, model_width)
    input_grad = grad_inputs.reshape(tile_count, seq_length, model_width)
    (
        shard_attend,
        shard_project,
        shard_widen,
        shard_narrow,
        shard_heads,
        shard_hidden,
        shard_vectors,
    ) = (
        summed_on_arrival(grad_attend.astype(jnp.bfloat16), "dp", 0),
        summed_on_arrival(grad_project.astype(jnp.bfloat16), "dp", 1),
        summed_on_arrival(grad_widen.astype(jnp.bfloat16), "dp", 0),
        summed_on_arrival(grad_narrow.astype(jnp.bfloat16), "dp", 1),
        summed_on_arrival(grad_heads.astype(jnp.bfloat16), "dp", 2),
        summed_on_arrival(grad_hidden.astype(jnp.bfloat16), "dp", 1),
        summed_on_arrival(grad_vectors.astype(jnp.bfloat16), "dp", 1),
    )
    correction = 1.0 - 0.5**STEP
    new_attend, first_attend, second_attend = adamw_update(
        attend_weight,
        attend_first,
        attend_second,
        shard_attend,
        (D // 2) ** (-0.5),
        DECAY,
        correction,
    )
    new_project, first_project, second_project = adamw_update(
        project_weight,
        project_first,
        project_second,
        shard_project,
        (D // 16) ** (-0.5),
        DECAY,
        correction,
    )
    new_widen, first_widen, second_widen = adamw_update(
        widen_weight, widen_first, widen_second, shard_widen, D ** (-0.5), DECAY, correction
    )
    new_narrow, first_narrow, second_narrow = adamw_update(
        narrow_weight, narrow_first, narrow_second, shard_narrow, FF ** (-0.5), DECAY, correction
    )
    new_heads, first_heads, second_heads = adamw_update(
        heads_offset, heads_first, heads_second, shard_heads, 0.1, 0.0, correction
    )
    new_hidden, first_hidden, second_hidden = adamw_update(
        hidden_offset, hidden_first, hidden_second, shard_hidden, 0.1, 0.0, correction
    )
    new_vectors, first_vectors, second_vectors = adamw_update(
        layer_vectors, vectors_first, vectors_second, shard_vectors, 0.15, 0.0, correction
    )
    return (
        output,
        input_grad,
        shard_attend,
        shard_project,
        shard_widen,
        shard_narrow,
        shard_heads,
        shard_hidden,
        shard_vectors,
        new_attend,
        new_project,
        new_widen,
        new_narrow,
        new_heads,
        new_hidden,
        new_vectors,
        first_attend,
        first_project,
        first_widen,
        first_narrow,
        first_heads,
        first_hidden,
        first_vectors,
        second_attend,
        second_project,
        second_widen,
        second_narrow,
        second_heads,
        second_hidden,
        second_vectors,
        new_attend.astype(jnp.bfloat16),
        new_project.astype(jnp.bfloat16),
        new_widen.astype(jnp.bfloat16),
        new_narrow.astype(jnp.bfloat16),
        new_heads.astype(jnp.bfloat16),
        new_hidden.astype(jnp.bfloat16),
        new_vectors.astype(jnp.bfloat16),
    )


F32 = jnp.float32
BF16 = jnp.bfloat16
MESH = pl.DeviceIdType.MESH
ANY = pl.ANY


def nn(former, latter):
    return lax.dot_general(former, latter, (((1,), (0,)), ((), ())), preferred_element_type=F32)


def nt(former, latter):
    return lax.dot_general(former, latter, (((1,), (1,)), ((), ())), preferred_element_type=F32)


def tn(former, latter):
    return lax.dot_general(former, latter, (((0,), (0,)), ((), ())), preferred_element_type=F32)


def iota(shape, dim):
    return lax.broadcasted_iota(jnp.int32, shape, dim)


def whole(ref_shape):
    rank = len(ref_shape)
    return pl.BlockSpec(ref_shape, lambda *_: (0,) * rank)


def pick_vector(d):
    shape = (128, D)
    lane, column = iota(shape, 0), iota(shape, 1)
    return ((column - lane == 96 * d) & (lane < 96)).astype(F32).astype(BF16)


def pick_head(d):
    shape = (128, D)
    lane, column = iota(shape, 0), iota(shape, 1)
    same = (lax.shift_right_logical(column, 6) == lax.shift_right_logical(lane, 3)) & ((column & 7) == (lane & 7))
    return (same & ((lax.shift_right_logical(column, 3) & 7) == d) & (lane < 24)).astype(F32).astype(BF16)


def pick_row():
    shape = (128, D)
    return (lax.shift_right_logical(iota(shape, 1), 6) == iota(shape, 0)).astype(F32).astype(BF16)


def hidden_places(d):
    shape = (8, D)
    column = iota(shape, 1)
    return ((column & 7) == iota(shape, 0)) & ((lax.shift_right_logical(column, 3) & 7) == d)


def pack_kernel(attend, project, widen, narrow, heads, hidden, vectors, w_out, s_out, scratch):
    w_out[0] = jnp.concatenate([attend[0], attend[1], attend[2], project[...].T], axis=1).astype(BF16)
    w_out[1] = widen[...].astype(BF16)
    w_out[2] = narrow[...].astype(BF16)
    scratch[...] = jnp.zeros_like(scratch)
    scratch[0:6, 0:96] = vectors[...]
    for r in range(3):
        scratch[6:8, 8 * r : 8 * r + 8] = heads[r]
    scratch[8:16, 0:12] = hidden[...]
    s_out[...] = scratch[...].astype(BF16)


def spread_small(s_ref, vec_out, off_out):
    row_pick = pick_row()
    vec = jnp.zeros((16, D), F32)
    heads = [jnp.zeros((16, D), F32) for _ in range(4)]
    hidden = [jnp.zeros((1, D), F32) for _ in range(4)]
    for d in range(8):
        vec += nn(s_ref[0, 0, d // 2, d % 2], pick_vector(d))
        head_pick, places = pick_head(d), hidden_places(d)
        for m in range(4):
            block = s_ref[m // 2, m % 2, d // 2, d % 2]
            heads[m] += nn(block, head_pick)
            spread = nn(block, row_pick)[8:16]
            hidden[m] += jnp.sum(jnp.where(places, spread, 0.0), axis=0, keepdims=True)
    vec_out[...] = vec
    for m in range(4):
        off_out[m, 0:2, :] = heads[m][6:8]
        off_out[m, 2:3, :] = hidden[m]
        off_out[m, 3:8, :] = jnp.zeros((5, D), F32)


def squeeze_small(fore_ref, back_ref, hid_ref, heads_ref, out_ref, rows):
    rows[...] = jnp.zeros_like(rows)
    rows[0:2, :] = back_ref[0:2, :]
    rows[2:6, :] = fore_ref[0:4, :]
    row_pick = pick_row()
    shape = (8, 128)
    for m in range(4):
        rows[6:7, 0:192] = heads_ref[m, 0:1, 0:192]
        rows[7:8, 0:192] = heads_ref[m, 1:2, 0:192]
        block = rows[...].astype(BF16)
        wide = jnp.broadcast_to(hid_ref[m, 0:1, :], (8, D))
        for d in range(8):
            upper = jnp.where(iota(shape, 0) < 6, nt(block, pick_vector(d)), nt(block, pick_head(d)))
            lower = nt(jnp.where(hidden_places(d), wide, 0.0).astype(BF16), row_pick)
            out_ref[m // 2, m % 2, d // 2, d % 2] = jnp.concatenate([upper, lower], axis=0).astype(BF16)


def ln(values):
    center = values - jnp.mean(values, axis=-1, keepdims=True)
    inverse = lax.rsqrt(jnp.mean(center * center, axis=-1, keepdims=True) + LN_EPS)
    return center * inverse, inverse


def ln_back(grad, normed, inverse):
    return inverse * (
        grad
        - jnp.mean(grad, axis=-1, keepdims=True)
        - normed * jnp.mean(grad * normed, axis=-1, keepdims=True)
    )


def position_rows():
    plane = np.zeros((128, D), np.float32)
    time_width, space_width = D // 16 * 4, D // 16 * 6

    def sines(count, width):
        half = width // 2
        spread = np.arange(half, dtype=np.float32) / np.float32(half)
        frequency = np.exp(np.float32(-math.log(10000.0)) * spread).astype(np.float32)
        angles = np.arange(count, dtype=np.float32)[:, None] * frequency
        return np.concatenate([np.sin(angles), np.cos(angles)], axis=-1).astype(np.float32)

    plane[0:3, 0:time_width] = sines(3, time_width)
    plane[3 : 3 + GRID, time_width : time_width + space_width] = sines(GRID, space_width)
    plane[3 + GRID : 3 + 2 * GRID, time_width + space_width :] = sines(GRID, space_width)
    parts, rest = [], plane
    for _ in range(3):
        part = rest.astype(jnp.bfloat16)
        parts.append(part)
        rest = rest - part.astype(np.float32)
    return np.stack(parts)


def spread_lanes(ref, wide):
    for g in range(D // 128):
        part = ref[:, :, 128 * g : 128 * g + 128].astype(F32)
        wide[g] = part.reshape(part.shape[0] * 8, 128)


def place_rows(places):
    frame = (places >= GRID * GRID).astype(jnp.int32) + (places >= 2 * GRID * GRID).astype(jnp.int32)
    within = places - frame * (GRID * GRID)
    row = jnp.floor((within.astype(F32) + 0.5) * (1.0 / GRID)).astype(jnp.int32)
    column = within - row * GRID
    lane = iota((places.shape[0], 128), 1)
    hot = (lane == frame) | (lane == 3 + row) | (lane == 3 + GRID + column)
    return hot.astype(F32).astype(BF16)


def lay_tokens(seq, pad, tiles, at, tok_ref, vis_ref, tab_ref, x_out, wide):
    head = seq - seq % 8
    spread_lanes(tok_ref, wide)
    for t in range(tiles):
        hot = place_rows(vis_ref[:, t : t + 1])
        table = nn(hot, tab_ref[0]) + nn(hot, tab_ref[1]) + nn(hot, tab_ref[2])
        x_out[t * pad + head : (t + 1) * pad, :] = jnp.zeros((pad - head, D), F32)
        for g in range(D // 128):
            lanes = slice(128 * g, 128 * g + 128)
            x_out[t * pad : t * pad + seq, lanes] = wide[g, pl.ds(at + t, seq, stride=8), :] + table[:, lanes]


def lay_cotangent(seq, pad, tiles, at, live_ref, cot_ref, dy_out, wide, grad):
    head = seq - seq % 8
    spread_lanes(cot_ref, wide)
    for t in range(tiles):
        live = live_ref[t : t + 1, :]
        grad[t * pad + head : (t + 1) * pad, :] = jnp.zeros((pad - head, D), F32)
        for g in range(D // 128):
            lanes = slice(128 * g, 128 * g + 128)
            grad[t * pad : t * pad + seq, lanes] = wide[g, pl.ds(at + t, seq, stride=8), :] * live
    dy_out[...] = grad[...].astype(BF16)


def fore_kernel(seq, pad, tiles, x_ref, a_ref, dy_t, vec_ref, off_ref, w_ref, part2, own3,
                h_out, qkv_out, p_out, o_out, r_out, slope_out, g3_out, c_t, w2_out, f3,
                low, f2, send, recv, local):
    step = pl.program_id(0)
    m = step % 4
    rows_of = lambda t: pl.ds(pl.multiple_of(t * pad, 16), pad)
    p = Place()
    s = Sends(send, recv)
    g2 = Gather(p, s, f2, 48, part=part2)
    halves = pl.ds(0, 384), pl.ds(384, 384)
    g3 = [Gather(p, s, f3, 48, cols, own=own3.at[0, :, cols]) for cols in halves]
    mine = [
        *Gather.present(p, part2, f2, 48, local),
        pltpu.make_async_copy(own3.at[0], f3.at[p.x, p.c, p.z, p.y], local.at[4]),
    ]
    hand_on = pltpu.make_async_copy(f2, w2_out, local.at[5])

    @pl.when(step == 0)
    def _():
        p.greet()
        g2.third()
        for g in g3:
            g.along_z()
        start(mine)
        h_out[...] = x_ref[...] + vec_ref[4:5, :]

    @pl.when(step < 4)
    def _():
        linear = nn(a_ref[...], w_ref[0, :, 0:576])
        zero = jnp.zeros((1, 192), F32)
        offset = jnp.concatenate([off_ref[0, 0:1, 0:192], zero, off_ref[0, 1:2, 0:192]], axis=1)
        qkv_out[0] = (linear + offset).astype(BF16)

        @pl.loop(0, tiles, unroll=2)
        def _(t):
            rows = rows_of(t)
            qkv = qkv_out[0, rows, :]
            parts = []
            for h in range(3):
                q, k, v = (qkv[:, 192 * j + 64 * h : 192 * j + 64 * h + 64] for j in range(3))
                s = nt(q, k) * 0.125
                s = jnp.where(iota(s.shape, 1) < seq, s, -1e30)
                e = jnp.exp(s - jnp.max(s, axis=-1, keepdims=True))
                low_p = (e * (1.0 / jnp.sum(e, axis=-1, keepdims=True))).astype(BF16)
                p_out[0, h, rows, :] = low_p
                parts.append(nn(low_p, v))
            o_out[0, rows, :] = jnp.concatenate(parts, axis=1).astype(BF16)

        h_out[...] += nt(o_out[0], w_ref[0, :, 576:768])

    @pl.when(step == 0)
    def _():
        for copy in mine:
            copy.wait()

    @pl.when(step == 1)
    def _():
        g3[0].second()

    @pl.when(step == 2)
    def _():
        g3[1].second()

    @pl.when(step == 3)
    def _():
        g2.last()

        @pl.loop(0, tiles)
        def _(t):
            normed, _ = ln(h_out[rows_of(t), :])
            low[rows_of(t), :] = (normed * vec_ref[2:3, :] + vec_ref[3:4, :]).astype(BF16)

        g2.done()
        hand_on.start()

    @pl.when(step >= 4)
    def _():
        @pl.loop(0, 3)
        def _(n):
            cols = pl.ds(pl.multiple_of(n * 256, 256), 256)
            w2 = f2[m // 2, m % 2, :, :, :, cols].reshape(D, 256)
            u = nn(low[...], w2) + off_ref[0, 2:3, cols]
            cdf = 0.5 * (1.0 + lax.erf(u * math.sqrt(0.5)))
            r = (u * cdf).astype(BF16)
            r_out[0, :, cols] = r
            slope_out[0, :, cols] = cdf + u * (jnp.exp(-0.5 * u * u) * (1.0 / math.sqrt(2.0 * math.pi)))
            g3_out[0, :, cols] = nn(dy_t[...], r).astype(BF16)

    @pl.when(step == 4)
    def _():
        g3[0].third()
        g3[1].third()

    @pl.when(step == 7)
    def _():
        g3[0].last()
        c_t[...] = low[...].T
        g3[1].last()
        for g in g3:
            g.done()
        hand_on.wait()
        s.finish()


def back_kernel(seq, pad, tiles, live_ref, dy, h_ref, c_t, a_t, vec_ref, w2_ref, w3_ref, r_ref, slope_ref,
                w_ref, qkv_ref, p_ref, o_ref, g3,
                da, dh, sum_two, hid_out, head_out, g1_out, part_out, low_out, all_out,
                low, dh_t, y, dc, do, dqkv, g2, own_out, *scratch):
    *buffers, send, recv, local = scratch
    step = pl.program_id(0)
    m = step % 4
    rows_of = lambda t: pl.ds(pl.multiple_of(t * pad, 16), pad)
    p = Place()
    s = Sends(send, recv)
    halves = pl.ds(0, 384), pl.ds(384, 384)
    early = [FeedReduce(p, s, g3, buffers[7 * i : 7 * i + 7], cols, local.at[i]) for i, cols in enumerate(halves)]
    late = [FeedReduce(p, s, g2, buffers[14 + 6 * i : 20 + 6 * i], cols) for i, cols in enumerate(halves)]
    trade = Trade(p, s, own_out, all_out, local.at[2], 1)

    @pl.when(step == 0)
    def _():
        p.greet()
        for r in early:
            r.cores()
        sum_two[...] = jnp.zeros_like(sum_two)

        @pl.loop(0, tiles)
        def _(t):
            sum_two[3:4, :] += jnp.sum(dy[rows_of(t), :].astype(F32), axis=0, keepdims=True)

        y[...] = jnp.zeros_like(y)
        dc[...] = jnp.zeros_like(dc)

    @pl.when(step < 4)
    def _():
        @pl.loop(0, 3)
        def _(n):
            cols = pl.ds(pl.multiple_of(n * 256, 256), 256)
            du = (nn(dy[...], w3_ref[0, :, cols]) * slope_ref[0, :, cols]).astype(BF16)
            hid_out[0, 0:1, cols] = jnp.sum(du.astype(F32), axis=0, keepdims=True)
            g2[m // 2, m % 2, :, :, :, cols] = nn(c_t[...], du).astype(BF16).reshape(4, 2, 96, 256)
            y[...] += nt(r_ref[0, :, cols], w3_ref[0, :, cols])
            dc[...] += nt(du, w2_ref[0, :, cols])

    @pl.when(step == 0)
    def _():
        for r in early:
            r.first()

    @pl.when(step == 2)
    def _():
        early[0].second()
        early[0].low_second()

    @pl.when(step == 3)
    def _():
        for r in late:
            r.cores()

        @pl.loop(0, tiles)
        def _(t):
            rows = rows_of(t)
            h = h_ref[rows, :]
            own_out[rows, :] = ((h + y[rows, :] + vec_ref[5:6, :]) * live_ref[pl.ds(t, 1), 0:1]).astype(BF16)
            normed, inverse = ln(h)
            grad = dc[rows, :]
            back = dy[rows, :].astype(F32) + ln_back(grad * vec_ref[2:3, :], normed, inverse)
            dh[rows, :] = back
            sum_two[0:1, :] += jnp.sum(grad * normed, axis=0, keepdims=True)
            sum_two[1:2, :] += jnp.sum(grad, axis=0, keepdims=True)
            sum_two[2:3, :] += jnp.sum(back, axis=0, keepdims=True)
            low[rows, :] = back.astype(BF16)

        trade.begin()
        early[1].second()
        early[1].low_second()
        for r in late:
            r.first()
        dh_t[...] = low[...].T
        da[...] = jnp.zeros_like(da)

    @pl.when(step >= 4)
    def _():
        do[...] = nn(low[...], w_ref[0, :, 576:768]).astype(BF16)
        g1_out[0, :, 576:768] = nn(dh_t[...], o_ref[0]).astype(BF16)

        @pl.loop(0, tiles, unroll=2)
        def _(t):
            rows = rows_of(t)
            qkv = qkv_ref[0, rows, :]
            grad = do[rows, :]
            parts = [[], [], []]
            for h in range(3):
                q, k, v = (qkv[:, 192 * j + 64 * h : 192 * j + 64 * h + 64] for j in range(3))
                g = grad[:, 64 * h : 64 * h + 64]
                low_p = p_ref[0, h, rows, :]
                prob = low_p.astype(F32)
                dp = nt(g, v)
                ds = (prob * (dp - jnp.sum(dp * prob, axis=-1, keepdims=True))).astype(BF16)
                parts[0].append(nn(ds, k) * 0.125)
                parts[1].append(tn(ds, q) * 0.125)
                parts[2].append(tn(low_p, g))
            dqkv[rows, :] = jnp.concatenate(parts[0] + parts[1] + parts[2], axis=1).astype(BF16)

        sums = jnp.sum(dqkv[...].astype(F32), axis=0, keepdims=True)
        head_out[0, 0:1, 0:192] = sums[:, 0:192]
        head_out[0, 1:2, 0:192] = sums[:, 384:576]
        g1_out[0, :, 0:576] = nn(a_t[...], dqkv[...]).astype(BF16)
        da[...] += nt(dqkv[...], w_ref[0, :, 0:576])

    @pl.when(step == 5)
    def _():
        early[0].low_third()
        late[0].second()
        late[0].low_second()

    @pl.when(step == 6)
    def _():
        late[1].second()
        late[1].low_second()
        early[1].low_third()
        trade.relay()

    @pl.when(step == 7)
    def _():
        for r in late:
            r.low_third()
        for i, r in enumerate(late + early):
            r.hand_on(part_out, low_out, i // 2, halves[i % 2])
        trade.done()
        s.finish()


def lay_kernel(seq, out_ref, in_ref, out_out, in_out):
    for ref, out in ((out_ref, out_out), (in_ref, in_out)):
        by_place = jnp.swapaxes(ref[...].astype(F32), 0, 1)[0:seq]
        out[...] = by_place.astype(out.dtype)


def update_kernel(*refs):
    attend_ref, feed_ref, small_ref = refs[:3]
    state, outs = refs[3:24], refs[24:]
    correction = 1.0 - 0.5**STEP
    rates = ((D // 2) ** -0.5, (D // 16) ** -0.5, D**-0.5, FF**-0.5, 0.1, 0.1, 0.15)

    def update(i, at, gradient):
        master, first, second = (state[i + 7 * j][at] for j in range(3))
        decay = DECAY if i < 4 else 0.0
        values = adamw_update(master, first, second, gradient, rates[i], decay, correction)
        for j, value in enumerate((gradient,) + values + (values[0].astype(BF16),)):
            outs[i + 7 * j][at] = value

    every = (slice(None), slice(None))
    for j in range(3):
        update(0, (j,) + every, attend_ref[:, 192 * j : 192 * j + 192])
    update(1, every, attend_ref[:, 576:768].T)
    update(2, every, feed_ref[0])
    update(3, every, feed_ref[1])
    for r in range(3):
        update(4, (r,) + every, small_ref[6:8, 8 * r : 8 * r + 8])
    update(5, every, small_ref[8:16, 0:12])
    update(6, every, small_ref[0:6, 0:96])


ALL = slice(None)


class Place:
    def __init__(self):
        dp, mp = lax.axis_index("dp"), lax.axis_index("mp")
        self.z, self.y = dp // 2, dp % 2
        self.x, self.c = mp // 2, mp % 2
        self.zs = [(self.z + k) % 4 for k in (1, 2, 3)]
        self.oy, self.ox, self.oc = 1 - self.y, 1 - self.x, 1 - self.c
        self.to_z = [self.id(z=z) for z in self.zs]
        self.to_y, self.to_x, self.to_c = self.id(y=self.oy), self.id(x=self.ox), self.id(c=self.oc)

    def id(self, z=None, y=None, x=None, c=None):
        z, y, x, c = (own if new is None else new for own, new in ((self.z, z), (self.y, y), (self.x, x), (self.c, c)))
        return (2 * z + y, 2 * x + c)

    def greet(self):
        barrier = pltpu.get_barrier_semaphore()
        for device in (*self.to_z, self.to_y, self.to_x, self.to_c):
            pl.semaphore_signal(barrier, inc=1, device_id=device, device_id_type=MESH)
        pl.semaphore_wait(barrier, 6)


class Sends:
    def __init__(self, send, recv):
        self.send, self.recv, self.all = send, recv, []

    def copy(self, src, dst, device):
        i = len(self.all)
        self.all.append(
            pltpu.make_async_remote_copy(
                src_ref=src,
                dst_ref=dst,
                send_sem=self.send.at[i],
                recv_sem=self.recv.at[i],
                device_id=device,
                device_id_type=MESH,
            )
        )
        return self.all[-1]

    def start(self, src, dst, device):
        copy = self.copy(src, dst, device)
        copy.start()
        return copy

    def finish(self):
        for copy in self.all:
            copy.wait_send()


def start(copies):
    for copy in copies:
        copy.start()


def arrived(copies):
    for copy in copies:
        copy.wait_recv()


class Gather:
    def __init__(self, p, s, full, split, cols=ALL, own=None, part=None, to_end=True):
        every = full.shape[4]
        of = lambda ref, x, c, z, y, rows: ref.at[x, c, z, y, rows, cols]
        at = lambda *where: of(full, *where)
        source = full if part is None else part
        both = lambda where, device, ref=full: s.copy(of(ref, *where), at(*where), device)
        high, low = pl.ds(0, split), pl.ds(split, every - split)
        self.z, self.two, self.core_two, self.core_three, self.core_last = [], [], [], [], []
        if own is not None:
            here = at(p.x, p.c, p.z, p.y, ALL)
            self.z = [s.copy(own, here, device) for device in p.to_z]
            self.two = [both((p.x, p.c, ALL, p.y, high), p.to_y)]
            self.core_two = [both((p.x, p.c, ALL, p.y, ALL), p.to_c)]
            if split < every:
                self.two.append(both((p.x, p.c, ALL, p.y, low), p.to_x))
        if to_end:
            self.three = [both((p.x, p.c, ALL, ALL, high), p.to_x, source)]
            self.core_three = [both((p.x, p.c, ALL, p.oy, high), p.to_c, source)]
            self.core_last = [both((p.ox, p.c, ALL, ALL, high), p.to_c)]
            if split < every:
                self.three += [both((x, p.c, ALL, p.y, low), p.to_y, source) for x in (0, 1)]
                self.core_three.append(both((p.ox, p.c, ALL, p.y, low), p.to_c, source))
                self.core_last += [both((x, p.c, ALL, p.oy, low), p.to_c) for x in (0, 1)]

    @staticmethod
    def present(p, part, full, split, local):
        high, low = pl.ds(0, split), pl.ds(split, full.shape[4] - split)
        where = [(p.x, p.c, ALL, ALL, high), (p.x, p.oc, ALL, p.y, ALL), *((x, p.c, ALL, p.y, low) for x in (0, 1))]
        return [pltpu.make_async_copy(part.at[w], full.at[w], local.at[i]) for i, w in enumerate(where)]

    def along_z(self):
        start(self.z)

    def second(self):
        arrived(self.z)
        start(self.two)
        start(self.core_two)

    def third(self):
        arrived(self.two)
        start(self.three)
        start(self.core_three)

    def last(self):
        arrived(self.three)
        start(self.core_last)

    def done(self):
        arrived(self.core_two + self.core_three + self.core_last)

    COPIES = 14
    COPIES_WHOLE = 8


def gather_kernel(seq, pad, tiles, w_ref, s_ref, tok, cot, vis_ref, tab_ref, live_ref,
                  f1, part2, x_out, dy_out, dy_t, a_out, a_t, vec_out, off_out, fs, tok_ref, cot_ref, wide, grad, send, recv, local):
    p = Place()
    s = Sends(send, recv)
    thirds = [pl.ds(256 * i, 256) for i in range(3)]
    gathers = [
        Gather(p, s, fs, 16, own=s_ref),
        *(Gather(p, s, f1, 48, cols, own=w_ref.at[0, :, cols]) for cols in thirds),
    ]
    ahead = Gather(p, s, part2, 48, own=w_ref.at[1], to_end=False)
    group = pl.ds(pl.multiple_of(8 * p.x, 8), 8)
    rows_in = [
        pltpu.make_async_copy(tok.at[:, group], tok_ref, local.at[3]),
        pltpu.make_async_copy(cot.at[:, group], cot_ref, local.at[4]),
    ]
    mine = [
        pltpu.make_async_copy(s_ref, fs.at[p.x, p.c, p.z, p.y], local.at[0]),
        pltpu.make_async_copy(w_ref.at[0], f1.at[p.x, p.c, p.z, p.y], local.at[1]),
        pltpu.make_async_copy(w_ref.at[1], part2.at[p.x, p.c, p.z, p.y], local.at[2]),
    ]
    p.greet()
    for g in gathers:
        g.along_z()
    ahead.along_z()
    start(mine)
    start(rows_in)
    rows_in[0].wait()
    lay_tokens(seq, pad, tiles, p.c * tiles, tok_ref, vis_ref, tab_ref, x_out, wide)
    for copy in mine:
        copy.wait()
    gathers[0].second()
    gathers[1].second()
    rows_in[1].wait()
    lay_cotangent(seq, pad, tiles, p.c * tiles, live_ref, cot_ref, dy_out, wide, grad)
    stages = [("second", 2), ("third", 0), ("third", 1), ("second", 3), ("last", 0), ("third", 2), ("third", 3), ("done", 0)]
    for name, i in stages:
        getattr(gathers[i], name)()
    spread_small(fs, vec_out, off_out)
    gathers[1].last()

    @pl.loop(0, tiles)
    def _(t):
        rows = pl.ds(pl.multiple_of(t * pad, 16), pad)
        normed, _ = ln(x_out[rows, :])
        a_out[rows, :] = (normed * vec_out[0:1, :] + vec_out[1:2, :]).astype(BF16)

    a_t[...] = a_out[...].T
    dy_t[...] = dy_out[...].T
    gathers[2].last()
    ahead.second()
    for name, i in [("last", 3), ("done", 1), ("done", 2), ("done", 3)]:
        getattr(gathers[i], name)()
    arrived(ahead.two + ahead.core_two)
    s.finish()


def add_into(target, other, lead):
    total = math.prod(lead)

    @pl.loop(0, total)
    def _(i):
        index = []
        for size in reversed(lead):
            index.append(i % size)
            i = i // size
        index = tuple(reversed(index))
        target[index] = (target[index].astype(F32) + other(*index).astype(F32)).astype(BF16)


class Reduce:
    COPIES = 6

    def __init__(self, p, s, parts, buffers, out, cols, load):
        own, r0, r1, r2, r3 = buffers
        self.p, self.out, self.r0, self.r1, self.r2, self.r3 = p, out, r0, r1, r2, r3
        self.load = pltpu.make_async_copy(parts.at[:, p.c, :, :, :, cols], own, load)
        self.own = lambda x, z, y: own[x, z, y]
        self.core = [s.copy(parts.at[:, p.oc, :, :, :, cols], r0, p.to_c)]
        self.over_y = [s.copy(r0.at[:, :, p.oy], r1, p.to_y)]
        self.over_x = [s.copy(r1.at[p.ox], r2, p.to_x)]
        self.over_z = [s.copy(r2.at[z], r3.at[k], device) for k, (z, device) in enumerate(zip(p.zs, p.to_z))]

    def cores(self):
        start(self.core)
        self.load.start()

    def first(self):
        self.load.wait()
        arrived(self.core)
        add_into(self.r0, self.own, self.r0.shape[:3])
        start(self.over_y)

    def second(self):
        arrived(self.over_y)
        add_into(self.r1, lambda x, z: self.r0[x, z, self.p.y], self.r1.shape[:2])
        start(self.over_x)

    def third(self):
        arrived(self.over_x)
        add_into(self.r2, lambda z: self.r1[self.p.x, z], self.r2.shape[:1])
        start(self.over_z)

    def last(self):
        arrived(self.over_z)
        r2, r3 = self.r2, self.r3
        self.out[...] = r2[self.p.z].astype(F32) + r3[0].astype(F32) + r3[1].astype(F32) + r3[2].astype(F32)

    @staticmethod
    def scratch(rows, columns):
        lead = (2, 4, 2), (2, 4, 2), (2, 4), (4,), (3,)
        return [pltpu.VMEM(shape + (rows, columns), BF16) for shape in lead]


class FeedReduce:
    COPIES = 8

    def __init__(self, p, s, parts, buffers, cols, load=None):
        *own, r0, r1, r2, e1, e2, e3 = buffers
        self.p, self.r0, self.r1, self.r2, self.e1, self.e2, self.e3 = p, r0, r1, r2, e1, e2, e3
        every, split = r0.shape[3], r1.shape[2]
        self.split = split
        high, low = pl.ds(0, split), pl.ds(split, every - split)
        if own:
            self.load = [pltpu.make_async_copy(parts.at[:, p.c, :, :, :, cols], own[0], load)]
            self.own = lambda x, z, y: own[0][x, z, y]
        else:
            self.load, self.own = [], lambda x, z, y: parts[x, p.c, z, y, :, cols]
        self.core = [s.copy(parts.at[:, p.oc, :, :, :, cols], r0, p.to_c)]
        self.over_y = [s.copy(r0.at[:, :, p.oy, high], r1, p.to_y)]
        self.over_x = [s.copy(r1.at[p.ox], r2, p.to_x)]
        self.low_z = [s.copy(r0.at[:, z, :, low], e1.at[k], device) for k, (z, device) in enumerate(zip(p.zs, p.to_z))]
        self.low_y = [s.copy(e1.at[0, :, p.oy], e2, p.to_y)]
        self.low_x = [s.copy(e2.at[p.ox], e3, p.to_x)]

    def cores(self):
        start(self.core + self.load)

    def first(self):
        for copy in self.load:
            copy.wait()
        arrived(self.core)
        add_into(self.r0, self.own, self.r0.shape[:3])
        start(self.over_y + self.low_z)

    def second(self):
        arrived(self.over_y)
        add_into(self.r1, lambda x, z: self.r0[x, z, self.p.y, 0 : self.split], self.r1.shape[:2])
        start(self.over_x)

    def low_second(self):
        arrived(self.low_z)
        for x in range(2):
            for y in range(2):
                total = self.r0[x, self.p.z, y, self.split :].astype(F32)
                for k in range(3):
                    total += self.e1[k, x, y].astype(F32)
                self.e1[0, x, y] = total.astype(BF16)
        start(self.low_y)

    def low_third(self):
        arrived(self.low_y)
        for x in range(2):
            self.e2[x] = (self.e2[x].astype(F32) + self.e1[0, x, self.p.y].astype(F32)).astype(BF16)
        start(self.low_x)

    def hand_on(self, out, low_out, i, cols):
        arrived(self.over_x)
        for z in range(4):
            out[z, i, :, cols] = (self.r2[z].astype(F32) + self.r1[self.p.x, z].astype(F32)).astype(BF16)
        arrived(self.low_x)
        low_out[i, :, cols] = self.e2[self.p.x].astype(F32) + self.e3[...].astype(F32)

    @staticmethod
    def scratch(rows, split, columns):
        low = rows - split
        shapes = (2, 4, 2, rows), (2, 4, 2, rows), (2, 4, split), (4, split), (3, 2, 2, low), (2, low), (low,)
        return [pltpu.VMEM(shape + (columns,), BF16) for shape in shapes]


class Trade:
    def __init__(self, p, s, own, full, local, pieces):
        here, there = full.at[p.x, p.c], full.at[p.ox, p.c]
        self.mine = pltpu.make_async_copy(own, here, local)
        size = own.shape[0] // pieces
        cuts = [pl.ds(size * i, size) for i in range(pieces)]
        self.x = [s.copy(own.at[cut], here.at[cut], p.to_x) for cut in cuts]
        self.c = [s.copy(own, here, p.to_c)]
        self.further = [s.copy(there, there, p.to_c)]

    def begin(self):
        start(self.x[:1])
        start(self.c)
        self.mine.start()

    def more(self, i):
        start(self.x[i : i + 1])

    def relay(self):
        arrived(self.x)
        start(self.further)

    def done(self):
        arrived(self.c + self.further)
        self.mine.wait()


def reduce_kernel(pad, tiles, g1, x_in, da_in, dh_in, vec_ref, part, part_low, sum_two, sum_hid, sum_head,
                  total, feed, small, all_in, x, da, dh, own_in, sum_one, part_z, gs, lines, *scratch):
    *buffers, send, recv, local = scratch
    fetch = [pltpu.make_async_copy(src, dst, local.at[5 + i]) for i, (src, dst) in enumerate(((x_in, x), (da_in, da), (dh_in, dh)))]
    p = Place()
    s = Sends(send, recv)
    thirds = [pl.ds(256 * i, 256) for i in range(3)]
    reduces = [
        Reduce(p, s, g1, buffers[5 * i : 5 * i + 5], total.at[:, cols], cols, local.at[i])
        for i, cols in enumerate(thirds)
    ]
    reduces.append(Reduce(p, s, gs, buffers[15:20], small, ALL, local.at[3]))
    over_z = [s.copy(part.at[z], part_z.at[k], device) for k, (z, device) in enumerate(zip(p.zs, p.to_z))]
    trade = Trade(p, s, own_in, all_in, local.at[4], 4)
    p.greet()
    for r in reduces[:3]:
        r.cores()
    start(over_z)
    start(fetch)
    sum_one[...] = jnp.zeros_like(sum_one)
    for r in reduces[:3]:
        r.first()
    for copy in fetch:
        copy.wait()

    @pl.loop(0, tiles)
    def _(t):
        rows = pl.ds(pl.multiple_of(t * pad, 16), pad)
        normed, inverse = ln(x[rows, :])
        grad = da[rows, :]
        back = ln_back(grad * vec_ref[0:1, :], normed, inverse)
        own_in[rows, :] = (dh[rows, :] + back).astype(BF16)
        sum_one[0:1, :] += jnp.sum(grad * normed, axis=0, keepdims=True)
        sum_one[1:2, :] += jnp.sum(grad, axis=0, keepdims=True)

    trade.begin()
    squeeze_small(sum_two, sum_one, sum_hid, sum_head, gs, lines)
    reduces[3].cores()
    reduces[0].second()
    trade.more(1)
    reduces[3].first()
    reduces[0].third()
    reduces[1].second()
    trade.more(2)
    reduces[1].third()
    reduces[3].second()
    reduces[2].second()
    trade.more(3)
    reduces[3].third()
    reduces[2].third()
    arrived(over_z)
    for i in range(2):
        feed[i, 0:64] = part[p.z, i].astype(F32) + sum(part_z[k, i].astype(F32) for k in range(3))
        feed[i, 64:96] = part_low[i]
    for r in reduces:
        r.last()
    trade.relay()
    trade.done()
    s.finish()


def fast_shards(*args):
    (tokens, cotangent, visible, tile_counts, *state) = args
    tile_count, seq, width = tokens.shape
    mp_size = lax.axis_size("mp")
    tiles = tile_count // mp_size
    pad = -(-seq // 16) * 16
    rows = tiles * pad
    native = lambda i, a: a.transpose(1, 0, 2) if i in (0, 4) else a.T if i in (3, 5) else a
    state = [native(i % 7, a) for i, a in enumerate(state)]
    params = lambda limit=None, **kw: pltpu.CompilerParams(vmem_limit_bytes=60 << 20, **kw)
    shape = jax.ShapeDtypeStruct
    me = lax.axis_index("mp").astype(jnp.int32)
    place = me * tiles + jnp.arange(tiles, dtype=jnp.int32)
    live = jnp.broadcast_to((place < tile_counts[0]).astype(F32)[:, None], (tiles, 128))
    by_place = lambda a: a.transpose(1, 0, 2)
    places = lax.dynamic_slice(visible, (me * tiles, 0), (tiles, seq)).T
    table = jnp.asarray(position_rows())
    vmem, anywhere = pl.BlockSpec(memory_space=pltpu.VMEM), pl.BlockSpec(memory_space=ANY)

    own, own_small = pl.pallas_call(
        pack_kernel,
        out_shape=(shape((3, 96, D), BF16), shape((16, 128), BF16)),
        scratch_shapes=[pltpu.VMEM((16, 128), F32)],
        compiler_params=params(),
        name="pack",
    )(*state[:7])

    full = shape((2, 2, 4, 2, 96, D), BF16)
    dma = lambda count: pltpu.SemaphoreType.DMA((count,))
    copies = 3 * Gather.COPIES + Gather.COPIES_WHOLE + 6
    f1, part2, x, dy, dy_t, a, a_t, vec, off = pl.pallas_call(
        functools.partial(gather_kernel, seq, pad, tiles),
        out_shape=(
            full,
            full,
            shape((rows, D), F32),
            shape((rows, D), BF16),
            shape((D, rows), BF16),
            shape((rows, D), BF16),
            shape((D, rows), BF16),
            shape((16, D), F32),
            shape((4, 8, D), F32),
        ),
        in_specs=[vmem] * 2 + [anywhere] * 2 + [vmem] * 3,
        out_specs=[anywhere] * 2 + [vmem] * 7,
        scratch_shapes=[
            pltpu.VMEM((2, 2, 4, 2, 16, 128), BF16),
            pltpu.VMEM((seq, 8, D), BF16),
            pltpu.VMEM((seq, 8, D), BF16),
            pltpu.VMEM((D // 128, seq * 8, 128), F32),
            pltpu.VMEM((rows, D), F32),
            dma(copies),
            dma(copies),
            dma(5),
        ],
        compiler_params=params(collective_id=0, has_side_effects=True),
        name="gather",
    )(own, own_small, by_place(tokens), by_place(cotangent), places, table, live)
    w1 = f1.reshape(4, D, D)

    all_of1 = lambda *shape: pl.BlockSpec(shape, lambda i: (0,) * len(shape))
    each = lambda *shape: pl.BlockSpec((1,) + shape, lambda i: (i % 4,) + (0,) * len(shape))
    former = lambda *shape: pl.BlockSpec((1,) + shape, lambda i: (i + i // 4 * (3 - i),) + (0,) * len(shape))
    latter = lambda *shape: pl.BlockSpec((1,) + shape, lambda i: (i // 4 * (i - 4),) + (0,) * len(shape))
    copies = Gather.COPIES * 3 - 6
    h, qkv, probs, o, r, slope, g3, c_t, f2, f3 = pl.pallas_call(
        functools.partial(fore_kernel, seq, pad, tiles),
        out_shape=(
            shape((rows, D), F32),
            shape((4, rows, 576), BF16),
            shape((4, 3, rows, pad), BF16),
            shape((4, rows, 192), BF16),
            shape((4, rows, D), BF16),
            shape((4, rows, D), F32),
            shape((4, D, D), BF16),
            shape((D, rows), BF16),
            full,
            full,
        ),
        grid=(8,),
        in_specs=[all_of1(rows, D), all_of1(rows, D), all_of1(D, rows), all_of1(16, D), each(8, D), former(D, D),
                  anywhere,
                  pl.BlockSpec((1, 96, D), lambda i: (2, 0, 0))],
        out_specs=[all_of1(rows, D), former(rows, 576), former(3, rows, pad), former(rows, 192), latter(rows, D),
                   latter(rows, D), latter(D, D), all_of1(D, rows), anywhere, anywhere],
        scratch_shapes=[
            pltpu.VMEM((rows, D), BF16),
            pltpu.VMEM((2, 2, 4, 2, 96, D), BF16),
            dma(copies),
            dma(copies),
            dma(6),
        ],
        compiler_params=params(collective_id=2, has_side_effects=True),
        name="fore",
    )(x, a, dy_t, vec, off, w1, part2, own)
    w2, w3 = (f.reshape(4, D, D) for f in (f2, f3))

    by_device = lambda g: g.reshape(2, 2, 4, 2, 96, D)
    everyone = shape((2, 2, rows, D), BF16)
    copies = 4 * FeedReduce.COPIES + 3
    da, dh, sum_two, sum_hid, sum_head, g1, part, part_low, all_out = pl.pallas_call(
        functools.partial(back_kernel, seq, pad, tiles),
        out_shape=(
            shape((rows, D), F32),
            shape((rows, D), F32),
            shape((8, D), F32),
            shape((4, 8, D), F32),
            shape((4, 8, D), F32),
            shape((4, D, D), BF16),
            shape((4, 2, 64, D), BF16),
            shape((2, 32, D), F32),
            everyone,
        ),
        grid=(8,),
        in_specs=[all_of1(tiles, 128), all_of1(rows, D), all_of1(rows, D), all_of1(D, rows), all_of1(D, rows), all_of1(16, D),
                  former(D, D), former(D, D), former(rows, D), former(rows, D), latter(D, D), latter(rows, 576),
                  latter(3, rows, pad), latter(rows, 192), anywhere],
        out_specs=[all_of1(rows, D), all_of1(rows, D), all_of1(8, D), former(8, D), latter(8, D), latter(D, D),
                   all_of1(4, 2, 64, D), all_of1(2, 32, D), anywhere],
        scratch_shapes=[
            pltpu.VMEM((rows, D), BF16),
            pltpu.VMEM((D, rows), BF16),
            pltpu.VMEM((rows, D), F32),
            pltpu.VMEM((rows, D), F32),
            pltpu.VMEM((rows, 192), BF16),
            pltpu.VMEM((rows, 576), BF16),
            pltpu.VMEM((2, 2, 4, 2, 96, D), BF16),
            pltpu.VMEM((rows, D), BF16),
            *(2 * FeedReduce.scratch(96, 64, 384)),
            *(2 * FeedReduce.scratch(96, 64, 384)[1:]),
            dma(copies),
            dma(copies),
            dma(3),
        ],
        compiler_params=params(collective_id=3, has_side_effects=True),
        name="back",
    )(live, dy, h, c_t, a_t, vec, w2, w3, r, slope, w1, qkv, probs, o, by_device(g3))

    copies = 4 * Reduce.COPIES + 3 + 6
    total_attend, total_feed, small, all_in = pl.pallas_call(
        functools.partial(reduce_kernel, pad, tiles),
        out_shape=(shape((96, D), F32), shape((2, 96, D), F32), shape((16, 128), F32), everyone),
        in_specs=[anywhere] * 4 + [vmem] * 6,
        out_specs=[vmem] * 3 + [anywhere],
        scratch_shapes=[
            pltpu.VMEM((rows, D), F32),
            pltpu.VMEM((rows, D), F32),
            pltpu.VMEM((rows, D), F32),
            pltpu.VMEM((rows, D), BF16),
            pltpu.VMEM((8, D), F32),
            pltpu.VMEM((3, 2, 64, D), BF16),
            pltpu.VMEM((2, 2, 4, 2, 16, 128), BF16),
            pltpu.VMEM((8, D), F32),
            *(3 * Reduce.scratch(96, 256)),
            *Reduce.scratch(16, 128),
            dma(copies),
            dma(copies),
            dma(8),
        ],
        compiler_params=params(collective_id=1, has_side_effects=True),
        name="reduce",
    )(by_device(g1), x, da, dh, vec, part, part_low, sum_two, sum_hid, sum_head)

    block = pl.BlockSpec((tile_count, pad, 128), lambda n: (0, 0, n))
    output, input_grad = pl.pallas_call(
        functools.partial(lay_kernel, seq),
        out_shape=(shape((seq, tile_count, D), BF16), shape((seq, tile_count, D), F32)),
        grid=(D // 128,),
        in_specs=[block, block],
        out_specs=(pl.BlockSpec((seq, tile_count, 128), lambda n: (0, 0, n)),) * 2,
        compiler_params=params(),
        name="lay",
    )(*(a.reshape(tile_count, pad, D) for a in (all_out, all_in)))
    output, input_grad = by_place(output), by_place(input_grad)

    kinds = [shape(a.shape, F32) for a in state[:7]]
    results = pl.pallas_call(
        update_kernel,
        out_shape=tuple(kinds * 4 + [shape(a.shape, BF16) for a in kinds]),
        compiler_params=params(),
        name="update",
    )(total_attend, total_feed, small, *state)
    return (output, input_grad) + tuple(native(i % 7, a) for i, a in enumerate(results))


def solution(mesh):
    in_specs = (
        P("dp", None, None),
        P("dp", None, None),
        P("dp", None),
        P("dp"),
        P("dp", None, "mp"),
        P("mp", "dp"),
        P("dp", "mp"),
        P("mp", "dp"),
        P(None, "mp", "dp"),
        P("mp", "dp"),
        P(None, "dp"),
        P("dp", None, "mp"),
        P("mp", "dp"),
        P("dp", "mp"),
        P("mp", "dp"),
        P(None, "mp", "dp"),
        P("mp", "dp"),
        P(None, "dp"),
        P("dp", None, "mp"),
        P("mp", "dp"),
        P("dp", "mp"),
        P("mp", "dp"),
        P(None, "mp", "dp"),
        P("mp", "dp"),
        P(None, "dp"),
    )
    out_specs = (
        P("dp", None, None),
        P("dp", None, None),
        P("dp", None, "mp"),
        P("mp", "dp"),
        P("dp", "mp"),
        P("mp", "dp"),
        P(None, "mp", "dp"),
        P("mp", "dp"),
        P(None, "dp"),
        P("dp", None, "mp"),
        P("mp", "dp"),
        P("dp", "mp"),
        P("mp", "dp"),
        P(None, "mp", "dp"),
        P("mp", "dp"),
        P(None, "dp"),
        P("dp", None, "mp"),
        P("mp", "dp"),
        P("dp", "mp"),
        P("mp", "dp"),
        P(None, "mp", "dp"),
        P("mp", "dp"),
        P(None, "dp"),
        P("dp", None, "mp"),
        P("mp", "dp"),
        P("dp", "mp"),
        P("mp", "dp"),
        P(None, "mp", "dp"),
        P("mp", "dp"),
        P(None, "dp"),
        P("dp", None, "mp"),
        P("mp", "dp"),
        P("dp", "mp"),
        P("mp", "dp"),
        P(None, "mp", "dp"),
        P("mp", "dp"),
        P(None, "dp"),
    )
    sizes = (mesh.shape["dp"], mesh.shape["mp"])
    body = fast_shards if sizes == (8, 4) else shards
    return jax.shard_map(body, mesh=mesh, in_specs=in_specs, out_specs=out_specs, check_vma=False)
```
